128 devices in a mesh: fsdp: 2 (over y_hi), ctx: 8 (over x, y_lo), tp: 8 (over z, core).
Axes of the slice: x: 4, y: 4 (y_hi: 2, y_lo: 2; y = y_hi * 2 + y_lo), z: 4, core: 2. Of those that a mesh axis runs over, the one named last changes fastest.
Arguments:
- layer_input: bfloat16 [2, 4096, 2048], P('fsdp', 'ctx'), may hold values from -6 to 6
- doc_ids: int32 [2, 4096], P('fsdp'), may hold values from 0 to 63, never falling along the last dimension, each value on 1 to 2048 neighbouring positions
- pre_gain: float32 [2048], P(('fsdp', 'ctx')), may hold values from 0.5 to 1.5
- pre_shift: float32 [2048], P(('fsdp', 'ctx')), may hold values from -1.8 to 1.8
- query_weight: float32 [2048, 2048], P(('fsdp', 'ctx'), 'tp'), may hold values from -0.125 to 0.125
- query_bias: float32 [8, 256], P('tp', ('fsdp', 'ctx')), may hold values from -3 to 3
- key_weight: float32 [2048, 2048], P(('fsdp', 'ctx'), 'tp'), may hold values from -0.125 to 0.125
- value_weight: float32 [2048, 2048], P(('fsdp', 'ctx'), 'tp'), may hold values from -0.125 to 0.125
- value_bias: float32 [8, 256], P('tp', ('fsdp', 'ctx')), may hold values from -3 to 3
- output_weight: float32 [2048, 2048], P('tp', ('fsdp', 'ctx')), may hold values from -0.5 to 0.5
- output_bias: float32 [2048], P(('fsdp', 'ctx')), may hold values from -3 to 3
- mid_gain: float32 [2048], P(('fsdp', 'ctx')), may hold values from 0.5 to 1.5
- mid_shift: float32 [2048], P(('fsdp', 'ctx')), may hold values from -1.8 to 1.8
- expand_weight: float32 [2048, 8192], P(('fsdp', 'ctx'), 'tp'), may hold values from -0.125 to 0.125
- expand_bias: float32 [8, 1024], P('tp', ('fsdp', 'ctx')), may hold values from -3 to 3
- contract_weight: float32 [8192, 2048], P('tp', ('fsdp', 'ctx')), may hold values from -0.0625 to 0.0625
- contract_bias: float32 [2048], P(('fsdp', 'ctx')), may hold values from -3 to 3
- cotangent: bfloat16 [2, 4096, 2048], P('fsdp', 'ctx'), may hold values from -6 to 6
Outputs:
- layer_output: bfloat16 [2, 4096, 2048], P('fsdp', 'ctx')
- input_grad: float32 [2, 4096, 2048], P('fsdp', 'ctx')
- pre_gain_grad: float32 [2048], P(('fsdp', 'ctx'))
- pre_shift_grad: float32 [2048], P(('fsdp', 'ctx'))
- query_weight_grad: float32 [2048, 2048], P(('fsdp', 'ctx'), 'tp')
- query_bias_grad: float32 [8, 256], P('tp', ('fsdp', 'ctx'))
- key_weight_grad: float32 [2048, 2048], P(('fsdp', 'ctx'), 'tp')
- value_weight_grad: float32 [2048, 2048], P(('fsdp', 'ctx'), 'tp')
- value_bias_grad: float32 [8, 256], P('tp', ('fsdp', 'ctx'))
- output_weight_grad: float32 [2048, 2048], P('tp', ('fsdp', 'ctx'))
- output_bias_grad: float32 [2048], P(('fsdp', 'ctx'))
- mid_gain_grad: float32 [2048], P(('fsdp', 'ctx'))
- mid_shift_grad: float32 [2048], P(('fsdp', 'ctx'))
- expand_weight_grad: float32 [2048, 8192], P(('fsdp', 'ctx'), 'tp')
- expand_bias_grad: float32 [8, 1024], P('tp', ('fsdp', 'ctx'))
- contract_weight_grad: float32 [8192, 2048], P('tp', ('fsdp', 'ctx'))
- contract_bias_grad: float32 [2048], P(('fsdp', 'ctx'))
The draws below stay inside these ranges and needn't reach their ends.
Inputs may be any that keep to these rules, and one draw needn't show every extreme that they name: `doc_ids`: document numbers never fall along a sequence, and no document has more than 2048 tokens.
All inputs are finite; a program needn't handle non-finite values.
Results may differ from the reference program's by a relative error of at most 0.028.
Values may be sent and summed in bfloat16 or wider, within the bound.
No kernel may reach another device: no remote copies, remote signals or barrier semaphores. Data moves between devices by JAX's collectives and lax.ppermute only.
A program may use at most 192 MiB of HBM per device.

```python
import math
import jax
import jax.numpy as jnp
import numpy as np
from jax import lax

D = 2048
FF = 8192
HEADS = 16
HEAD_DIM = 128
LEN = 4096
SEQS = 2
DOCS = 64
DOC_MOST = 2048
N_TP = 8


def block_levels(own_key, dims, shards, least, largest):
    def one(axis_at, blocks):
        heights = jax.random.uniform(jax.random.fold_in(jax.random.fold_in(own_key, 6), axis_at), (blocks,), jnp.float32, least / len(shards), largest / len(shards))
        return jnp.repeat(jnp.exp(heights), dims[axis_at] // blocks).reshape((-1,) + (1,) * (len(dims) - axis_at - 1))

    loudness = one(*shards[0])
    for cut in shards[1:]:
        loudness = loudness * one(*cut)
    return loudness


def split_up(number_of, total, reach, skew):
    portions = [(1 << 20) // math.isqrt(grade ** skew) + 1 for grade in range(2, number_of + 1)]
    surplus, holding = total - reach - (number_of - 1), [1] * (number_of - 1)
    while surplus > 0:
        candidates = [i for i in range(number_of - 1) if holding[i] < reach]
        whole, budget = sum([portions[i] for i in candidates]), surplus
        for i in candidates:
            extra = min(reach - holding[i], max(1, budget * portions[i] // whole), surplus)
            holding[i] = holding[i] + extra
            surplus = surplus - extra
    return np.array([reach] + holding)


def ragged(own_key, count, total, limit, slope):
    if count == 2:
        one = jax.random.randint(own_key, (), max(1, total - limit), min(limit, total - 1) + 1)
        return jnp.stack([one, total - one])
    tallies = jnp.asarray(split_up(count, total, limit, slope), jnp.int32)
    twos = (count - 1) // 2
    giver, receiver = tallies[1:1 + 2 * twos:2], tallies[2:2 + 2 * twos:2]
    slack = jnp.minimum(giver - 1, limit - receiver)
    moved = jax.random.randint(jax.random.fold_in(own_key, 1), (twos,), 0, 1 << 20) % (slack + 1)
    tallies = tallies.at[1:1 + 2 * twos:2].set(giver - moved).at[2:2 + 2 * twos:2].set(receiver + moved)
    return tallies[jax.random.permutation(jax.random.fold_in(own_key, 2), count)]


def gaussian(rng, shape, width, bound, pieces=(), held_as=jnp.bfloat16):
    values = width * jax.random.normal(rng, shape, jnp.float32)
    if pieces:
        values = values * block_levels(rng, shape, pieces, -0.22, 0.18)
    return jnp.clip(values, -bound, bound).astype(held_as)


def setup_inputs(seed: int = 0) -> dict:
    streams_of = jax.random.split(jax.random.key(seed), 19)
    layer_input = gaussian(streams_of[0], (SEQS, LEN, D), 1.0, 6.0, ((0, 2), (1, 8)))
    doc_ids = jax.vmap(lambda own: jnp.searchsorted(jnp.cumsum(ragged(own, DOCS, LEN, DOC_MOST, 2)), jnp.arange(LEN), side="right"))(jax.random.split(streams_of[1], SEQS)).reshape((SEQS, LEN)).astype(jnp.int32)
    pre_gain = jnp.clip(1.0 + 0.1 * jax.random.normal(streams_of[2], (D,), jnp.float32), 0.5, 1.5)
    pre_shift = gaussian(streams_of[3], (D,), 0.3, 1.8, ((0, 16),), jnp.float32)
    query_weight = gaussian(streams_of[4], (D, D), D ** -0.5, 0.125, ((0, 16), (1, 8)), jnp.float32)
    query_bias = gaussian(streams_of[5], (N_TP, D // N_TP), 0.5, 3.0, ((0, 8), (1, 16)), jnp.float32)
    key_weight = gaussian(streams_of[6], (D, D), D ** -0.5, 0.125, ((0, 16), (1, 8)), jnp.float32)
    value_weight = gaussian(streams_of[7], (D, D), D ** -0.5, 0.125, ((0, 16), (1, 8)), jnp.float32)
    value_bias = gaussian(streams_of[8], (N_TP, D // N_TP), 0.5, 3.0, ((0, 8), (1, 16)), jnp.float32)
    output_weight = gaussian(streams_of[9], (D, D), (D // 16) ** -0.5, 0.5, ((0, 8), (1, 16)), jnp.float32)
    output_bias = gaussian(streams_of[10], (D,), 0.5, 3.0, ((0, 16),), jnp.float32)
    mid_gain = jnp.clip(1.0 + 0.1 * jax.random.normal(streams_of[11], (D,), jnp.float32), 0.5, 1.5)
    mid_shift = gaussian(streams_of[12], (D,), 0.3, 1.8, ((0, 16),), jnp.float32)
    expand_weight = gaussian(streams_of[13], (D, FF), D ** -0.5, 0.125, ((0, 16), (1, 8)), jnp.float32)
    expand_bias = gaussian(streams_of[14], (N_TP, FF // N_TP), 0.5, 3.0, ((0, 8), (1, 16)), jnp.float32)
    contract_weight = gaussian(streams_of[15], (FF, D), FF ** -0.5, 0.0625, ((0, 8), (1, 16)), jnp.float32)
    contract_bias = gaussian(streams_of[16], (D,), 0.5, 3.0, ((0, 16),), jnp.float32)
    cotangent = gaussian(streams_of[17], (SEQS, LEN, D), 1.0, 6.0, ((0, 2), (1, 8)))
    return dict(layer_input=layer_input, doc_ids=doc_ids, pre_gain=pre_gain, pre_shift=pre_shift, query_weight=query_weight, query_bias=query_bias, key_weight=key_weight, value_weight=value_weight, value_bias=value_bias, output_weight=output_weight, output_bias=output_bias, mid_gain=mid_gain, mid_shift=mid_shift, expand_weight=expand_weight, expand_bias=expand_bias, contract_weight=contract_weight, contract_bias=contract_bias, cotangent=cotangent)


@jax.custom_vjp
def low(v):
    return lax.optimization_barrier(v.astype(jnp.bfloat16)).astype(jnp.float32)

@jax.custom_vjp
def low_back(v):
    return v

def low_keep(v):
    return (low(v), None)

def low_pass(kept, grad):
    return (grad,)

def back_keep(v):
    return (v, None)

def back_low(kept, grad):
    return (low(grad),)
low.defvjp(low_keep, low_pass)
low_back.defvjp(back_keep, back_low)

def matmul(operand_left, operand_right):
    return jnp.dot(operand_left, operand_right, precision=lax.Precision.HIGHEST)

def normalize(values, norm_gain, norm_shift):
    centre = values - lax.optimization_barrier(jnp.mean(values, axis=-1, keepdims=True))
    spread = lax.rsqrt(lax.optimization_barrier(jnp.mean(centre * centre, axis=-1, keepdims=True)) + 1e-05)
    scaled = centre * spread
    return scaled * norm_gain + norm_shift

def attend(queries, key_rows, values, seq_docs):
    seq_len = queries.shape[0]
    block_rows = math.gcd(seq_len, 512)
    score_scale = 1.0 / math.sqrt(HEAD_DIM)
    query_heads = queries.reshape(seq_len, HEADS, HEAD_DIM)
    key_heads = key_rows.reshape(seq_len, HEADS, HEAD_DIM)
    value_heads = values.reshape(seq_len, HEADS, HEAD_DIM)
    key_place = jnp.arange(seq_len, dtype=jnp.int32)

    def one_block(block_index):
        block_start = (block_index * block_rows).astype(jnp.int32)
        block_queries = lax.dynamic_slice_in_dim(query_heads, block_start, block_rows, 0)
        block_docs = lax.dynamic_slice_in_dim(seq_docs, block_start, block_rows, 0)
        block_place = block_start + jnp.arange(block_rows, dtype=jnp.int32)
        scores = jnp.einsum('qhd,khd->hqk', block_queries, key_heads, precision=lax.Precision.HIGHEST) * score_scale
        scores = low_back(scores)
        allowed = (block_docs[:, None] == seq_docs[None, :]) & (key_place[None, :] <= block_place[:, None])
        scores = jnp.where(allowed[None], scores, -1e+30)
        weights = low(jax.nn.softmax(scores, axis=-1))
        return jnp.einsum('hqk,khd->qhd', weights, value_heads, precision=lax.Precision.HIGHEST)
    mixture = lax.map(jax.checkpoint(one_block), jnp.arange(seq_len // block_rows, dtype=jnp.int32))
    return mixture.reshape(seq_len, HEADS * HEAD_DIM)

def layer_forward(params, layer_in, seq_docs):
    pre_gain, pre_shift, query_weight, query_bias, key_weight, value_weight, value_bias, output_weight, output_bias, mid_gain, mid_shift, expand_weight, expand_bias, contract_weight, contract_bias = params
    normed = low(normalize(layer_in, low(pre_gain), low(pre_shift)))
    queries = low(low_back(matmul(normed, low(query_weight)) + low(query_bias).reshape(-1)))
    key_rows = low(low_back(matmul(normed, low(key_weight))))
    values = low(low_back(matmul(normed, low(value_weight)) + low(value_bias).reshape(-1)))
    attended = low(low_back(attend(queries, key_rows, values, seq_docs)))
    middle = layer_in + low_back(matmul(attended, low(output_weight)) + low(output_bias))
    normed_two = low(normalize(middle, low(mid_gain), low(mid_shift)))
    pre_act = low_back(matmul(normed_two, low(expand_weight)) + low(expand_bias).reshape(-1))
    activated = low(jax.nn.gelu(pre_act, approximate=False))
    return middle + (matmul(activated, low(contract_weight)) + low(contract_bias))

def reference(layer_input, doc_ids, pre_gain, pre_shift, query_weight, query_bias, key_weight, value_weight, value_bias, output_weight, output_bias, mid_gain, mid_shift, expand_weight, expand_bias, contract_weight, contract_bias, cotangent):
    params = (pre_gain, pre_shift, query_weight, query_bias, key_weight, value_weight, value_bias, output_weight, output_bias, mid_gain, mid_shift, expand_weight, expand_bias, contract_weight, contract_bias)
    inputs = layer_input.astype(jnp.float32)

    def whole_forward(params, inputs):

        def per_sequence(carried, sequence_pair):
            return (carried, layer_forward(params, sequence_pair[0], sequence_pair[1]))
        return lax.scan(per_sequence, jnp.zeros((), jnp.float32), (inputs, doc_ids))[1]
    output, pullback = jax.vjp(whole_forward, params, inputs)
    param_grads, input_grad = pullback(cotangent.astype(jnp.float32))
    pre_gain_grad, pre_shift_grad, query_weight_grad, query_bias_grad, key_weight_grad, value_weight_grad, value_bias_grad, output_weight_grad, output_bias_grad, mid_gain_grad, mid_shift_grad, expand_weight_grad, expand_bias_grad, contract_weight_grad, contract_bias_grad = param_grads
    return (output.astype(jnp.bfloat16), input_grad, pre_gain_grad, pre_shift_grad, query_weight_grad, query_bias_grad, key_weight_grad, value_weight_grad, value_bias_grad, output_weight_grad, output_bias_grad, mid_gain_grad, mid_shift_grad, expand_weight_grad, expand_bias_grad, contract_weight_grad, contract_bias_grad)
```

```python
import math

import jax
import jax.numpy as jnp
from jax import lax
from jax.experimental import pallas as pl
from jax.experimental.pallas import tpu as pltpu
from jax.sharding import PartitionSpec as P

HEAD_DIM = 128
BF = jnp.bfloat16
F32 = jnp.float32
XY = ("fsdp", "ctx")
NEG = -1e30
SCALE = 1.0 / math.sqrt(HEAD_DIM)


def lin(x, y):
    return (y // 2) * 8 + x * 2 + y % 2


def pairs_xy(move):
    out = []
    for x in range(4):
        for y in range(4):
            to = move(x, y)
            if to is not None:
                out.append((lin(x, y), lin(*to)))
    return out


PERM = {
    "X1": pairs_xy(lambda x, y: (x ^ 1, y)),
    "X3": pairs_xy(lambda x, y: (x ^ 3, y)),
    "Y1": pairs_xy(lambda x, y: (x, y ^ 1)),
    "Y3": pairs_xy(lambda x, y: (x, y ^ 3)),
    "C": [(t, t ^ 1) for t in range(8)],
    "Z1": [(t, t ^ 2) for t in range(8)],
    "Z3": [(t, t ^ 6) for t in range(8)],
}
VEC = {"X1": (1, 0), "X3": (3, 0), "Y1": (0, 1), "Y3": (0, 3)}
ORDERS = (
    ("X1", "Y1", "X3", "Y3"),
    ("Y1", "X3", "Y3", "X1"),
    ("X3", "Y3", "X1", "Y1"),
    ("Y3", "X1", "Y1", "X3"),
)


def swap(value, kind):
    return lax.ppermute(value, XY if kind in VEC else "tp", PERM[kind])


def block_of(order, position):
    x = y = 0
    for k, kind in enumerate(order):
        if (position >> k) & 1:
            x ^= VEC[kind][0]
            y ^= VEC[kind][1]
    return lin(x, y)


def own_bits():
    f = lax.axis_index("fsdp")
    c = lax.axis_index("ctx")
    t = lax.axis_index("tp")
    x1, x0, y1, y0 = c // 4, (c // 2) % 2, f, c % 2
    z1, z0, k = t // 4, (t // 2) % 2, t % 2
    return {"X1": x0 ^ x1, "X3": x1, "Y1": y0 ^ y1, "Y3": y1, "Z1": z0 ^ z1, "Z3": z1, "C": k}


def pick(bit, if_zero, if_one):
    return jnp.where(bit == 0, if_zero, if_one)


def merge(bit, own, got):
    return jnp.concatenate([pick(bit, own, got), pick(bit, got, own)], axis=0)


VMEM = pl.BlockSpec(memory_space=pltpu.VMEM)
SMEM = pl.BlockSpec(memory_space=pltpu.SMEM)


def small_limit(mib):
    return pltpu.CompilerParams(vmem_limit_bytes=mib << 20)


def assemble_kernel(rows, width, extra, bits_ref, *refs):
    n = len(ORDERS)
    own, got = refs[:n], refs[n : 2 * n]
    out = refs[2 * n]
    for s, order in enumerate(ORDERS):
        bit = bits_ref[s]
        for q in range(8):
            mine, theirs = own[s][q], got[s][q]
            for high in range(2):
                take = jnp.where(bit == high, mine, theirs)
                block = block_of(order, q + 8 * high)
                out[block * rows : (block + 1) * rows, s * width : (s + 1) * width] = take[:rows]
                if extra and s == 0:
                    refs[2 * n + 1][block] = take[rows:]


def gather_xy(streams, bits, rows, extra=0):
    width = streams[0].shape[1]
    bufs = [s[None] for s in streams]
    for k in range(3):
        got = [swap(b, o[k]) for b, o in zip(bufs, ORDERS)]
        bufs = [merge(bits[o[k]], b, g) for b, g, o in zip(bufs, got, ORDERS)]
    got = [swap(b, o[3]) for b, o in zip(bufs, ORDERS)]
    last = jnp.stack([bits[o[3]] for o in ORDERS]).astype(jnp.int32)
    shapes = [jax.ShapeDtypeStruct((16 * rows, 4 * width), BF)]
    if extra:
        shapes.append(jax.ShapeDtypeStruct((16, extra, width), BF))
    size = 16 * rows * 4 * width * 2
    out = pl.pallas_call(
        lambda *refs: assemble_kernel(rows, width, extra, *refs),
        out_shape=shapes,
        in_specs=[SMEM] + [VMEM] * 8,
        out_specs=[VMEM] * len(shapes),
        compiler_params=small_limit(8),
        cost_estimate=pl.CostEstimate(flops=0, bytes_accessed=2 * size, transcendentals=0),
        name="assemble",
    )(last, *bufs, *got)
    return out if extra else out[0]


def split_kernel(rows, width, bits_ref, grad_ref, *outs):
    n = len(ORDERS)
    for s, order in enumerate(ORDERS):
        bit = bits_ref[s]
        cols = slice(s * width, (s + 1) * width)
        for q in range(8):
            low, high = block_of(order, q), block_of(order, q + 8)
            a = grad_ref[low * rows : (low + 1) * rows, cols]
            b = grad_ref[high * rows : (high + 1) * rows, cols]
            outs[s][q] = jnp.where(bit == 0, b, a)
            outs[n + s][q] = jnp.where(bit == 0, a, b)


def scatter_xy(grad, bits):
    rows, width = grad.shape[0] // 16, grad.shape[1] // 4
    first = jnp.stack([bits[o[3]] for o in ORDERS]).astype(jnp.int32)
    half = jax.ShapeDtypeStruct((8, rows, width), BF)
    out = pl.pallas_call(
        lambda *refs: split_kernel(rows, width, *refs),
        out_shape=[half] * 8,
        in_specs=[SMEM, VMEM],
        out_specs=[VMEM] * 8,
        compiler_params=small_limit(10),
        cost_estimate=pl.CostEstimate(flops=0, bytes_accessed=4 * grad.size, transcendentals=0),
        name="split",
    )(first, grad)
    send, keep = out[:4], out[4:]
    for k in (3, 2, 1, 0):
        got = [swap(v, o[k]) for v, o in zip(send, ORDERS)]
        total = [a.astype(F32) + b.astype(F32) for a, b in zip(keep, got)]
        if k:
            n = total[0].shape[0] // 2
            flags = [bits[o[k - 1]] for o in ORDERS]
            send = [pick(f, v[n:], v[:n]).astype(BF) for f, v in zip(flags, total)]
            keep = [pick(f, v[:n], v[n:]) for f, v in zip(flags, total)]
    return jnp.concatenate([v[0] for v in total], axis=1)


def shard_rows(value, bits):
    base = bits["C"] * 256
    one = base + bits["Z1"] * 64 + bits["Z3"] * 32
    two = base + 128 + bits["Z3"] * 64 + bits["Z1"] * 32
    return jnp.concatenate(
        [lax.dynamic_slice_in_dim(value, one, 32, 0), lax.dynamic_slice_in_dim(value, two, 32, 0)], axis=0
    )


def halves(value, bits):
    send = lax.dynamic_slice_in_dim(value, (1 - bits["C"]) * 256, 256, 0)
    keep = lax.dynamic_slice_in_dim(value, bits["C"] * 256, 256, 0)
    return send, keep


def reduce_tp(product, lhs, bits):
    send, keep = halves(lhs, bits)
    got = swap(product(send).astype(BF), "C")
    total = product(keep) + got.astype(F32)
    parts = [total[:128], total[128:]]
    for kinds in (("Z1", "Z3"), ("Z3", "Z1")):
        n = parts[0].shape[0] // 2
        send = [pick(bits[t], v[n:], v[:n]).astype(BF) for t, v in zip(kinds, parts)]
        got = [swap(v, t) for v, t in zip(send, kinds)]
        parts = [pick(bits[t], v[:n], v[n:]) + g.astype(F32) for t, v, g in zip(kinds, parts, got)]
    return jnp.concatenate(parts, axis=0)


def gather_tp(shard, bits):
    parts = [shard[:32], shard[32:]]
    for kinds in (("Z3", "Z1"), ("Z1", "Z3")):
        got = [swap(v, t) for v, t in zip(parts, kinds)]
        parts = [merge(bits[t], v, g) for t, v, g in zip(kinds, parts, got)]
    own = jnp.concatenate(parts, axis=0)
    return merge(bits["C"], own, swap(own, "C"))


Y_FLIP = PERM["Y1"]
Y_FLIP_DOWN = pairs_xy(lambda x, y: (x, y ^ 1) if y % 2 == 1 else None)
Y_FLIP_UP = pairs_xy(lambda x, y: (x, y ^ 1) if y % 2 == 0 else None)
X_UP = pairs_xy(lambda x, y: (x + 1, y) if x < 3 else None)
X_UP2 = pairs_xy(lambda x, y: (x + 2, y) if x < 2 else None)
X_DOWN = pairs_xy(lambda x, y: (x - 1, y) if x > 0 else None)
X_DOWN2 = pairs_xy(lambda x, y: (x - 2, y) if x > 1 else None)
SLOTS = 6


def slot_blocks():
    c = lax.axis_index("ctx")
    x, low = c // 2, c % 2
    return [c, 2 * x + 1 - low, c - 2, 2 * (x - 1) + 1 - low, c - 4, 2 * (x - 2) + 1 - low]


def nt(a, b):
    return lax.dot_general(a, b, (((1,), (1,)), ((), ())), preferred_element_type=F32)


def tn(a, b):
    return lax.dot_general(a, b, (((0,), (0,)), ((), ())), preferred_element_type=F32)


def nn(a, b):
    return jnp.dot(a, b, preferred_element_type=F32)


def visible(slot, block, length, start_ref, c):
    keys = lax.broadcasted_iota(jnp.int32, (length, length), 0) + block * length
    mask = keys >= start_ref[...]
    if slot == 0:
        mask = mask & (keys <= lax.broadcasted_iota(jnp.int32, (length, length), 1) + c * length)
    return mask


def attn_fwd_kernel(heads, meta_ref, start_ref, q_ref, *refs):
    kv = refs[:SLOTS]
    att_ref, mix_ref, lse_ref, m_ref, l_ref = refs[SLOTS:]
    length = q_ref.shape[0]
    hidden = heads * HEAD_DIM
    c = meta_ref[SLOTS]
    for slot in range(SLOTS):
        block = meta_ref[slot]

        def run(slot=slot, block=block):
            mask = visible(slot, block, length, start_ref, c)
            for h in range(heads):
                cols = slice(h * HEAD_DIM, (h + 1) * HEAD_DIM)
                key = kv[slot][:, cols]
                val = kv[slot][:, hidden + h * HEAD_DIM : hidden + (h + 1) * HEAD_DIM]
                s = jnp.where(mask, nt(key, q_ref[:, cols]) * SCALE, NEG)
                top = jnp.max(s, axis=0, keepdims=True)
                if slot == 0:
                    p = jnp.exp(s - top)
                    m_ref[h : h + 1] = top
                    l_ref[h : h + 1] = jnp.sum(p, axis=0, keepdims=True)
                    mix_ref[cols] = tn(val, p.astype(BF))
                else:
                    old = m_ref[h : h + 1]
                    new = jnp.maximum(old, top)
                    p = jnp.exp(s - new)
                    shrink = jnp.exp(old - new)
                    m_ref[h : h + 1] = new
                    l_ref[h : h + 1] = l_ref[h : h + 1] * shrink + jnp.sum(p, axis=0, keepdims=True)
                    mix_ref[cols] = mix_ref[cols] * shrink + tn(val, p.astype(BF))

        if slot == 0:
            run()
        else:
            pl.when(meta_ref[SLOTS + 1 + slot] == 1)(run)
    for h in range(heads):
        cols = slice(h * HEAD_DIM, (h + 1) * HEAD_DIM)
        out = mix_ref[cols] / l_ref[h : h + 1]
        mix_ref[cols] = out
        att_ref[:, cols] = out.T.astype(BF)
        lse_ref[h : h + 1] = m_ref[h : h + 1] + jnp.log(l_ref[h : h + 1])


def attn_bwd_kernel(heads, meta_ref, start_ref, q_ref, do_ref, mix_ref, lse_ref, *refs):
    kv = refs[:SLOTS]
    dq_ref, dkv = refs[SLOTS], refs[SLOTS + 1 : 2 * SLOTS + 1]
    dqt_ref, delta_ref = refs[2 * SLOTS + 1 :]
    length = q_ref.shape[0]
    hidden = heads * HEAD_DIM
    c = meta_ref[SLOTS]
    for h in range(heads):
        cols = slice(h * HEAD_DIM, (h + 1) * HEAD_DIM)
        dot_t = do_ref[:, cols].astype(F32).T
        delta_ref[h : h + 1] = jnp.sum(dot_t * mix_ref[cols], axis=0, keepdims=True)
    for slot in range(SLOTS):
        block = meta_ref[slot]

        def run(slot=slot, block=block):
            mask = visible(slot, block, length, start_ref, c)
            for h in range(heads):
                cols = slice(h * HEAD_DIM, (h + 1) * HEAD_DIM)
                vcols = slice(hidden + h * HEAD_DIM, hidden + (h + 1) * HEAD_DIM)
                key, val = kv[slot][:, cols], kv[slot][:, vcols]
                q, do = q_ref[:, cols], do_ref[:, cols]
                s = jnp.where(mask, nt(key, q) * SCALE, NEG)
                p = jnp.exp(s - lse_ref[h : h + 1])
                ds = (p * (nt(val, do) - delta_ref[h : h + 1])).astype(BF)
                dkv[slot][:, cols] = (nn(ds, q) * SCALE).astype(dkv[slot].dtype)
                dkv[slot][:, vcols] = nn(p.astype(BF), do).astype(dkv[slot].dtype)
                part = tn(key, ds)
                if slot == 0:
                    dqt_ref[cols] = part
                else:
                    dqt_ref[cols] = dqt_ref[cols] + part

        if slot == 0:
            run()
        else:
            pl.when(meta_ref[SLOTS + 1 + slot] == 1)(run)

            @pl.when(meta_ref[SLOTS + 1 + slot] == 0)
            def _(slot=slot):
                dkv[slot][...] = jnp.zeros(dkv[slot].shape, dkv[slot].dtype)

    for h in range(heads):
        cols = slice(h * HEAD_DIM, (h + 1) * HEAD_DIM)
        dq_ref[:, cols] = (dqt_ref[cols] * SCALE).T.astype(BF)


def norm_stats(v):
    mean = jnp.mean(v, axis=-1, keepdims=True)
    centre = v - mean
    spread = lax.rsqrt(jnp.mean(centre * centre, axis=-1, keepdims=True) + 1e-05)
    return centre * spread, spread


def norm_back(grad, gain, scaled, spread):
    weighted = grad * gain
    inner = jnp.mean(weighted, axis=-1, keepdims=True)
    cross = jnp.mean(weighted * scaled, axis=-1, keepdims=True)
    return spread * (weighted - inner - scaled * cross)


def cols_of(w, n=4):
    k = w.shape[1] // n
    return [w[:, i * k : (i + 1) * k] for i in range(n)]


def body(
    layer_input,
    doc_ids,
    pre_gain,
    pre_shift,
    query_weight,
    query_bias,
    key_weight,
    value_weight,
    value_bias,
    output_weight,
    output_bias,
    mid_gain,
    mid_shift,
    expand_weight,
    expand_bias,
    contract_weight,
    contract_bias,
    cotangent,
):
    bits = own_bits()
    x = layer_input[0]
    cot = cotangent[0]
    length, width = x.shape
    hidden = query_weight.shape[1]
    heads = hidden // HEAD_DIM
    inner = expand_weight.shape[1]
    c = lax.axis_index("ctx")

    nb, ne = query_bias.shape[1], expand_bias.shape[1]
    tail = jnp.concatenate([query_bias[0], value_bias[0], expand_bias[0], jnp.zeros((128 - 2 * nb - ne,), F32)])
    params = jnp.stack(
        [pre_gain, pre_shift, output_bias, mid_gain, mid_shift, contract_bias, tail]
        + [jnp.zeros((128,), F32)] * 9
    ).astype(BF)
    kv_cols = cols_of(jnp.concatenate([key_weight, value_weight], axis=1).astype(BF))
    kv_cols[0] = jnp.concatenate([kv_cols[0], params], axis=0)
    kv_full, params_full = gather_xy(kv_cols, bits, 128, 16)
    qo_full = gather_xy(cols_of(jnp.concatenate([query_weight.astype(BF), output_weight.astype(BF).T], axis=1)), bits, 128)
    contract_full = gather_xy(cols_of(contract_weight.astype(BF).T), bits, 128)
    expand_full = lax.all_gather(expand_weight.astype(BF), XY, axis=0, tiled=True)

    pf = params_full.astype(F32)
    gain1, shift1, out_bias, gain2, shift2, con_bias = [pf[:, i].reshape(1, width) for i in range(6)]
    q_bias = pf[:, 6, :nb].reshape(1, hidden)
    v_bias = pf[:, 6, nb : 2 * nb].reshape(1, hidden)
    e_bias = pf[:, 6, 2 * nb : 2 * nb + ne].reshape(1, inner)
    q_full, o_full = qo_full[:, :hidden], qo_full[:, hidden:]

    docs = doc_ids[0]
    own_docs = lax.dynamic_slice_in_dim(docs, c * length, length, 0)
    start = jnp.sum((docs[:, None] < own_docs[None, :]).astype(jnp.int32), axis=0)
    blocks = jnp.stack(slot_blocks()).astype(jnp.int32)
    need = (blocks >= 0) & (blocks < c) & (blocks * length + length - 1 >= start[0])
    meta = jnp.concatenate([blocks, c.astype(jnp.int32)[None], need.astype(jnp.int32), jnp.zeros((3,), jnp.int32)])
    start = start[None]

    xf = x.astype(F32)
    scaled1, spread1 = norm_stats(xf)
    normed = (scaled1 * gain1 + shift1).astype(BF)
    kv_bias = jnp.concatenate([jnp.zeros((1, hidden), F32), v_bias], axis=1)
    kv_own = (nn(normed, kv_full) + kv_bias).astype(BF)
    kv_e1 = lax.ppermute(kv_own, XY, Y_FLIP)
    kv_f1 = lax.ppermute(kv_own, XY, X_UP)
    kv_f2 = lax.ppermute(kv_own, XY, X_UP2)
    queries = (nn(normed, q_full) + q_bias).astype(BF)
    kv_g1 = lax.ppermute(kv_e1, XY, X_UP)
    kv_e3 = lax.ppermute(kv_f2, XY, Y_FLIP_DOWN)
    slots = [kv_own, kv_e1, kv_f1, kv_g1, kv_f2, kv_e3]
    attended, mixture, lse = pl.pallas_call(
        lambda *refs: attn_fwd_kernel(heads, *refs),
        out_shape=[
            jax.ShapeDtypeStruct((length, hidden), BF),
            jax.ShapeDtypeStruct((hidden, length), F32),
            jax.ShapeDtypeStruct((heads, length), F32),
        ],
        in_specs=[SMEM] + [VMEM] * (2 + SLOTS),
        out_specs=[VMEM] * 3,
        scratch_shapes=[pltpu.VMEM((heads, length), F32), pltpu.VMEM((heads, length), F32)],
        compiler_params=small_limit(24),
        cost_estimate=pl.CostEstimate(flops=10**10, bytes_accessed=6 << 20, transcendentals=3 * 10**6),
        name="attn_fwd",
    )(meta, start, queries, *slots)

    attn_total = reduce_tp(lambda v: nt(v, o_full), attended, bits)
    x_shard = shard_rows(x, bits).astype(F32)
    middle = x_shard + (attn_total + out_bias)
    scaled2, spread2 = norm_stats(middle)
    normed_two = gather_tp((scaled2 * gain2 + shift2).astype(BF), bits)

    grad_act = nn(cot, contract_full)
    pre_act = nn(normed_two, expand_full) + e_bias
    cdf = 0.5 * (1.0 + lax.erf(pre_act * (1.0 / math.sqrt(2.0))))
    activated = (pre_act * cdf).astype(BF)
    slope = cdf + pre_act * jnp.exp(-0.5 * pre_act * pre_act) * (1.0 / math.sqrt(2.0 * math.pi))
    grad_pre = (slope * grad_act).astype(BF)
    grad_norm2 = reduce_tp(lambda v: nt(v, expand_full), grad_pre, bits)
    grad_contract = tn(cot, activated).astype(BF)
    grad_expand = tn(normed_two, grad_pre).astype(BF)
    contract_grad = lax.psum_scatter(grad_contract, XY, scatter_dimension=0, tiled=True)
    expand_grad = scatter_xy(grad_expand, bits)
    e_bias_grad = jnp.sum(grad_pre.astype(F32), axis=0)

    cot_shard = shard_rows(cot, bits).astype(F32)
    grad_middle = cot_shard + norm_back(grad_norm2, gain2, scaled2, spread2)
    grad_attn_shard = grad_middle.astype(BF)
    gain2_part = jnp.sum(grad_norm2 * scaled2, axis=0)
    shift2_part = jnp.sum(grad_norm2, axis=0)
    out_bias_part = jnp.sum(grad_attn_shard.astype(F32), axis=0)
    con_bias_part = jnp.sum(cot_shard, axis=0)
    grad_attn = gather_tp(grad_attn_shard, bits)

    mlp_total = reduce_tp(lambda v: nt(v, contract_full), activated, bits)
    layer_output = gather_tp((middle + (mlp_total + con_bias)).astype(BF), bits)

    grad_att = nn(grad_attn, o_full).astype(BF)
    part = jax.ShapeDtypeStruct((length, 2 * hidden), BF)
    grad_q, own_part, p_e1, p_f1, p_g1, p_f2, p_e3 = pl.pallas_call(
        lambda *refs: attn_bwd_kernel(heads, *refs),
        out_shape=[jax.ShapeDtypeStruct((length, hidden), BF), jax.ShapeDtypeStruct((length, 2 * hidden), F32)] + [part] * 5,
        in_specs=[SMEM] + [VMEM] * (5 + SLOTS),
        out_specs=[VMEM] * 7,
        scratch_shapes=[pltpu.VMEM((hidden, length), F32), pltpu.VMEM((heads, length), F32)],
        compiler_params=small_limit(32),
        cost_estimate=pl.CostEstimate(flops=2 * 10**10, bytes_accessed=10 << 20, transcendentals=3 * 10**6),
        name="attn_bwd",
    )(meta, start, queries, grad_att, mixture, lse, *slots)
    from_g1 = lax.ppermute(p_g1, XY, X_DOWN)
    from_e3 = lax.ppermute(p_e3, XY, Y_FLIP_UP)
    from_f1 = lax.ppermute(p_f1, XY, X_DOWN)
    from_e1 = lax.ppermute((p_e1.astype(F32) + from_g1.astype(F32)).astype(BF), XY, Y_FLIP)
    from_f2 = lax.ppermute((p_f2.astype(F32) + from_e3.astype(F32)).astype(BF), XY, X_DOWN2)
    grad_kv = (own_part + from_f1.astype(F32) + from_e1.astype(F32) + from_f2.astype(F32)).astype(BF)

    grad_o = tn(grad_attn, attended).astype(BF)
    grad_qw = tn(normed, grad_q).astype(BF)
    qo_grad = scatter_xy(jnp.concatenate([grad_qw, grad_o], axis=1), bits)
    kv_grad = scatter_xy(tn(normed, grad_kv).astype(BF), bits)
    q_bias_grad = jnp.sum(grad_q.astype(F32), axis=0)
    v_bias_grad = jnp.sum(grad_kv[:, hidden:].astype(F32), axis=0)

    qkv_full = jnp.concatenate([q_full, kv_full], axis=1)
    grad_qkv = jnp.concatenate([grad_q, grad_kv], axis=1)
    grad_norm1 = reduce_tp(lambda v: nt(v, qkv_full), grad_qkv, bits)
    x_scaled, x_spread = norm_stats(x_shard)
    grad_x = grad_middle + norm_back(grad_norm1, gain1, x_scaled, x_spread)
    gain1_part = jnp.sum(grad_norm1 * x_scaled, axis=0)
    shift1_part = jnp.sum(grad_norm1, axis=0)
    input_grad = gather_tp(grad_x.astype(BF), bits).astype(F32)

    vectors = [gain1_part, shift1_part, out_bias_part, gain2_part, shift2_part, con_bias_part]
    small = jnp.stack([v.reshape(16, 128) for v in vectors], axis=1)
    for kind in ("C", "Z1", "Z3"):
        small = small + swap(small, kind)
    biases = jnp.concatenate(
        [
            q_bias_grad.reshape(16, nb),
            v_bias_grad.reshape(16, nb),
            e_bias_grad.reshape(16, ne),
            jnp.zeros((16, 128 - 2 * nb - ne), F32),
        ],
        axis=1,
    )
    small = jnp.concatenate([small, biases[:, None], jnp.zeros((16, 1, 128), F32)], axis=1)
    order = ORDERS[0]
    natural = small
    small = jnp.concatenate([natural[block_of(order, p)][None] for p in range(16)], axis=0)
    for k in (3, 2, 1, 0):
        n = small.shape[0] // 2
        bit = bits[order[k]]
        small = pick(bit, small[:n], small[n:]) + swap(pick(bit, small[n:], small[:n]), order[k])
    small = small[0]

    return (
        layer_output[None],
        input_grad[None],
        small[0],
        small[1],
        qo_grad[:, :hidden],
        small[6:7, :nb],
        kv_grad[:, :hidden],
        kv_grad[:, hidden:],
        small[6:7, nb : 2 * nb],
        qo_grad[:, hidden:].T,
        small[2],
        small[3],
        small[4],
        expand_grad,
        small[6:7, 2 * nb : 2 * nb + ne],
        contract_grad.astype(F32).T,
        small[5],
    )


def solution(mesh):
    both = ("fsdp", "ctx")
    rows, cols, vec = P(both, "tp"), P("tp", both), P(both)
    act = P("fsdp", "ctx", None)
    return jax.shard_map(
        body,
        mesh=mesh,
        in_specs=(
            act, P("fsdp", None), vec, vec, rows, cols, rows, rows, cols, cols, vec, vec, vec,
            rows, cols, cols, vec, act,
        ),
        out_specs=(
            act, act, vec, vec, rows, cols, rows, rows, cols, cols, vec, vec, vec, rows, cols, cols, vec,
        ),
        check_vma=False,
    )
```

```python
import math

import jax
import jax.numpy as jnp
from jax import lax
from jax.experimental import pallas as pl
from jax.experimental.pallas import tpu as pltpu
from jax.sharding import PartitionSpec as P

HEAD_DIM = 128
BF = jnp.bfloat16
F32 = jnp.float32
XY = ("fsdp", "ctx")
NEG = -1e30
SCALE = 1.0 / math.sqrt(HEAD_DIM)


def lin(x, y):
    return (y // 2) * 8 + x * 2 + y % 2


def pairs_xy(move):
    out = []
    for x in range(4):
        for y in range(4):
            to = move(x, y)
            if to is not None:
                out.append((lin(x, y), lin(*to)))
    return out


PERM = {
    "X1": pairs_xy(lambda x, y: (x ^ 1, y)),
    "X3": pairs_xy(lambda x, y: (x ^ 3, y)),
    "Y1": pairs_xy(lambda x, y: (x, y ^ 1)),
    "Y3": pairs_xy(lambda x, y: (x, y ^ 3)),
    "C": [(t, t ^ 1) for t in range(8)],
    "Z1": [(t, t ^ 2) for t in range(8)],
    "Z3": [(t, t ^ 6) for t in range(8)],
}
VEC = {"X1": (1, 0), "X3": (3, 0), "Y1": (0, 1), "Y3": (0, 3)}
ORDER_A = ("X1", "Y1", "X3", "Y3")
ORDER_B = ("Y1", "X3", "Y3", "X1")
ORDER_C = ("X3", "Y3", "X1", "Y1")
ORDER_D = ("Y3", "X1", "Y1", "X3")
ORDER_E = ("X1", "X3", "Y1", "Y3")
ORDER_F = ("X3", "X1", "Y3", "Y1")
ORDER_P = ("X3", "X1", "Y3", "Y1")
ORDER_Q = ("X3", "X1", "Y1", "Y3")
ORDER_R = ("Y3", "Y1", "X3", "X1")
ORDER_S = ("Y3", "Y1", "X1", "X3")


def swap(value, kind):
    return lax.ppermute(value, XY if kind in VEC else "tp", PERM[kind])


def offsets(order):
    out = []
    for p in range(16):
        x = y = 0
        for k, kind in enumerate(order):
            if (p >> k) & 1:
                x ^= VEC[kind][0]
                y ^= VEC[kind][1]
        out.append(lin(x, y))
    return out


def own_bits():
    c = lax.axis_index("ctx")
    t = lax.axis_index("tp")
    z1, z0, k = t // 4, (t // 2) % 2, t % 2
    me = (lax.axis_index("fsdp") * 8 + c).astype(jnp.int32)
    return {"Z1": z0 ^ z1, "Z3": z1, "C": k, "me": me[None]}


def pick(bit, if_zero, if_one):
    return jnp.where(bit == 0, if_zero, if_one)


def merge(bit, own, got):
    return jnp.concatenate([pick(bit, own, got), pick(bit, got, own)], axis=0)


VMEM = pl.BlockSpec(memory_space=pltpu.VMEM)
SMEM = pl.BlockSpec(memory_space=pltpu.SMEM)


def local_call(kernel, name, out_shape, args, in_smem=0, mib=20, scratch=(), flops=0, moved=0, exps=0):
    return pl.pallas_call(
        kernel,
        out_shape=out_shape,
        in_specs=[SMEM] * in_smem + [VMEM] * (len(args) - in_smem),
        out_specs=jax.tree.map(lambda _: VMEM, out_shape),
        scratch_shapes=list(scratch),
        compiler_params=pltpu.CompilerParams(vmem_limit_bytes=mib << 20),
        cost_estimate=pl.CostEstimate(flops=flops, bytes_accessed=moved, transcendentals=exps),
        name=name,
    )(*args)


def shape(dims, dtype=BF):
    return jax.ShapeDtypeStruct(dims, dtype)


def after(value, *events):
    return lax.optimization_barrier((value, events))[0]


def join_kernel(count, *refs):
    for own, got, out in zip(refs[:count], refs[count : 2 * count], refs[2 * count :]):
        n = own.shape[0]
        out[:n] = own[...]
        out[n:] = got[...]


def join(owns, gots):
    shapes = [shape((2 * v.shape[0],) + v.shape[1:]) for v in owns]
    size = sum(v.size for v in owns)
    count = len(owns)
    return local_call(lambda *r: join_kernel(count, *r), "join", shapes, [*owns, *gots], mib=4, moved=8 * size)


def swaps(bufs, orders, k):
    return [swap(b, o[k]) for b, o in zip(bufs, orders)]


def place_kernel(rows, plan, count, extra, me_ref, *refs):
    owns, gots, outs = refs[:count], refs[count : 2 * count], refs[2 * count :]
    me = me_ref[0]
    for s, (order, target, column) in enumerate(plan):
        width = owns[s].shape[2]
        away = offsets(order)
        for p in range(16):
            src = owns[s] if p < 8 else gots[s]
            block = me ^ away[p]
            row = pl.multiple_of(block * rows, rows)
            outs[target][pl.ds(row, rows), column : column + width] = src[p % 8, :rows]
            if extra and s == 0:
                outs[-1][block] = src[p % 8, rows:]


def place(owns, gots, bits, rows, plan, widths, extra=0):
    shapes = [shape((16 * rows, w)) for w in widths]
    if extra:
        shapes.append(shape((16, extra, owns[0].shape[2])))
    count = len(owns)
    return local_call(
        lambda *r: place_kernel(rows, plan, count, extra, *r),
        "place",
        shapes,
        [bits["me"], *owns, *gots],
        in_smem=1,
        mib=6,
        moved=64 * rows * sum(widths),
    )


def part(grads, gots, bits, plan, step, half=None, small=None):
    rows = grads[0].shape[0] // 16
    low, count = (1 << step, 1 << step) if step >= 0 else (0, 1)
    if half is not None:
        count //= 2
        low += half * count
    n, ng = len(plan), len(grads)
    extra = 16 if small is not None and step >= 0 else 0
    shapes = [shape((count, rows + (extra if s == 0 else 0), p[3]), BF if step >= 0 else F32) for s, p in enumerate(plan)]
    if small is not None and step < 0:
        shapes.append(shape((8, 128), F32))

    def kernel(me_ref, *refs):
        me = me_ref[0]
        first = ng + n * len(gots)
        outs = refs[first + (small is not None) :]
        for s, (order, source, column, width) in enumerate(plan):
            away = offsets(order)
            for q in range(count):
                p = low + q
                row = pl.multiple_of((me ^ away[p]) * rows, rows)
                piece = refs[source][pl.ds(row, rows), column : column + width]
                if gots:
                    piece = piece.astype(F32)
                    for j, (_, base) in enumerate(gots):
                        piece = piece + refs[ng + n * j + s][p - base, :rows].astype(F32)
                outs[s][q, :rows] = piece.astype(outs[s].dtype)
                if small is not None and s == 0:
                    lane = pl.multiple_of((me ^ away[p]) * 128, 128)
                    vectors = jnp.concatenate([refs[first][:, pl.ds(lane, 128)], jnp.zeros((8, 128), F32)], axis=0)
                    for j, (_, base) in enumerate(gots):
                        vectors = vectors + refs[ng + n * j][p - base, rows:, :128].astype(F32)
                    if step >= 0:
                        outs[0][q, rows:, :128] = vectors.astype(BF)
                        outs[0][q, rows:, 128:] = jnp.zeros((16, width - 128), BF)
                    else:
                        outs[-1][...] = vectors[:8]

    args = [bits["me"], *grads, *[g for got, _ in gots for g in got]] + ([small] if small is not None else [])
    moved = 2 * count * rows * sum(p[3] for p in plan) * (2 + len(gots))
    return local_call(kernel, "part", shapes, args, in_smem=1, mib=6, moved=moved)


BIG = ((ORDER_P, ORDER_Q), (ORDER_R, ORDER_S))


def big_part(grads, gots, bits, step, keep=False):
    rows, width = grads[0].shape[0] // 16, grads[0].shape[1]
    half = width // 2
    low, count = (0 if keep else 1 << step), 1 << step
    wide = step < 2
    dtype = F32 if keep else BF
    in_specs, args, spans = [], [], []

    def add(array, block, index, span):
        in_specs.append(pl.BlockSpec(block, index))
        args.append(array)
        spans.append(span)

    for m, pair in enumerate(BIG):
        for s, order in enumerate(pair):
            near = [offsets(order)[1 << k] for k in range(4)]

            def block_at(q, me, near=near):
                p = low + q
                where = me[0]
                for k, away in enumerate(near):
                    where = where ^ (((p >> k) & 1) * away)
                return where

            add(grads[m], (rows, half), lambda q, me, s=s, f=block_at: (f(q, me), s), (m, s * half))
            for j, got in enumerate(gots):
                if 3 - j >= 2:
                    array, column = got[2 * m + s], 0
                else:
                    array, column = got[m], s
                add(array, (1, rows, half), lambda q, me, c=column: (low + q, 0, c), (m, s * half))
    per = 1 + len(gots)

    def kernel(me_ref, *refs):
        outs = refs[len(args) :]
        for i in range(4):
            piece = refs[per * i][...]
            if gots:
                piece = piece.astype(F32)
                for j in range(1, per):
                    piece = piece + refs[per * i + j][0].astype(F32)
            m, column = spans[per * i]
            if wide:
                outs[m][0, :, column : column + half] = piece.astype(dtype)
            else:
                outs[i][0] = piece.astype(dtype)

    outs = [shape((count, rows, width if wide else half), dtype)] * (2 if wide else 4)
    return pl.pallas_call(
        kernel,
        grid_spec=pltpu.PrefetchScalarGridSpec(
            num_scalar_prefetch=1,
            grid=(count,),
            in_specs=in_specs,
            out_specs=[pl.BlockSpec((1,) + o.shape[1:], lambda q, me: (q, 0, 0)) for o in outs],
        ),
        out_shape=outs,
        compiler_params=pltpu.CompilerParams(vmem_limit_bytes=12 << 20),
        cost_estimate=pl.CostEstimate(flops=0, bytes_accessed=4 * count * rows * width * (1 + per), transcendentals=0),
        name="big_part",
    )(bits["me"], *args)


def big_swaps(values, step):
    if step >= 2:
        return [swap(v, o[step]) for v, o in zip(values, BIG[0] + BIG[1])]
    return [swap(v, pair[0][step]) for v, pair in zip(values, BIG)]


def shard_rows(value, bits):
    base = bits["C"] * 256
    one = base + bits["Z1"] * 64 + bits["Z3"] * 32
    two = base + 128 + bits["Z3"] * 64 + bits["Z1"] * 32
    return jnp.concatenate(
        [lax.dynamic_slice_in_dim(value, one, 32, 0), lax.dynamic_slice_in_dim(value, two, 32, 0)], axis=0
    )


def halves(value, bits):
    send = lax.dynamic_slice_in_dim(value, (1 - bits["C"]) * 256, 256, 0)
    keep = lax.dynamic_slice_in_dim(value, bits["C"] * 256, 256, 0)
    return send, keep


def reduce_tp(products, operands, bits, beside=None):
    count = len(products)
    pairs = [halves(v, bits) for v in operands]
    send = jnp.concatenate([p(v[0]).astype(BF) for p, v in zip(products, pairs)], axis=0)
    first = swap(send, "C")
    kept = [p(v[1]) for p, v in zip(products, pairs)]
    events = [send]
    if beside:
        first = after(first, beside(0, events, kept))
    totals = [v + first[i * 256 : (i + 1) * 256].astype(F32) for i, v in enumerate(kept)]
    events.append(first)
    streams = [[v[:128] for v in totals], [v[128:] for v in totals]]
    for stage, kinds in enumerate((("Z1", "Z3"), ("Z3", "Z1"))):
        n = streams[0][0].shape[0] // 2
        give = [
            jnp.concatenate([pick(bits[t], v[n:], v[:n]).astype(BF) for v in parts], axis=0)
            for t, parts in zip(kinds, streams)
        ]
        got = [swap(v, t) for v, t in zip(give, kinds)]
        if beside:
            got = after(got, beside(1 + stage, events, kept))
        events.append(got)
        streams = [
            [pick(bits[t], v[:n], v[n:]) + g[i * n : (i + 1) * n].astype(F32) for i, v in enumerate(parts)]
            for t, parts, g in zip(kinds, streams, got)
        ]
    out = [jnp.concatenate([streams[0][i], streams[1][i]], axis=0) for i in range(count)]
    return out, events, kept


def merge_rows(bit, own, got):
    return jnp.concatenate([pick(bit, own, got), pick(bit, got, own)], axis=1)


def gather_tp(shards, bits, beside=None):
    parts = [shards[:, :32], shards[:, 32:]]
    events = [shards]
    for stage, kinds in enumerate((("Z3", "Z1"), ("Z1", "Z3"))):
        got = [swap(v, t) for v, t in zip(parts, kinds)]
        if beside:
            got = after(got, beside(3 + stage, events, None))
        events.append(got)
        parts = [merge_rows(bits[t], v, g) for t, v, g in zip(kinds, parts, got)]
    own = jnp.concatenate(parts, axis=1)
    last = swap(own, "C")
    if beside:
        last = after(last, beside(5, events, None))
    events.append(last)
    return merge_rows(bits["C"], own, last), events


Y_FLIP = PERM["Y1"]
Y_FLIP_DOWN = pairs_xy(lambda x, y: (x, y ^ 1) if y % 2 == 1 else None)
Y_FLIP_UP = pairs_xy(lambda x, y: (x, y ^ 1) if y % 2 == 0 else None)
X_UP = pairs_xy(lambda x, y: (x + 1, y) if x < 3 else None)
X_UP2 = pairs_xy(lambda x, y: (x + 2, y) if x < 2 else None)
X_DOWN = pairs_xy(lambda x, y: (x - 1, y) if x > 0 else None)
X_DOWN2 = pairs_xy(lambda x, y: (x - 2, y) if x > 1 else None)
SLOTS = 6


def slot_blocks():
    c = lax.axis_index("ctx")
    x, low = c // 2, c % 2
    return [c, 2 * x + 1 - low, c - 2, 2 * (x - 1) + 1 - low, c - 4, 2 * (x - 2) + 1 - low]


def nt(a, b):
    return lax.dot_general(a, b, (((1,), (1,)), ((), ())), preferred_element_type=F32)


def tn(a, b):
    return lax.dot_general(a, b, (((0,), (0,)), ((), ())), preferred_element_type=F32)


def nn(a, b):
    return jnp.dot(a, b, preferred_element_type=F32)


def visible(slot, block, length, start_ref, c):
    keys = lax.broadcasted_iota(jnp.int32, (length, length), 0) + block * length
    mask = keys >= start_ref[...]
    if slot == 0:
        mask = mask & (keys <= lax.broadcasted_iota(jnp.int32, (length, length), 1) + c * length)
    return mask


def attn_fwd_kernel(heads, meta_ref, start_ref, q_ref, *refs):
    kv = refs[:SLOTS]
    att_ref, mix_ref, lse_ref, m_ref, l_ref = refs[SLOTS:]
    length = q_ref.shape[0]
    hidden = heads * HEAD_DIM
    c = meta_ref[SLOTS]
    for slot in range(SLOTS):
        block = meta_ref[slot]

        def run(slot=slot, block=block):
            mask = visible(slot, block, length, start_ref, c)
            for h in range(heads):
                cols = slice(h * HEAD_DIM, (h + 1) * HEAD_DIM)
                key = kv[slot][:, cols]
                val = kv[slot][:, hidden + h * HEAD_DIM : hidden + (h + 1) * HEAD_DIM]
                s = jnp.where(mask, nt(key, q_ref[:, cols]) * SCALE, NEG)
                top = jnp.max(s, axis=0, keepdims=True)
                if slot == 0:
                    p = jnp.exp(s - top)
                    m_ref[h : h + 1] = top
                    l_ref[h : h + 1] = jnp.sum(p, axis=0, keepdims=True)
                    mix_ref[cols] = tn(val, p.astype(BF))
                else:
                    old = m_ref[h : h + 1]
                    new = jnp.maximum(old, top)
                    p = jnp.exp(s - new)
                    shrink = jnp.exp(old - new)
                    m_ref[h : h + 1] = new
                    l_ref[h : h + 1] = l_ref[h : h + 1] * shrink + jnp.sum(p, axis=0, keepdims=True)
                    mix_ref[cols] = mix_ref[cols] * shrink + tn(val, p.astype(BF))

        if slot == 0:
            run()
        else:
            pl.when(meta_ref[SLOTS + 1 + slot] == 1)(run)
    for h in range(heads):
        cols = slice(h * HEAD_DIM, (h + 1) * HEAD_DIM)
        out = mix_ref[cols] / l_ref[h : h + 1]
        mix_ref[cols] = out
        att_ref[:, cols] = out.T.astype(BF)
        lse_ref[h : h + 1] = m_ref[h : h + 1] + jnp.log(l_ref[h : h + 1])


def attn_bwd_kernel(heads, meta_ref, start_ref, q_ref, do_ref, mix_ref, lse_ref, *refs):
    kv = refs[:SLOTS]
    dq_ref, dkv = refs[SLOTS], refs[SLOTS + 1 : 2 * SLOTS + 1]
    dqt_ref, delta_ref = refs[2 * SLOTS + 1 :]
    length = q_ref.shape[0]
    hidden = heads * HEAD_DIM
    c = meta_ref[SLOTS]
    for h in range(heads):
        cols = slice(h * HEAD_DIM, (h + 1) * HEAD_DIM)
        dot_t = do_ref[:, cols].astype(F32).T
        delta_ref[h : h + 1] = jnp.sum(dot_t * mix_ref[cols], axis=0, keepdims=True)
    for slot in range(SLOTS):
        block = meta_ref[slot]

        def run(slot=slot, block=block):
            mask = visible(slot, block, length, start_ref, c)
            for h in range(heads):
                cols = slice(h * HEAD_DIM, (h + 1) * HEAD_DIM)
                vcols = slice(hidden + h * HEAD_DIM, hidden + (h + 1) * HEAD_DIM)
                key, val = kv[slot][:, cols], kv[slot][:, vcols]
                q, do = q_ref[:, cols], do_ref[:, cols]
                s = jnp.where(mask, nt(key, q) * SCALE, NEG)
                p = jnp.exp(s - lse_ref[h : h + 1])
                ds = (p * (nt(val, do) - delta_ref[h : h + 1])).astype(BF)
                dkv[slot][:, cols] = (nn(ds, q) * SCALE).astype(dkv[slot].dtype)
                dkv[slot][:, vcols] = nn(p.astype(BF), do).astype(dkv[slot].dtype)
                part = tn(key, ds)
                if slot == 0:
                    dqt_ref[cols] = part
                else:
                    dqt_ref[cols] = dqt_ref[cols] + part

        if slot == 0:
            run()
        else:
            pl.when(meta_ref[SLOTS + 1 + slot] == 1)(run)

            @pl.when(meta_ref[SLOTS + 1 + slot] == 0)
            def _(slot=slot):
                dkv[slot][...] = jnp.zeros(dkv[slot].shape, dkv[slot].dtype)

    for h in range(heads):
        cols = slice(h * HEAD_DIM, (h + 1) * HEAD_DIM)
        dq_ref[:, cols] = (dqt_ref[cols] * SCALE).T.astype(BF)


def norm_stats(v):
    mean = jnp.mean(v, axis=-1, keepdims=True)
    centre = v - mean
    spread = lax.rsqrt(jnp.mean(centre * centre, axis=-1, keepdims=True) + 1e-05)
    return centre * spread, spread


def norm_back(grad, gain, scaled, spread):
    weighted = grad * gain
    inner = jnp.mean(weighted, axis=-1, keepdims=True)
    cross = jnp.mean(weighted * scaled, axis=-1, keepdims=True)
    return spread * (weighted - inner - scaled * cross)


def cols_of(w, n=4):
    k = w.shape[1] // n
    return [w[:, i * k : (i + 1) * k] for i in range(n)]


def body(
    layer_input,
    doc_ids,
    pre_gain,
    pre_shift,
    query_weight,
    query_bias,
    key_weight,
    value_weight,
    value_bias,
    output_weight,
    output_bias,
    mid_gain,
    mid_shift,
    expand_weight,
    expand_bias,
    contract_weight,
    contract_bias,
    cotangent,
):
    bits = own_bits()
    x = layer_input[0]
    cot = cotangent[0]
    length, width = x.shape
    hidden = query_weight.shape[1]
    heads = hidden // HEAD_DIM
    inner = expand_weight.shape[1]
    c = lax.axis_index("ctx")

    nb, ne = query_bias.shape[1], expand_bias.shape[1]
    tail = jnp.concatenate([query_bias[0], value_bias[0], expand_bias[0], jnp.zeros((128 - 2 * nb - ne,), F32)])
    params = jnp.stack([pre_gain, pre_shift, output_bias, mid_gain, mid_shift, contract_bias, tail, tail]).astype(BF)
    params = jnp.concatenate([params, jnp.zeros((8, 128), BF)], axis=0)
    params = jnp.concatenate([params, jnp.zeros((16, hidden - 128), BF)], axis=1)
    first_orders, big_orders = (ORDER_A, ORDER_B, ORDER_C, ORDER_D), (ORDER_E, ORDER_F)
    kv_orders, qo_orders = (ORDER_A, ORDER_B), (ORDER_A,)
    bufs = [
        jnp.concatenate([key_weight.astype(BF), params], axis=0)[None],
        value_weight.astype(BF)[None],
        query_weight.astype(BF)[None],
        output_weight.astype(BF).T[None],
    ]
    con = [v[None] for v in cols_of(contract_weight.astype(BF).T, 2)]
    bufs = join(bufs, swaps(bufs, first_orders, 0))
    got = swaps(bufs, first_orders, 1)
    one = swaps(con[:1], big_orders[:1], 0)
    bufs = join(bufs, after(got, one))
    got = swaps(bufs, first_orders, 2)
    two = swaps(con[1:], big_orders[1:], 0)
    bufs = join(bufs, after(got, two))
    con = join(con, one + two)
    got = swaps(bufs, first_orders, 3)
    plan = [(ORDER_A, 0, 0), (ORDER_B, 0, hidden), (ORDER_C, 1, 0), (ORDER_D, 2, 0)]
    kv_full, q_full, o_full, params_full = place(bufs, got, bits, 128, plan, [2 * hidden, hidden, hidden], 16)
    got_con = swaps(after(con, got), big_orders, 1)
    exp_orders = (ORDER_A, ORDER_B)
    exp = [v[None] for v in cols_of(expand_weight.astype(BF), 2)]
    got_exp = swaps(after(exp, got), exp_orders, 0)

    pf = params_full[:, :, :128].astype(F32)
    gain1, shift1, out_bias, gain2, shift2, con_bias = [pf[:, i].reshape(1, width) for i in range(6)]
    q_bias = pf[:, 6, :nb].reshape(1, hidden)
    v_bias = pf[:, 6, nb : 2 * nb].reshape(1, hidden)
    e_bias = pf[:, 6, 2 * nb : 2 * nb + ne].reshape(1, inner)

    docs = doc_ids[0]
    own_docs = lax.dynamic_slice_in_dim(docs, c * length, length, 0)
    start = jnp.sum((docs[:, None] < own_docs[None, :]).astype(jnp.int32), axis=0)
    blocks = jnp.stack(slot_blocks()).astype(jnp.int32)
    need = (blocks >= 0) & (blocks < c) & (blocks * length + length - 1 >= start[0])
    meta = jnp.concatenate([blocks, c.astype(jnp.int32)[None], need.astype(jnp.int32), jnp.zeros((3,), jnp.int32)])
    start = start[None]

    xf = x.astype(F32)
    scaled1, spread1 = norm_stats(xf)
    normed = (scaled1 * gain1 + shift1).astype(BF)
    kv_bias = jnp.concatenate([jnp.zeros((1, hidden), F32), v_bias], axis=1)
    kv_own = (nn(normed, kv_full) + kv_bias).astype(BF)
    con = join(con, got_con)
    exp = join(exp, got_exp)
    kv_own = after(kv_own, con, exp)
    kv_e1 = lax.ppermute(kv_own, XY, Y_FLIP)
    kv_f1 = lax.ppermute(kv_own, XY, X_UP)
    kv_f2 = lax.ppermute(kv_own, XY, X_UP2)
    got_con = swaps(con, big_orders, 2)
    kv_g1 = lax.ppermute(kv_e1, XY, X_UP)
    kv_e3 = lax.ppermute(kv_f2, XY, Y_FLIP_DOWN)
    queries = (nn(normed, q_full) + q_bias).astype(BF)
    con = join(con, after(got_con, kv_e1))
    got_con = swaps(con, big_orders, 3)

    slots = [kv_own, kv_e1, kv_f1, kv_g1, kv_f2, kv_e3]
    attended, mixture, lse = local_call(
        lambda *refs: attn_fwd_kernel(heads, *refs),
        "attn_fwd",
        [shape((length, hidden)), shape((hidden, length), F32), shape((heads, length), F32)],
        [meta, start, after(queries, con), *slots],
        in_smem=1,
        mib=12,
        scratch=[pltpu.VMEM((heads, length), F32), pltpu.VMEM((heads, length), F32)],
        flops=10**9,
        moved=6 << 20,
        exps=3 * 10**6,
    )

    feed = {}

    def beside_a(stage, events, kept):
        now = events[-1]
        if stage == 0:
            plan = [(ORDER_E, 0, 0), (ORDER_F, 0, inner // 2)]
            feed["contract"] = place(con, got_con, bits, 128, plan, [inner])[0]
            feed["got"] = swaps(after(exp, now), exp_orders, 1)
            return [feed["contract"], feed["got"]]
        if stage == 1:
            feed["exp"] = join(exp, after(feed["got"], now))
            feed["got"] = swaps(feed["exp"], exp_orders, 2)
        if stage == 2:
            return feed["got"]
        if stage == 3:
            feed["exp"] = join(feed["exp"], after(feed["got"], now))
            feed["got"] = swaps(feed["exp"], exp_orders, 3)
        return []

    (attn_total,), _, _ = reduce_tp([lambda v: nt(v, o_full)], [attended], bits, beside_a)
    contract_full = feed["contract"]
    x_shard = shard_rows(x, bits).astype(F32)
    middle = x_shard + (attn_total + out_bias)
    scaled2, spread2 = norm_stats(middle)
    normed_two, _ = gather_tp((scaled2 * gain2 + shift2).astype(BF)[None], bits, beside_a)
    normed_two = normed_two[0]

    plan = [(ORDER_A, 0, 0), (ORDER_B, 0, inner // 2)]
    expand_full = place(feed["exp"], feed["got"], bits, 128, plan, [inner])[0]
    grad_act = nn(cot, contract_full)
    pre_act = nn(normed_two, expand_full) + e_bias
    cdf = 0.5 * (1.0 + lax.erf(pre_act * (1.0 / math.sqrt(2.0))))
    activated = (pre_act * cdf).astype(BF)
    slope = cdf + pre_act * jnp.exp(-0.5 * pre_act * pre_act) * (1.0 / math.sqrt(2.0 * math.pi))
    grad_pre = (slope * grad_act).astype(BF)
    big = {}

    def beside_de(stage, events, kept):
        if stage == 0:
            held = after((cot, activated, normed_two, grad_pre), events[-1])
            big["grads"] = [tn(held[2], held[3]).astype(BF), tn(held[0], held[1]).astype(BF)]
            big["send"] = big_part(big["grads"], [], bits, 3)
            return big["send"]
        if stage == 1:
            big["got3"] = big_swaps(after(big["send"], events[-1]), 3)
            return []
        if stage == 3:
            return big["got3"]
        if stage == 4:
            big["send"] = big_part(big["grads"], [after(big["got3"], events[-1])], bits, 2)
            big["got2"] = big_swaps(big["send"], 2)
            return big["send"]
        if stage == 5:
            return big["got2"]
        return []

    def early_vectors(grad_attn_shard):
        vectors = [
            jnp.sum(grad_attn_shard.astype(F32), axis=0),
            jnp.sum(grad_norm2 * scaled2, axis=0),
            jnp.sum(grad_norm2, axis=0),
            jnp.sum(cot_shard, axis=0),
        ]
        return jnp.stack(vectors)

    (grad_norm2, mlp_total), _, _ = reduce_tp(
        [lambda v: nt(v, expand_full), lambda v: nt(v, contract_full)], [grad_pre, activated], bits, beside_de
    )

    cot_shard = shard_rows(cot, bits).astype(F32)
    grad_middle = cot_shard + norm_back(grad_norm2, gain2, scaled2, spread2)
    grad_attn_shard = grad_middle.astype(BF)
    grad_attn, _ = gather_tp(grad_attn_shard[None], bits, beside_de)
    grad_attn = grad_attn[0]

    grad_att = nn(grad_attn, o_full).astype(BF)
    got3 = big["got3"]
    got2 = big["got2"]
    send = big_part(big["grads"], [got3, got2], bits, 1)
    kept = big_part(big["grads"], [got3, got2], bits, 1, keep=True)
    got1 = big_swaps(send, 1)
    dkv = shape((length, 2 * hidden))
    grad_q, own_part, p_e1, p_f1, p_g1, p_f2, p_e3 = local_call(
        lambda *refs: attn_bwd_kernel(heads, *refs),
        "attn_bwd",
        [shape((length, hidden)), shape((length, 2 * hidden), F32)] + [dkv] * 5,
        [meta, start, queries, after(grad_att, send, kept), mixture, lse, *slots],
        in_smem=1,
        mib=16,
        scratch=[pltpu.VMEM((hidden, length), F32), pltpu.VMEM((heads, length), F32)],
        flops=2 * 10**9,
        moved=10 << 20,
        exps=3 * 10**6,
    )
    from_g1 = lax.ppermute(p_g1, XY, X_DOWN)
    from_e3 = lax.ppermute(p_e3, XY, Y_FLIP_UP)
    from_f1 = lax.ppermute(p_f1, XY, X_DOWN)

    grad_o = tn(grad_attn, after(attended, grad_q)).astype(BF)
    qo_grads = [jnp.concatenate([tn(normed, grad_q).astype(BF), grad_o], axis=1)]
    qo_plan = [(ORDER_A, 0, 0, 2 * hidden)]
    qo_send = part(qo_grads, [], bits, qo_plan, 3, 0), part(qo_grads, [], bits, qo_plan, 3, 1)
    big["early"] = early_vectors(after(grad_attn_shard, grad_q))
    from_g1 = after(from_g1, got1)
    from_e1 = lax.ppermute((p_e1.astype(F32) + from_g1.astype(F32)).astype(BF), XY, Y_FLIP)
    from_f2 = lax.ppermute((p_f2.astype(F32) + from_e3.astype(F32)).astype(BF), XY, X_DOWN2)
    biases = jnp.concatenate(
        [
            jnp.sum(after(grad_att, grad_q).astype(F32), axis=0).reshape(16, nb),
            jnp.sum(grad_pre.astype(F32), axis=0).reshape(16, ne),
            jnp.zeros((16, 128 - nb - ne), F32),
        ],
        axis=1,
    ).reshape(1, width)
    q_bias_grad = jnp.sum(grad_q.astype(F32), axis=0).reshape(16, nb)
    q_bias_grad = jnp.concatenate([q_bias_grad, jnp.zeros((16, 128 - nb), F32)], axis=1).reshape(1, width)
    from_e1 = after(from_e1, q_bias_grad, biases, big["early"])
    got0 = big_swaps([(v[1:] + g[1:].astype(F32)).astype(BF) for v, g in zip(kept, got1)], 0)
    from_f2 = after(from_f2, got0)
    grad_kv = (own_part + from_f1.astype(F32) + from_e1.astype(F32) + from_f2.astype(F32)).astype(BF)

    qkv_full = jnp.concatenate([q_full, kv_full], axis=1)
    grad_qkv = jnp.concatenate([grad_q, grad_kv], axis=1)
    tail = {}

    kv_plan = [(ORDER_A, 0, 0, hidden), (ORDER_B, 0, hidden, hidden)]

    def beside_fg(stage, events, kept):
        now = events[-1]
        if stage == 0:
            tail["q3"] = swaps(after(qo_send[0], now), qo_orders, 3)
            tail["kv"] = [tn(normed, after(grad_kv, now)).astype(BF)]
            return tail["kv"]
        if stage == 1:
            rows = halves(scaled1, bits)
            gone = events[0].astype(F32)
            vectors = [
                jnp.sum(gone * rows[0], axis=0) + jnp.sum(kept[0] * rows[1], axis=0),
                jnp.sum(gone, axis=0) + jnp.sum(kept[0], axis=0),
            ]
            tail["small"] = jnp.concatenate([jnp.stack(vectors), big["early"], biases, q_bias_grad], axis=0)
            tail["send"] = part(tail["kv"], [], bits, kv_plan, 3, small=tail["small"])
            tail["k3"] = swaps(tail["send"], kv_orders, 3)
            return tail["send"]
        if stage == 2:
            tail["q3_high"] = swaps(after(qo_send[1], tail["q3"], now), qo_orders, 3)
            return [tail["k3"], tail["q3"]]
        small = dict(small=tail["small"])
        if stage == 3:
            tail["k2"] = swaps(part(tail["kv"], [(after(tail["k3"], now), 0)], bits, kv_plan, 2, **small), kv_orders, 2)
            tail["q2"] = swaps(part(qo_grads, [(after(tail["q3_high"], now), 4)], bits, qo_plan, 2), qo_orders, 2)
            return tail["k2"]
        if stage == 4:
            gots = [(tail["k3"], 0), (after(tail["k2"], now), 0)]
            tail["k1"] = swaps(part(tail["kv"], gots, bits, kv_plan, 1, **small), kv_orders, 1)
            return [tail["k1"], tail["q2"]]
        gots = [(tail["k3"], 0), (tail["k2"], 0), (after(tail["k1"], now), 0)]
        tail["k0"] = swaps(part(tail["kv"], gots, bits, kv_plan, 0, **small), kv_orders, 0)
        gots = [(tail["q3"], 0), (after(tail["q2"], now), 0)]
        tail["q1"] = swaps(part(qo_grads, gots, bits, qo_plan, 1), qo_orders, 1)
        return [tail["k0"], tail["q1"]]

    (grad_norm1,), _, _ = reduce_tp([lambda v: nt(v, qkv_full)], [grad_qkv], bits, beside_fg)
    x_scaled, x_spread = norm_stats(x_shard)
    grad_x = grad_middle + norm_back(grad_norm1, gain1, x_scaled, x_spread)
    layer_shard = (middle + (mlp_total + con_bias)).astype(BF)
    both, _ = gather_tp(jnp.stack([grad_x.astype(BF), layer_shard]), bits, beside_fg)
    input_grad, layer_output = both[0].astype(F32), both[1]
    gots = [(tail[k], 0) for k in ("k3", "k2", "k1", "k0")]
    k_grad, v_grad, small = part(tail["kv"], gots, bits, kv_plan, -1, small=tail["small"])
    biases, q_bias_grad = small[6:7], small[7:8]
    for kind in ("C", "Z1", "Z3"):
        small = small + swap(small, kind)
    gots = [(v, 0) for v in (tail["q3"], tail["q2"], tail["q1"])]
    qo0 = swaps(part(qo_grads, gots, bits, qo_plan, 0), qo_orders, 0)
    gots = gots + [(qo0, 0)]
    qo_grad = part(qo_grads, gots, bits, qo_plan, -1)[0][0]
    expand_grad, contract_grad = [
        v[0] + g[0].astype(F32) + h[0].astype(F32) for v, g, h in zip(kept, got1, got0)
    ]

    return (
        layer_output[None],
        input_grad[None],
        small[0],
        small[1],
        qo_grad[:, :hidden],
        q_bias_grad[:, :nb],
        k_grad[0],
        v_grad[0],
        biases[:, :nb],
        qo_grad[:, hidden:].T,
        small[2],
        small[3],
        small[4],
        expand_grad,
        biases[:, nb : nb + ne],
        contract_grad.T,
        small[5],
    )


def solution(mesh):
    both = ("fsdp", "ctx")
    rows, cols, vec = P(both, "tp"), P("tp", both), P(both)
    act = P("fsdp", "ctx", None)
    return jax.shard_map(
        body,
        mesh=mesh,
        in_specs=(
            act, P("fsdp", None), vec, vec, rows, cols, rows, rows, cols, cols, vec, vec, vec,
            rows, cols, cols, vec, act,
        ),
        out_specs=(
            act, act, vec, vec, rows, cols, rows, rows, cols, cols, vec, vec, vec, rows, cols, cols, vec,
        ),
        check_vma=False,
    )
```

```python
import math

import jax
import jax.numpy as jnp
from jax import lax
from jax.experimental import pallas as pl
from jax.experimental.pallas import tpu as pltpu
from jax.sharding import PartitionSpec as P

HEAD_DIM = 128
BF = jnp.bfloat16
F32 = jnp.float32
XY = ("fsdp", "ctx")
NEG = -1e30
SCALE = 1.0 / math.sqrt(HEAD_DIM)


def lin(x, y):
    return (y // 2) * 8 + x * 2 + y % 2


def pairs_xy(move):
    out = []
    for x in range(4):
        for y in range(4):
            to = move(x, y)
            if to is not None:
                out.append((lin(x, y), lin(*to)))
    return out


PERM = {
    "X1": pairs_xy(lambda x, y: (x ^ 1, y)),
    "X3": pairs_xy(lambda x, y: (x ^ 3, y)),
    "Y1": pairs_xy(lambda x, y: (x, y ^ 1)),
    "Y3": pairs_xy(lambda x, y: (x, y ^ 3)),
    "C": [(t, t ^ 1) for t in range(8)],
    "Z1": [(t, t ^ 2) for t in range(8)],
    "Z3": [(t, t ^ 6) for t in range(8)],
}
VEC = {"X1": (1, 0), "X3": (3, 0), "Y1": (0, 1), "Y3": (0, 3)}
ORDER_A = ("X1", "Y1", "X3", "Y3")
ORDER_B = ("Y1", "X3", "Y3", "X1")
ORDER_C = ("X3", "Y3", "X1", "Y1")
ORDER_D = ("Y3", "X1", "Y1", "X3")
ORDER_E = ("X1", "X3", "Y1", "Y3")
ORDER_F = ("X3", "X1", "Y3", "Y1")
ORDER_P = ("X3", "X1", "Y3", "Y1")
ORDER_Q = ("X3", "X1", "Y1", "Y3")
ORDER_R = ("Y3", "Y1", "X3", "X1")
ORDER_S = ("Y3", "Y1", "X1", "X3")


def swap(value, kind):
    return lax.ppermute(value, XY if kind in VEC else "tp", PERM[kind])


def offsets(order):
    out = []
    for p in range(16):
        x = y = 0
        for k, kind in enumerate(order):
            if (p >> k) & 1:
                x ^= VEC[kind][0]
                y ^= VEC[kind][1]
        out.append(lin(x, y))
    return out


def own_bits():
    c = lax.axis_index("ctx")
    t = lax.axis_index("tp")
    z1, z0, k = t // 4, (t // 2) % 2, t % 2
    me = (lax.axis_index("fsdp") * 8 + c).astype(jnp.int32)
    return {"Z1": z0 ^ z1, "Z3": z1, "C": k, "me": me[None]}


def pick(bit, if_zero, if_one):
    return jnp.where(bit == 0, if_zero, if_one)


def merge(bit, own, got):
    return jnp.concatenate([pick(bit, own, got), pick(bit, got, own)], axis=0)


VMEM = pl.BlockSpec(memory_space=pltpu.VMEM)
SMEM = pl.BlockSpec(memory_space=pltpu.SMEM)


def local_call(kernel, name, out_shape, args, in_smem=0, mib=20, scratch=(), flops=0, moved=0, exps=0):
    return pl.pallas_call(
        kernel,
        out_shape=out_shape,
        in_specs=[SMEM] * in_smem + [VMEM] * (len(args) - in_smem),
        out_specs=jax.tree.map(lambda _: VMEM, out_shape),
        scratch_shapes=list(scratch),
        compiler_params=pltpu.CompilerParams(vmem_limit_bytes=mib << 20),
        cost_estimate=pl.CostEstimate(flops=flops, bytes_accessed=moved, transcendentals=exps),
        name=name,
    )(*args)


def fetch_call(kernel, name, out_shape, args, scratch=(), moved=0):
    args = [pltpu.with_memory_space_constraint(v, pltpu.HBM) for v in args]

    def whole(v):
        return pl.BlockSpec(v.shape, lambda i: (0,) * len(v.shape))

    return pl.pallas_call(
        kernel,
        grid=(1,),
        out_shape=out_shape,
        in_specs=[whole(v) for v in args],
        out_specs=jax.tree.map(whole, out_shape),
        scratch_shapes=list(scratch),
        compiler_params=pltpu.CompilerParams(vmem_limit_bytes=12 << 20),
        cost_estimate=pl.CostEstimate(flops=0, bytes_accessed=moved, transcendentals=0),
        name=name,
    )(*args)


def shape(dims, dtype=BF):
    return jax.ShapeDtypeStruct(dims, dtype)


def after(value, *events):
    return lax.optimization_barrier((value, events))[0]


def pack_kernel(key_ref, value_ref, query_ref, output_ref, *refs):
    vectors, outs, rows_ref = refs[:9], refs[9:13], refs[13]
    rows_ref[...] = jnp.zeros(rows_ref.shape, F32)
    for i, v in enumerate(vectors):
        rows_ref[i : i + 1, : v.shape[1]] = v[...]
    rows, width = key_ref.shape
    outs[0][:rows] = key_ref[...].astype(BF)
    outs[0][rows:, :128] = rows_ref[...].astype(BF)
    outs[0][rows:, 128:] = jnp.zeros((16, width - 128), BF)
    outs[1][...] = value_ref[...].astype(BF)
    outs[2][...] = query_ref[...].astype(BF)
    outs[3][...] = output_ref[...].T.astype(BF)


def pack_ffn_kernel(expand_ref, contract_ref, *outs):
    half = expand_ref.shape[1] // 2
    for i in range(2):
        outs[i][...] = expand_ref[:, i * half : (i + 1) * half].astype(BF)
        outs[2 + i][...] = contract_ref[i * half : (i + 1) * half].T.astype(BF)


def join_kernel(count, *refs):
    for own, got, out in zip(refs[:count], refs[count : 2 * count], refs[2 * count :]):
        n = own.shape[0]
        out[:n] = own[...]
        out[n:] = got[...]


def join(owns, gots):
    shapes = [shape((2 * v.shape[0],) + v.shape[1:]) for v in owns]
    size = sum(v.size for v in owns)
    count = len(owns)
    return local_call(lambda *r: join_kernel(count, *r), "join", shapes, [*owns, *gots], mib=4, moved=8 * size)


def swaps(bufs, orders, k):
    return [swap(b, o[k]) for b, o in zip(bufs, orders)]


def place_kernel(rows, plan, count, small, me_ref, *refs):
    owns, gots, outs = refs[:count], refs[count : 2 * count], refs[2 * count :]
    me = me_ref[0]
    if small:
        vec_ref, query_ref, expand_ref = outs[-3:]
        query_ref[...] = jnp.zeros(query_ref.shape, F32)
        expand_ref[...] = jnp.zeros(expand_ref.shape, F32)
    for s, (order, target, column) in enumerate(plan):
        width = owns[s].shape[2]
        away = offsets(order)
        for p in range(16):
            src = owns[s] if p < 8 else gots[s]
            block = me ^ away[p]
            row = pl.multiple_of(block * rows, rows)
            outs[target][pl.ds(row, rows), column : column + width] = src[p % 8, :rows]
            if small and s == 0:
                more = src[p % 8, rows:, :128].astype(F32)
                vec_ref[:, pl.ds(pl.multiple_of(block * 128, 128), 128)] = more[:8]
                cols = pl.ds(pl.multiple_of((block // 8) * 128, 128), 128)
                query_ref[:, cols] = query_ref[:, cols] + pltpu.roll(more[:8], (block % 8) * 16, 1)[6:7]
                cols = pl.ds(pl.multiple_of((block // 2) * 128, 128), 128)
                expand_ref[:, cols] = expand_ref[:, cols] + pltpu.roll(more[8:], (block % 2) * 64, 1)[0:1]


def place(owns, gots, bits, rows, plan, widths, small=()):
    shapes = [shape((16 * rows, w)) for w in widths]
    if small:
        shapes += [shape((8, 2048), F32)] + [shape((1, w), F32) for w in small]
    count = len(owns)
    return local_call(
        lambda *r: place_kernel(rows, plan, count, bool(small), *r),
        "place",
        shapes,
        [bits["me"], *owns, *gots],
        in_smem=1,
        mib=6,
        moved=64 * rows * sum(widths),
    )


def part(grads, gots, bits, plan, step, half=None, small=None):
    rows = grads[0].shape[0] // 16
    low, count = (1 << step, 1 << step) if step >= 0 else (0, 1)
    if half is not None:
        count //= 2
        low += half * count
    n, ng = len(plan), len(grads)
    extra = 16 if small is not None and step >= 0 else 0
    shapes = [shape((count, rows + (extra if s == 0 else 0), p[3]), BF if step >= 0 else F32) for s, p in enumerate(plan)]
    if small is not None and step < 0:
        shapes.append(shape((8, 128), F32))

    def kernel(me_ref, *refs):
        me = me_ref[0]
        first = ng + n * len(gots)
        outs = refs[first + (small is not None) :]
        for s, (order, source, column, width) in enumerate(plan):
            away = offsets(order)
            for q in range(count):
                p = low + q
                row = pl.multiple_of((me ^ away[p]) * rows, rows)
                piece = refs[source][pl.ds(row, rows), column : column + width]
                if gots:
                    piece = piece.astype(F32)
                    for j, (_, base) in enumerate(gots):
                        piece = piece + refs[ng + n * j + s][p - base, :rows].astype(F32)
                outs[s][q, :rows] = piece.astype(outs[s].dtype)
                if small is not None and s == 0:
                    lane = pl.multiple_of((me ^ away[p]) * 128, 128)
                    vectors = jnp.concatenate([refs[first][:, pl.ds(lane, 128)], jnp.zeros((8, 128), F32)], axis=0)
                    for j, (_, base) in enumerate(gots):
                        vectors = vectors + refs[ng + n * j][p - base, rows:, :128].astype(F32)
                    if step >= 0:
                        outs[0][q, rows:, :128] = vectors.astype(BF)
                        outs[0][q, rows:, 128:] = jnp.zeros((16, width - 128), BF)
                    else:
                        outs[-1][...] = vectors[:8]

    args = [bits["me"], *grads, *[g for got, _ in gots for g in got]] + ([small] if small is not None else [])
    moved = 2 * count * rows * sum(p[3] for p in plan) * (2 + len(gots))
    return local_call(kernel, "part", shapes, args, in_smem=1, mib=6, moved=moved)


BIG = ((ORDER_P, ORDER_Q), (ORDER_R, ORDER_S))


def big_part(grads, gots, bits, step):
    rows, width = grads[0].shape[0] // 16, grads[0].shape[1]
    half = width // 2
    count = 1 << step
    in_specs, args, spans, outs = [], [], [], []
    per = 1 + len(gots)
    for low in (count, 0) if step == 1 else (count,):
        for m, pair in enumerate(BIG):
            for s, order in enumerate(pair):
                near = [offsets(order)[1 << k] for k in range(4)]

                def block_at(q, me, near=near, low=low, s=s):
                    p = low + q
                    where = me[0]
                    for k, away in enumerate(near):
                        where = where ^ (((p >> k) & 1) * away)
                    return (where, s)

                in_specs.append(pl.BlockSpec((rows, half), block_at))
                args.append(grads[m])
                for got in gots:
                    in_specs.append(pl.BlockSpec((1, rows, half), lambda q, me, low=low: (low + q, 0, 0)))
                    args.append(got[2 * m + s])
                if step > 1:
                    outs.append(shape((count, rows, half)))
                    spans.append((len(outs) - 1, 0))
                elif s == 0:
                    outs.append(shape((count, rows, width), BF if low else F32))
                    spans.append((len(outs) - 1, 0))
                else:
                    spans.append((len(outs) - 1, half))

    def kernel(me_ref, *refs):
        out_refs = refs[len(args) :]
        for i, (at, column) in enumerate(spans):
            piece = refs[per * i][...]
            if gots:
                piece = piece.astype(F32)
                for j in range(1, per):
                    piece = piece + refs[per * i + j][0].astype(F32)
            out_refs[at][0, :, column : column + half] = piece.astype(outs[at].dtype)

    return pl.pallas_call(
        kernel,
        grid_spec=pltpu.PrefetchScalarGridSpec(
            num_scalar_prefetch=1,
            grid=(count,),
            in_specs=in_specs,
            out_specs=[pl.BlockSpec((1,) + o.shape[1:], lambda q, me: (q, 0, 0)) for o in outs],
        ),
        out_shape=outs,
        compiler_params=pltpu.CompilerParams(vmem_limit_bytes=12 << 20),
        cost_estimate=pl.CostEstimate(flops=0, bytes_accessed=4 * count * rows * width * (1 + per), transcendentals=0),
        name="big_part",
    )(bits["me"], *args)


def big_swaps(values, step):
    if step >= 2:
        return [swap(v, o[step]) for v, o in zip(values, BIG[0] + BIG[1])]
    return [swap(v, pair[0][step]) for v, pair in zip(values, BIG)]


def shard_rows(value, bits):
    base = bits["C"] * 256
    one = base + bits["Z1"] * 64 + bits["Z3"] * 32
    two = base + 128 + bits["Z3"] * 64 + bits["Z1"] * 32
    return jnp.concatenate(
        [lax.dynamic_slice_in_dim(value, one, 32, 0), lax.dynamic_slice_in_dim(value, two, 32, 0)], axis=0
    )


def halves(value, bits):
    send = lax.dynamic_slice_in_dim(value, (1 - bits["C"]) * 256, 256, 0)
    keep = lax.dynamic_slice_in_dim(value, bits["C"] * 256, 256, 0)
    return send, keep


def reduce_tp(products, operands, bits, beside=None):
    count = len(products)
    pairs = [halves(v, bits) for v in operands]
    send = jnp.concatenate([p(v[0]).astype(BF) for p, v in zip(products, pairs)], axis=0)
    first = swap(send, "C")
    kept = [p(v[1]) for p, v in zip(products, pairs)]
    events = [send]
    if beside:
        first = after(first, beside(0, events, kept))
    totals = [v + first[i * 256 : (i + 1) * 256].astype(F32) for i, v in enumerate(kept)]
    events.append(first)
    streams = [[v[:128] for v in totals], [v[128:] for v in totals]]
    for stage, kinds in enumerate((("Z1", "Z3"), ("Z3", "Z1"))):
        n = streams[0][0].shape[0] // 2
        give = [
            jnp.concatenate([pick(bits[t], v[n:], v[:n]).astype(BF) for v in parts], axis=0)
            for t, parts in zip(kinds, streams)
        ]
        got = [swap(v, t) for v, t in zip(give, kinds)]
        if beside:
            got = after(got, beside(1 + stage, events, kept))
        events.append(got)
        streams = [
            [pick(bits[t], v[:n], v[n:]) + g[i * n : (i + 1) * n].astype(F32) for i, v in enumerate(parts)]
            for t, parts, g in zip(kinds, streams, got)
        ]
    out = [jnp.concatenate([streams[0][i], streams[1][i]], axis=0) for i in range(count)]
    return out, events, kept


def merge_rows(bit, own, got):
    return jnp.concatenate([pick(bit, own, got), pick(bit, got, own)], axis=1)


def gather_tp(shards, bits, beside=None):
    parts = [shards[:, :32], shards[:, 32:]]
    events = [shards]
    for stage, kinds in enumerate((("Z3", "Z1"), ("Z1", "Z3"))):
        got = [swap(v, t) for v, t in zip(parts, kinds)]
        if beside:
            got = after(got, beside(3 + stage, events, None))
        events.append(got)
        parts = [merge_rows(bits[t], v, g) for t, v, g in zip(kinds, parts, got)]
    own = jnp.concatenate(parts, axis=1)
    last = swap(own, "C")
    if beside:
        last = after(last, beside(5, events, None))
    events.append(last)
    return merge_rows(bits["C"], own, last), events


Y_FLIP = PERM["Y1"]
Y_FLIP_DOWN = pairs_xy(lambda x, y: (x, y ^ 1) if y % 2 == 1 else None)
Y_FLIP_UP = pairs_xy(lambda x, y: (x, y ^ 1) if y % 2 == 0 else None)
X_UP = pairs_xy(lambda x, y: (x + 1, y) if x < 3 else None)
X_UP2 = pairs_xy(lambda x, y: (x + 2, y) if x < 2 else None)
X_DOWN = pairs_xy(lambda x, y: (x - 1, y) if x > 0 else None)
X_DOWN2 = pairs_xy(lambda x, y: (x - 2, y) if x > 1 else None)
SLOTS = 6


def slot_block(slot, c):
    back = slot // 2 * 2
    return c - back if slot % 2 == 0 else (c ^ 1) - back


def slot_needed(slot, c, length, first_ref):
    block = slot_block(slot, c)
    return (block >= 0) & (block < c) & (block * length + length - 1 >= first_ref[0])


def nt(a, b):
    return lax.dot_general(a, b, (((1,), (1,)), ((), ())), preferred_element_type=F32)


def tn(a, b):
    return lax.dot_general(a, b, (((0,), (0,)), ((), ())), preferred_element_type=F32)


def nn(a, b):
    return jnp.dot(a, b, preferred_element_type=F32)


def visible(slot, block, length, start_ref, c):
    keys = lax.broadcasted_iota(jnp.int32, (length, length), 0) + block * length
    mask = keys >= start_ref[...]
    if slot == 0:
        mask = mask & (keys <= lax.broadcasted_iota(jnp.int32, (length, length), 1) + c * length)
    return mask


def attn_fwd_kernel(heads, me_ref, first_ref, start_ref, q_ref, *refs):
    kv = refs[:SLOTS]
    att_ref, mix_ref, lse_ref, m_ref, l_ref = refs[SLOTS:]
    length = q_ref.shape[0]
    hidden = heads * HEAD_DIM
    c = me_ref[0] % 8
    for slot in range(SLOTS):
        block = slot_block(slot, c)

        def run(slot=slot, block=block):
            mask = visible(slot, block, length, start_ref, c)
            for h in range(heads):
                cols = slice(h * HEAD_DIM, (h + 1) * HEAD_DIM)
                key = kv[slot][:, cols]
                val = kv[slot][:, hidden + h * HEAD_DIM : hidden + (h + 1) * HEAD_DIM]
                s = jnp.where(mask, nt(key, q_ref[:, cols]) * SCALE, NEG)
                top = jnp.max(s, axis=0, keepdims=True)
                if slot == 0:
                    p = jnp.exp(s - top)
                    m_ref[h : h + 1] = top
                    l_ref[h : h + 1] = jnp.sum(p, axis=0, keepdims=True)
                    mix_ref[cols] = tn(val, p.astype(BF))
                else:
                    old = m_ref[h : h + 1]
                    new = jnp.maximum(old, top)
                    p = jnp.exp(s - new)
                    shrink = jnp.exp(old - new)
                    m_ref[h : h + 1] = new
                    l_ref[h : h + 1] = l_ref[h : h + 1] * shrink + jnp.sum(p, axis=0, keepdims=True)
                    mix_ref[cols] = mix_ref[cols] * shrink + tn(val, p.astype(BF))

        if slot == 0:
            run()
        else:
            pl.when(slot_needed(slot, c, length, first_ref))(run)
    for h in range(heads):
        cols = slice(h * HEAD_DIM, (h + 1) * HEAD_DIM)
        out = mix_ref[cols] / l_ref[h : h + 1]
        mix_ref[cols] = out
        att_ref[:, cols] = out.T.astype(BF)
        lse_ref[h : h + 1] = m_ref[h : h + 1] + jnp.log(l_ref[h : h + 1])


def attn_bwd_kernel(heads, me_ref, first_ref, start_ref, q_ref, do_ref, mix_ref, lse_ref, *refs):
    kv = refs[:SLOTS]
    dq_ref, dkv = refs[SLOTS], refs[SLOTS + 1 : 2 * SLOTS + 1]
    dqt_ref, delta_ref = refs[2 * SLOTS + 1 :]
    length = q_ref.shape[0]
    hidden = heads * HEAD_DIM
    c = me_ref[0] % 8
    for h in range(heads):
        cols = slice(h * HEAD_DIM, (h + 1) * HEAD_DIM)
        dot_t = do_ref[:, cols].astype(F32).T
        delta_ref[h : h + 1] = jnp.sum(dot_t * mix_ref[cols], axis=0, keepdims=True)
    for slot in range(SLOTS):
        block = slot_block(slot, c)

        def run(slot=slot, block=block):
            mask = visible(slot, block, length, start_ref, c)
            for h in range(heads):
                cols = slice(h * HEAD_DIM, (h + 1) * HEAD_DIM)
                vcols = slice(hidden + h * HEAD_DIM, hidden + (h + 1) * HEAD_DIM)
                key, val = kv[slot][:, cols], kv[slot][:, vcols]
                q, do = q_ref[:, cols], do_ref[:, cols]
                s = jnp.where(mask, nt(key, q) * SCALE, NEG)
                p = jnp.exp(s - lse_ref[h : h + 1])
                ds = (p * (nt(val, do) - delta_ref[h : h + 1])).astype(BF)
                dkv[slot][:, cols] = (nn(ds, q) * SCALE).astype(dkv[slot].dtype)
                dkv[slot][:, vcols] = nn(p.astype(BF), do).astype(dkv[slot].dtype)
                part = tn(key, ds)
                if slot == 0:
                    dqt_ref[cols] = part
                else:
                    dqt_ref[cols] = dqt_ref[cols] + part

        if slot == 0:
            run()
        else:
            pl.when(slot_needed(slot, c, length, first_ref))(run)

            @pl.when(jnp.logical_not(slot_needed(slot, c, length, first_ref)))
            def _(slot=slot):
                dkv[slot][...] = jnp.zeros(dkv[slot].shape, dkv[slot].dtype)

    for h in range(heads):
        cols = slice(h * HEAD_DIM, (h + 1) * HEAD_DIM)
        dq_ref[:, cols] = (dqt_ref[cols] * SCALE).T.astype(BF)


def stats_kernel(x_ref, mean_ref, spread_ref):
    for r in range(0, x_ref.shape[0], 64):
        v = x_ref[r : r + 64].astype(F32)
        mean = jnp.mean(v, axis=-1, keepdims=True)
        centre = v - mean
        spread = lax.rsqrt(jnp.mean(centre * centre, axis=-1, keepdims=True) + 1e-05)
        mean_ref[r : r + 64] = jnp.broadcast_to(mean, (64, 128))
        spread_ref[r : r + 64] = jnp.broadcast_to(spread, (64, 128))


def norm_kv_kernel(me_ref, x_ref, mean_ref, spread_ref, k_own, v_own, k_got, v_got, normed_ref, kv_ref, acc_ref):
    me = me_ref[0]
    hidden = k_own.shape[2]
    zero = jnp.zeros((1, 128), F32)
    bias = [zero, zero]
    away_k, away_v = offsets(ORDER_A), offsets(ORDER_B)
    for q in range(8):
        parts = []
        for src, p in ((k_own, q), (k_got, q + 8)):
            block = me ^ away_k[p]
            cols = pl.ds(pl.multiple_of(block * 128, 128), 128)
            small = src[q, 128:144, :128].astype(F32)
            scaled = (x_ref[:, cols].astype(F32) - mean_ref[...]) * spread_ref[...]
            part = (scaled * small[0:1] + small[1:2]).astype(BF)
            normed_ref[:, cols] = part
            parts.append(part)
            turned = pltpu.roll(small[:8], (block % 8) * 16, 1)[7:8]
            bias = [bias[0] + jnp.where(block < 8, turned, zero), bias[1] + jnp.where(block < 8, zero, turned)]
        weights = jnp.concatenate([k_own[q, :128], k_got[q, :128]], axis=0)
        term = jnp.dot(jnp.concatenate(parts, axis=1), weights, preferred_element_type=F32)
        acc_ref[...] = term if q == 0 else acc_ref[...] + term
    kv_ref[:, :hidden] = acc_ref[...].astype(BF)
    for q in range(8):
        parts = []
        for p in (q, q + 8):
            parts.append(normed_ref[:, pl.ds(pl.multiple_of((me ^ away_v[p]) * 128, 128), 128)])
        weights = jnp.concatenate([v_own[q], v_got[q]], axis=0)
        term = jnp.dot(jnp.concatenate(parts, axis=1), weights, preferred_element_type=F32)
        acc_ref[...] = term if q == 0 else acc_ref[...] + term
    kv_ref[:, hidden:] = (acc_ref[...] + jnp.concatenate(bias, axis=1)).astype(BF)


def early_kernel(att_ref, query_ref, pre_ref, attn_ref, norm_ref, scaled_ref, cot_ref, out_ref):
    def total(v):
        return jnp.sum(v.astype(F32), axis=0, keepdims=True)

    out_ref[0:2] = jnp.zeros((2, out_ref.shape[1]), F32)
    out_ref[2:3] = total(attn_ref[...])
    out_ref[3:4] = total(norm_ref[...] * scaled_ref[...])
    out_ref[4:5] = total(norm_ref[...])
    out_ref[5:6] = total(cot_ref[...])
    value, query, expand = total(att_ref[...]), total(query_ref[...]), total(pre_ref[...])
    lane = lax.broadcasted_iota(jnp.int32, (8, 128), 1)

    def taken(row, size, block, to):
        at = block * size
        wide = jnp.broadcast_to(row[:, at // 128 * 128 : at // 128 * 128 + 128], (8, 128))
        wide = pltpu.roll(wide, (128 - at % 128 + to) % 128, 1)
        return jnp.where((lane >= to) & (lane < to + size), wide, 0.0)[0:1]

    nb, ne = value.shape[1] // 16, expand.shape[1] // 16
    for block in range(16):
        cols = slice(block * 128, block * 128 + 128)
        out_ref[6:7, cols] = taken(value, nb, block, 0) + taken(expand, ne, block, nb)
        out_ref[7:8, cols] = taken(query, nb, block, 0)


def late_kernel(core_ref, x_ref, mean_ref, spread_ref, gone_ref, kept_ref, early_ref, out_ref):
    core = core_ref[0]
    size = gone_ref.shape[0]
    out_ref[...] = early_ref[...]
    first = jnp.zeros((1, x_ref.shape[1]), F32)
    second = first
    for src, base in ((gone_ref, (1 - core) * size), (kept_ref, core * size)):
        for r in range(0, size, 32):
            rows = pl.ds(pl.multiple_of(base + r, 32), 32)
            scaled = (x_ref[rows].astype(F32) - mean_ref[rows][:, :1]) * spread_ref[rows][:, :1]
            grad = src[r : r + 32].astype(F32)
            first = first + jnp.sum(grad * scaled, axis=0, keepdims=True)
            second = second + jnp.sum(grad, axis=0, keepdims=True)
    out_ref[0:1] = first
    out_ref[1:2] = second


def final_ffn_kernel(*refs):
    kept, one, zero, outs = refs[:2], refs[2:4], refs[4:6], refs[6:]
    total = [k[0] + a[0].astype(F32) + b[0].astype(F32) for k, a, b in zip(kept, one, zero)]
    outs[0][...] = total[0]
    for j in range(0, total[1].shape[1], 128):
        outs[1][j : j + 128] = total[1][:, j : j + 128].T


def final_qo_kernel(me_ref, grad_ref, *refs):
    gots, outs = refs[:-2], refs[-2:]
    piece = grad_ref[pl.ds(pl.multiple_of(me_ref[0] * 128, 128), 128)].astype(F32)
    for got in gots:
        piece = piece + got[0].astype(F32)
    half = piece.shape[1] // 2
    outs[0][...] = piece[:, :half]
    outs[1][...] = piece[:, half:].T


def norm_stats(v):
    mean = jnp.mean(v, axis=-1, keepdims=True)
    centre = v - mean
    spread = lax.rsqrt(jnp.mean(centre * centre, axis=-1, keepdims=True) + 1e-05)
    return centre * spread, spread


def norm_back(grad, gain, scaled, spread):
    weighted = grad * gain
    inner = jnp.mean(weighted, axis=-1, keepdims=True)
    cross = jnp.mean(weighted * scaled, axis=-1, keepdims=True)
    return spread * (weighted - inner - scaled * cross)


def cols_of(w, n=4):
    k = w.shape[1] // n
    return [w[:, i * k : (i + 1) * k] for i in range(n)]


def body(
    layer_input,
    doc_ids,
    pre_gain,
    pre_shift,
    query_weight,
    query_bias,
    key_weight,
    value_weight,
    value_bias,
    output_weight,
    output_bias,
    mid_gain,
    mid_shift,
    expand_weight,
    expand_bias,
    contract_weight,
    contract_bias,
    cotangent,
):
    bits = own_bits()
    x = layer_input[0]
    cot = cotangent[0]
    length, width = x.shape
    hidden = query_weight.shape[1]
    heads = hidden // HEAD_DIM
    inner = expand_weight.shape[1]
    c = lax.axis_index("ctx")

    nb, ne = query_bias.shape[1], expand_bias.shape[1]
    vectors = [pre_gain, pre_shift, output_bias, mid_gain, mid_shift, contract_bias]
    weights = [key_weight, value_weight, query_weight, output_weight]
    packed = shape((128, hidden))
    bufs = fetch_call(
        pack_kernel,
        "pack",
        [shape((144, hidden)), packed, packed, packed],
        [*weights, *[v[None] for v in vectors], query_bias, value_bias, expand_bias],
        scratch=[pltpu.VMEM((16, 128), F32)],
        moved=800 << 10,
    )
    bufs = [v[None] for v in bufs]
    first_orders, big_orders = (ORDER_A, ORDER_B, ORDER_C, ORDER_D), (ORDER_E, ORDER_F)
    kv_orders, qo_orders = (ORDER_A, ORDER_B), (ORDER_D,)
    half_shape = shape((128, inner // 2))
    ffn = fetch_call(
        pack_ffn_kernel, "pack_ffn", [half_shape] * 4, [expand_weight, contract_weight], moved=1536 << 10
    )
    con = [v[None] for v in ffn[2:]]
    bufs = join(bufs, swaps(bufs, first_orders, 0))
    got = swaps(bufs, first_orders, 1)
    stats = [shape((length, 128), F32)] * 2
    mean1, spread1 = local_call(stats_kernel, "stats", stats, [after(x, bufs)], mib=8, moved=3 << 20)
    one = swaps(con[:1], big_orders[:1], 0)
    bufs = join(bufs, after(got, one, mean1))
    got = swaps(bufs, first_orders, 2)
    two = swaps(con[1:], big_orders[1:], 0)
    bufs = join(bufs, after(got, two))
    con = join(con, one + two)
    got = swaps(bufs, first_orders, 3)
    got_con = swaps(after(con, got), big_orders, 1)
    exp_orders = (ORDER_A, ORDER_B)
    exp = [v[None] for v in ffn[:2]]
    got_exp = swaps(after(exp, got), exp_orders, 0)

    docs = doc_ids[0]
    own_docs = lax.dynamic_slice_in_dim(docs, c * length, length, 0)
    start = jnp.sum((docs[:, None] < own_docs[None, :]).astype(jnp.int32), axis=0)
    first_key = start[:1]
    start = start[None]

    normed, kv_own = local_call(
        norm_kv_kernel,
        "norm_kv",
        [shape((length, width)), shape((length, 2 * hidden))],
        [bits["me"], x, mean1, spread1, bufs[0], bufs[1], got[0], got[1]],
        in_smem=1,
        mib=10,
        scratch=[pltpu.VMEM((length, hidden), F32)],
        flops=2 * length * width * 2 * hidden,
        moved=6 << 20,
    )
    kv_own = after(kv_own, got_con, got_exp)
    kv_e1 = lax.ppermute(kv_own, XY, Y_FLIP)
    kv_f1 = lax.ppermute(kv_own, XY, X_UP)
    kv_f2 = lax.ppermute(kv_own, XY, X_UP2)
    con = join(con, got_con)
    exp = join(exp, got_exp)
    got_con = swaps(con, big_orders, 2)
    kv_e1 = after(kv_e1, exp, con, kv_f1)
    plan = [(ORDER_A, 0, 0), (ORDER_B, 0, hidden), (ORDER_C, 1, 0), (ORDER_D, 2, 0)]
    kv_full, q_full, o_full, vec, q_bias, e_bias = place(
        after(bufs, kv_e1), got, bits, 128, plan, [2 * hidden, hidden, hidden], [hidden, inner]
    )
    gain1, out_bias, gain2, shift2, con_bias = [vec[i : i + 1] for i in (0, 2, 3, 4, 5)]
    kv_g1 = lax.ppermute(after(kv_e1, kv_f2), XY, X_UP)
    kv_e3 = lax.ppermute(kv_f2, XY, Y_FLIP_DOWN)
    queries = (nn(normed, q_full) + q_bias).astype(BF)
    con = join(con, after(got_con, kv_e1))
    got_con = swaps(con, big_orders, 3)

    slots = [kv_own, kv_e1, kv_f1, kv_g1, kv_f2, kv_e3]
    attended, mixture, lse = local_call(
        lambda *refs: attn_fwd_kernel(heads, *refs),
        "attn_fwd",
        [shape((length, hidden)), shape((hidden, length), F32), shape((heads, length), F32)],
        [bits["me"], first_key, start, after(queries, con), *slots],
        in_smem=2,
        mib=12,
        scratch=[pltpu.VMEM((heads, length), F32), pltpu.VMEM((heads, length), F32)],
        flops=10**9,
        moved=6 << 20,
        exps=3 * 10**6,
    )

    feed = {}

    def beside_a(stage, events, kept):
        now = events[-1]
        if stage == 0:
            plan = [(ORDER_E, 0, 0), (ORDER_F, 0, inner // 2)]
            feed["contract"] = place(con, got_con, bits, 128, plan, [inner])[0]
            feed["got"] = swaps(after(exp, now), exp_orders, 1)
            return [feed["contract"], feed["got"]]
        if stage == 1:
            feed["exp"] = join(exp, after(feed["got"], now))
            feed["got"] = swaps(feed["exp"], exp_orders, 2)
        if stage == 2:
            return feed["got"]
        if stage == 3:
            feed["exp"] = join(feed["exp"], after(feed["got"], now))
            feed["got"] = swaps(feed["exp"], exp_orders, 3)
        return []

    (attn_total,), _, _ = reduce_tp([lambda v: nt(v, o_full)], [attended], bits, beside_a)
    contract_full = feed["contract"]
    x_shard = shard_rows(x, bits).astype(F32)
    middle = x_shard + (attn_total + out_bias)
    scaled2, spread2 = norm_stats(middle)
    normed_two, _ = gather_tp((scaled2 * gain2 + shift2).astype(BF)[None], bits, beside_a)
    normed_two = normed_two[0]

    plan = [(ORDER_A, 0, 0), (ORDER_B, 0, inner // 2)]
    expand_full = place(feed["exp"], feed["got"], bits, 128, plan, [inner])[0]
    grad_act = nn(cot, contract_full)
    pre_act = nn(normed_two, expand_full) + e_bias
    cdf = 0.5 * (1.0 + lax.erf(pre_act * (1.0 / math.sqrt(2.0))))
    activated = (pre_act * cdf).astype(BF)
    slope = cdf + pre_act * jnp.exp(-0.5 * pre_act * pre_act) * (1.0 / math.sqrt(2.0 * math.pi))
    grad_pre = (slope * grad_act).astype(BF)
    big = {}

    def beside_de(stage, events, kept):
        if stage == 0:
            held = after((cot, activated, normed_two, grad_pre), events[-1])
            big["grads"] = [tn(held[2], held[3]).astype(BF), tn(held[0], held[1]).astype(BF)]
            big["send"] = big_part(big["grads"], [], bits, 3)
            return big["send"]
        if stage == 1:
            big["got3"] = big_swaps(after(big["send"], events[-1]), 3)
            return []
        if stage == 4:
            return big["got3"]
        if stage < 5:
            return []
        big["send"] = big_part(big["grads"], [after(big["got3"], events[-1])], bits, 2)
        big["got2"] = big_swaps(big["send"], 2)
        return big["send"]

    (grad_norm2,), _, _ = reduce_tp([lambda v: nt(v, expand_full)], [grad_pre], bits, beside_de)

    cot_shard = shard_rows(cot, bits).astype(F32)
    grad_middle = cot_shard + norm_back(grad_norm2, gain2, scaled2, spread2)
    grad_attn_shard = grad_middle.astype(BF)
    grad_attn, _ = gather_tp(grad_attn_shard[None], bits, beside_de)
    grad_attn = grad_attn[0]

    grad_att = nn(grad_attn, o_full).astype(BF)
    dkv = shape((length, 2 * hidden))
    grad_q, own_part, p_e1, p_f1, p_g1, p_f2, p_e3 = local_call(
        lambda *refs: attn_bwd_kernel(heads, *refs),
        "attn_bwd",
        [shape((length, hidden)), shape((length, 2 * hidden), F32)] + [dkv] * 5,
        [bits["me"], first_key, start, queries, after(grad_att, big["send"]), mixture, lse, *slots],
        in_smem=2,
        mib=16,
        scratch=[pltpu.VMEM((hidden, length), F32), pltpu.VMEM((heads, length), F32)],
        flops=2 * 10**9,
        moved=10 << 20,
        exps=3 * 10**6,
    )
    got2 = after(big["got2"], grad_q)
    both = big_part(big["grads"], [big["got3"], got2], bits, 1)
    rest = both[2:]
    from_g1 = lax.ppermute(after(p_g1, got2), XY, X_DOWN)
    from_e3 = lax.ppermute(after(p_e3, got2), XY, Y_FLIP_UP)
    got1 = big_swaps(both[:2], 1)
    mlp_send, mlp_keep = halves(activated, bits)
    mlp_got = swap(after(nt(mlp_send, contract_full).astype(BF), got2), "C")

    grad_o = tn(grad_attn, after(attended, grad_q)).astype(BF)
    qo_grads = [jnp.concatenate([tn(normed, grad_q).astype(BF), grad_o], axis=1)]
    qo_plan = [(ORDER_D, 0, 0, 2 * hidden)]
    qo_send = part(qo_grads, [], bits, qo_plan, 3, 0), part(qo_grads, [], bits, qo_plan, 3, 1)
    from_g1 = after(from_g1, got1, qo_send)
    from_f1 = lax.ppermute(after(p_f1, from_g1), XY, X_DOWN)
    total = nt(mlp_keep, contract_full) + after(mlp_got, from_g1).astype(F32)
    one, two = total[:128], total[128:]
    two = [jnp.concatenate([two[i : i + 32], two[i + 64 : i + 96]], axis=0) for i in (0, 32)]
    give = [pick(bits["Z1"], one[64:], one[:64]), pick(bits["Z1"], two[1], two[0])]
    mlp_got = swap(jnp.concatenate(give, axis=0).astype(BF), "Z1")
    one = pick(bits["Z1"], one[:64], one[64:])
    two = pick(bits["Z1"], two[0], two[1])
    from_e1 = lax.ppermute((p_e1.astype(F32) + from_g1.astype(F32)).astype(BF), XY, Y_FLIP)
    from_f2 = lax.ppermute((p_f2.astype(F32) + from_e3.astype(F32)).astype(BF), XY, X_DOWN2)
    early = local_call(
        early_kernel,
        "early",
        shape((8, width), F32),
        [grad_att, grad_q, grad_pre, grad_attn_shard, grad_norm2, scaled2, cot_shard],
        mib=8,
        moved=4 << 20,
    )
    from_e1 = after(from_e1, early)
    send0 = [(v[1:] + g[1:].astype(F32)).astype(BF) for v, g in zip(rest, got1)]
    from_f2 = after(from_f2, send0)
    mlp_got = after(mlp_got, from_e1).astype(F32)
    one, two = one + mlp_got[:64], two + mlp_got[64:]
    give = [pick(bits["Z3"], v[32:], v[:32]).astype(BF) for v in (one, two)]
    mlp_give = jnp.concatenate(give, axis=0)
    mlp_kept = jnp.concatenate([pick(bits["Z3"], v[:32], v[32:]) for v in (one, two)], axis=0)
    from_f2 = after(from_f2, mlp_give)
    grad_kv = (own_part + from_f1.astype(F32) + from_e1.astype(F32) + from_f2.astype(F32)).astype(BF)

    qkv_full = jnp.concatenate([q_full, kv_full], axis=1)
    grad_qkv = jnp.concatenate([grad_q, grad_kv], axis=1)
    tail = {}

    kv_plan = [(ORDER_A, 0, 0, hidden), (ORDER_B, 0, hidden, hidden)]

    def beside_fg(stage, events, kept):
        now = events[-1]
        if stage == 0:
            tail["q3"] = swaps(after(qo_send[0], now), qo_orders, 3)
            big["got0"] = big_swaps(after(send0, now), 0)
            tail["mlp"] = swap(after(mlp_give, now), "Z3")
            tail["kv"] = [tn(normed, after(grad_kv, now)).astype(BF)]
            return tail["kv"]
        if stage == 1:
            tail["small"] = local_call(
                late_kernel,
                "late",
                shape((8, width), F32),
                [bits["C"].astype(jnp.int32)[None], x, mean1, spread1, events[0], kept[0], early],
                in_smem=1,
                mib=8,
                moved=6 << 20,
            )
            tail["send"] = part(tail["kv"], [], bits, kv_plan, 3, small=tail["small"])
            tail["k3"] = swaps(tail["send"], kv_orders, 3)
            return [tail["send"], big["got0"], tail["mlp"]]
        if stage == 2:
            big["final"] = local_call(
                final_ffn_kernel,
                "final_ffn",
                [shape((width // 16, inner), F32), shape((inner, width // 16), F32)],
                [*rest, *got1, *after(big["got0"], now)],
                mib=8,
                moved=4 << 20,
            )
            tail["q3_high"] = swaps(after(qo_send[1], tail["q3"], now), qo_orders, 3)
            return [tail["k3"], tail["q3"], big["final"]]
        small = dict(small=tail["small"])
        if stage == 3:
            tail["k2"] = swaps(part(tail["kv"], [(after(tail["k3"], now), 0)], bits, kv_plan, 2, **small), kv_orders, 2)
            tail["q2"] = swaps(part(qo_grads, [(after(tail["q3_high"], now), 4)], bits, qo_plan, 2), qo_orders, 2)
            return tail["k2"]
        if stage == 4:
            gots = [(tail["k3"], 0), (after(tail["k2"], now), 0)]
            tail["k1"] = swaps(part(tail["kv"], gots, bits, kv_plan, 1, **small), kv_orders, 1)
            return [tail["k1"], tail["q2"]]
        gots = [(tail["k3"], 0), (tail["k2"], 0), (after(tail["k1"], now), 0)]
        tail["k0"] = swaps(part(tail["kv"], gots, bits, kv_plan, 0, **small), kv_orders, 0)
        gots = [(tail["q3"], 0), (after(tail["q2"], now), 0)]
        tail["q1"] = swaps(part(qo_grads, gots, bits, qo_plan, 1), qo_orders, 1)
        return [tail["k0"], tail["q1"]]

    (grad_norm1,), _, _ = reduce_tp([lambda v: nt(v, qkv_full)], [grad_qkv], bits, beside_fg)
    x_scaled, x_spread = norm_stats(x_shard)
    grad_x = grad_middle + norm_back(grad_norm1, gain1, x_scaled, x_spread)
    mlp_total = mlp_kept + tail["mlp"].astype(F32)
    layer_shard = (middle + (mlp_total + con_bias)).astype(BF)
    both, _ = gather_tp(jnp.stack([grad_x.astype(BF), layer_shard]), bits, beside_fg)
    input_grad, layer_output = both[0].astype(F32), both[1]
    gots = [(tail[k], 0) for k in ("k3", "k2", "k1", "k0")]
    k_grad, v_grad, small = part(tail["kv"], gots, bits, kv_plan, -1, small=tail["small"])
    biases, q_bias_grad = small[6:7], small[7:8]
    for kind in ("C", "Z1", "Z3"):
        small = small + swap(small, kind)
    gots = [(v, 0) for v in (tail["q3"], tail["q2"], tail["q1"])]
    qo0 = swaps(part(qo_grads, gots, bits, qo_plan, 0), qo_orders, 0)
    gots = gots + [(qo0, 0)]
    q_grad, o_grad = local_call(
        final_qo_kernel,
        "final_qo",
        [shape((width // 16, hidden), F32), shape((hidden, width // 16), F32)],
        [bits["me"], *qo_grads, *[g for got, _ in gots for g in got]],
        in_smem=1,
        mib=6,
        moved=1 << 20,
    )
    expand_grad, contract_grad = big["final"]

    return (
        layer_output[None],
        input_grad[None],
        small[0],
        small[1],
        q_grad,
        q_bias_grad[:, :nb],
        k_grad[0],
        v_grad[0],
        biases[:, :nb],
        o_grad,
        small[2],
        small[3],
        small[4],
        expand_grad,
        biases[:, nb : nb + ne],
        contract_grad,
        small[5],
    )


def solution(mesh):
    both = ("fsdp", "ctx")
    rows, cols, vec = P(both, "tp"), P("tp", both), P(both)
    act = P("fsdp", "ctx", None)
    return jax.shard_map(
        body,
        mesh=mesh,
        in_specs=(
            act, P("fsdp", None), vec, vec, rows, cols, rows, rows, cols, cols, vec, vec, vec,
            rows, cols, cols, vec, act,
        ),
        out_specs=(
            act, act, vec, vec, rows, cols, rows, rows, cols, cols, vec, vec, vec, rows, cols, cols, vec,
        ),
        check_vma=False,
    )
```

```python
import math

import jax
import jax.numpy as jnp
from jax import lax
from jax.experimental import pallas as pl
from jax.experimental.pallas import tpu as pltpu
from jax.sharding import PartitionSpec as P

HEAD_DIM = 128
BF = jnp.bfloat16
F32 = jnp.float32
XY = ("fsdp", "ctx")
NEG = -1e30
SCALE = 1.0 / math.sqrt(HEAD_DIM)


def lin(x, y):
    return (y // 2) * 8 + x * 2 + y % 2


def pairs_xy(move):
    out = []
    for x in range(4):
        for y in range(4):
            to = move(x, y)
            if to is not None:
                out.append((lin(x, y), lin(*to)))
    return out


PERM = {
    "X1": pairs_xy(lambda x, y: (x ^ 1, y)),
    "X3": pairs_xy(lambda x, y: (x ^ 3, y)),
    "Y1": pairs_xy(lambda x, y: (x, y ^ 1)),
    "Y3": pairs_xy(lambda x, y: (x, y ^ 3)),
    "C": [(t, t ^ 1) for t in range(8)],
    "Z1": [(t, t ^ 2) for t in range(8)],
    "Z3": [(t, t ^ 6) for t in range(8)],
}
VEC = {"X1": (1, 0), "X3": (3, 0), "Y1": (0, 1), "Y3": (0, 3)}
ORDER_A = ("X1", "Y1", "X3", "Y3")
ORDER_B = ("Y1", "X3", "Y3", "X1")
ORDER_C = ("X3", "Y3", "X1", "Y1")
ORDER_D = ("Y3", "X1", "Y1", "X3")
ORDER_E = ("X1", "X3", "Y1", "Y3")
ORDER_F = ("X3", "X1", "Y3", "Y1")
ORDER_P = ("X3", "X1", "Y3", "Y1")
ORDER_Q = ("X3", "X1", "Y1", "Y3")
ORDER_R = ("Y3", "Y1", "X3", "X1")
ORDER_S = ("Y3", "Y1", "X1", "X3")


def swap(value, kind):
    return lax.ppermute(value, XY if kind in VEC else "tp", PERM[kind])


def offsets(order):
    out = []
    for p in range(16):
        x = y = 0
        for k, kind in enumerate(order):
            if (p >> k) & 1:
                x ^= VEC[kind][0]
                y ^= VEC[kind][1]
        out.append(lin(x, y))
    return out


def own_bits(length):
    c = lax.axis_index("ctx").astype(jnp.int32)
    t = lax.axis_index("tp").astype(jnp.int32)
    z1, z0, k = t >> 2, (t >> 1) & 1, t & 1
    near, far = z0 ^ z1, z1
    base = k * 256
    return lax.optimization_barrier(
        {
            "Z1": near == 1,
            "Z3": far == 1,
            "C": k == 1,
            "me": (lax.axis_index("fsdp").astype(jnp.int32) * 8 + c)[None],
            "core": k[None],
            "send": (1 - k) * 256,
            "keep": base,
            "one": base + near * 64 + far * 32,
            "two": base + 128 + far * 64 + near * 32,
            "place": c * length,
        }
    )


def rows_from(value, start, size):
    starts = (start,) + (jnp.int32(0),) * (value.ndim - 1)
    return lax.dynamic_slice(value, starts, (size,) + value.shape[1:], allow_negative_indices=False)


def pick(bit, if_zero, if_one):
    return jnp.where(bit, if_one, if_zero)


def merge(bit, own, got):
    return jnp.concatenate([pick(bit, own, got), pick(bit, got, own)], axis=0)


VMEM = pl.BlockSpec(memory_space=pltpu.VMEM)
SMEM = pl.BlockSpec(memory_space=pltpu.SMEM)


def local_call(kernel, name, out_shape, args, in_smem=0, mib=20, scratch=(), flops=0, moved=0, exps=0):
    return pl.pallas_call(
        kernel,
        out_shape=out_shape,
        in_specs=[SMEM] * in_smem + [VMEM] * (len(args) - in_smem),
        out_specs=jax.tree.map(lambda _: VMEM, out_shape),
        scratch_shapes=list(scratch),
        compiler_params=pltpu.CompilerParams(vmem_limit_bytes=mib << 20),
        cost_estimate=pl.CostEstimate(flops=flops, bytes_accessed=moved, transcendentals=exps),
        name=name,
    )(*args)


def fetch_call(kernel, name, out_shape, args, scratch=(), moved=0):
    args = [pltpu.with_memory_space_constraint(v, pltpu.HBM) for v in args]

    def whole(v):
        return pl.BlockSpec(v.shape, lambda i: (0,) * len(v.shape))

    return pl.pallas_call(
        kernel,
        grid=(1,),
        out_shape=out_shape,
        in_specs=[whole(v) for v in args],
        out_specs=jax.tree.map(whole, out_shape),
        scratch_shapes=list(scratch),
        compiler_params=pltpu.CompilerParams(vmem_limit_bytes=12 << 20),
        cost_estimate=pl.CostEstimate(flops=0, bytes_accessed=moved, transcendentals=0),
        name=name,
    )(*args)


def shape(dims, dtype=BF):
    return jax.ShapeDtypeStruct(dims, dtype)


def after(value, *events):
    return lax.optimization_barrier((value, events))[0]


def pack_kernel(key_ref, value_ref, query_ref, output_ref, *refs):
    vectors, outs, rows_ref = refs[:9], refs[9:13], refs[13]
    rows_ref[...] = jnp.zeros(rows_ref.shape, F32)
    for i, v in enumerate(vectors):
        rows_ref[i : i + 1, : v.shape[1]] = v[...]
    rows, width = key_ref.shape
    outs[0][:rows] = key_ref[...].astype(BF)
    outs[0][rows:, :128] = rows_ref[...].astype(BF)
    outs[0][rows:, 128:] = jnp.zeros((16, width - 128), BF)
    outs[1][...] = value_ref[...].astype(BF)
    outs[2][...] = query_ref[...].astype(BF)
    outs[3][...] = output_ref[...].T.astype(BF)


def pack_ffn_kernel(expand_ref, contract_ref, *outs):
    half = expand_ref.shape[1] // 2
    for i in range(2):
        outs[i][...] = expand_ref[:, i * half : (i + 1) * half].astype(BF)
        outs[2 + i][...] = contract_ref[i * half : (i + 1) * half].T.astype(BF)


def join_kernel(count, *refs):
    for own, got, out in zip(refs[:count], refs[count : 2 * count], refs[2 * count :]):
        n = own.shape[0]
        out[:n] = own[...]
        out[n:] = got[...]


def join(owns, gots):
    shapes = [shape((2 * v.shape[0],) + v.shape[1:]) for v in owns]
    size = sum(v.size for v in owns)
    count = len(owns)
    return local_call(lambda *r: join_kernel(count, *r), "join", shapes, [*owns, *gots], mib=4, moved=8 * size)


def swaps(bufs, orders, k):
    return [swap(b, o[k]) for b, o in zip(bufs, orders)]


def place_kernel(rows, plan, count, small, me_ref, *refs):
    owns, gots, outs = refs[:count], refs[count : 2 * count], refs[2 * count :]
    me = me_ref[0]
    if small:
        vec_ref, query_ref, expand_ref = outs[-3:]
        query_ref[...] = jnp.zeros(query_ref.shape, F32)
        expand_ref[...] = jnp.zeros(expand_ref.shape, F32)
    for s, (order, target, column) in enumerate(plan):
        width = owns[s].shape[2]
        away = offsets(order)
        for p in range(16):
            src = owns[s] if p < 8 else gots[s]
            block = me ^ away[p]
            row = pl.multiple_of(block * rows, rows)
            outs[target][pl.ds(row, rows), column : column + width] = src[p % 8, :rows]
            if small and s == 0:
                more = src[p % 8, rows:, :128].astype(F32)
                vec_ref[:, pl.ds(pl.multiple_of(block * 128, 128), 128)] = more[:8]
                cols = pl.ds(pl.multiple_of((block // 8) * 128, 128), 128)
                query_ref[:, cols] = query_ref[:, cols] + pltpu.roll(more[:8], (block % 8) * 16, 1)[6:7]
                cols = pl.ds(pl.multiple_of((block // 2) * 128, 128), 128)
                expand_ref[:, cols] = expand_ref[:, cols] + pltpu.roll(more[8:], (block % 2) * 64, 1)[0:1]


def place(owns, gots, bits, rows, plan, widths, small=()):
    shapes = [shape((16 * rows, w)) for w in widths]
    if small:
        shapes += [shape((8, 2048), F32)] + [shape((1, w), F32) for w in small]
    count = len(owns)
    return local_call(
        lambda *r: place_kernel(rows, plan, count, bool(small), *r),
        "place",
        shapes,
        [bits["me"], *owns, *gots],
        in_smem=1,
        mib=6,
        moved=64 * rows * sum(widths),
    )


def part(grads, gots, bits, plan, step, half=None, small=None):
    rows = grads[0].shape[0] // 16
    low, count = (1 << step, 1 << step) if step >= 0 else (0, 1)
    if half is not None:
        count //= 2
        low += half * count
    n, ng = len(plan), len(grads)
    extra = 16 if small is not None and step >= 0 else 0
    shapes = [shape((count, rows + (extra if s == 0 else 0), p[3]), BF if step >= 0 else F32) for s, p in enumerate(plan)]
    if small is not None and step < 0:
        shapes.append(shape((8, 128), F32))

    def kernel(me_ref, *refs):
        me = me_ref[0]
        first = ng + n * len(gots)
        outs = refs[first + (small is not None) :]
        for s, (order, source, column, width) in enumerate(plan):
            away = offsets(order)
            for q in range(count):
                p = low + q
                row = pl.multiple_of((me ^ away[p]) * rows, rows)
                piece = refs[source][pl.ds(row, rows), column : column + width]
                if gots:
                    piece = piece.astype(F32)
                    for j, (_, base) in enumerate(gots):
                        piece = piece + refs[ng + n * j + s][p - base, :rows].astype(F32)
                outs[s][q, :rows] = piece.astype(outs[s].dtype)
                if small is not None and s == 0:
                    lane = pl.multiple_of((me ^ away[p]) * 128, 128)
                    vectors = jnp.concatenate([refs[first][:, pl.ds(lane, 128)], jnp.zeros((8, 128), F32)], axis=0)
                    for j, (_, base) in enumerate(gots):
                        vectors = vectors + refs[ng + n * j][p - base, rows:, :128].astype(F32)
                    if step >= 0:
                        outs[0][q, rows:, :128] = vectors.astype(BF)
                        outs[0][q, rows:, 128:] = jnp.zeros((16, width - 128), BF)
                    else:
                        outs[-1][...] = vectors[:8]

    args = [bits["me"], *grads, *[g for got, _ in gots for g in got]] + ([small] if small is not None else [])
    moved = 2 * count * rows * sum(p[3] for p in plan) * (2 + len(gots))
    return local_call(kernel, "part", shapes, args, in_smem=1, mib=6, moved=moved)


BIG = ((ORDER_P, ORDER_Q), (ORDER_R, ORDER_S))


def big_part(grads, gots, bits, step):
    rows, width = grads[0].shape[0] // 16, grads[0].shape[1]
    half = width // 2
    count = 1 << step
    in_specs, args, spans, outs = [], [], [], []
    per = 1 + len(gots)
    for low in (count, 0) if step == 1 else (count,):
        for m, pair in enumerate(BIG):
            for s, order in enumerate(pair):
                near = [offsets(order)[1 << k] for k in range(4)]

                def block_at(q, me, near=near, low=low, s=s):
                    p = low + q
                    where = me[0]
                    for k, away in enumerate(near):
                        where = where ^ (((p >> k) & 1) * away)
                    return (where, s)

                in_specs.append(pl.BlockSpec((rows, half), block_at))
                args.append(grads[m])
                for got in gots:
                    in_specs.append(pl.BlockSpec((1, rows, half), lambda q, me, low=low: (low + q, 0, 0)))
                    args.append(got[2 * m + s])
                if step > 1:
                    outs.append(shape((count, rows, half)))
                    spans.append((len(outs) - 1, 0))
                elif s == 0:
                    outs.append(shape((count, rows, width), BF if low else F32))
                    spans.append((len(outs) - 1, 0))
                else:
                    spans.append((len(outs) - 1, half))

    def kernel(me_ref, *refs):
        out_refs = refs[len(args) :]
        for i, (at, column) in enumerate(spans):
            piece = refs[per * i][...]
            if gots:
                piece = piece.astype(F32)
                for j in range(1, per):
                    piece = piece + refs[per * i + j][0].astype(F32)
            out_refs[at][0, :, column : column + half] = piece.astype(outs[at].dtype)

    return pl.pallas_call(
        kernel,
        grid_spec=pltpu.PrefetchScalarGridSpec(
            num_scalar_prefetch=1,
            grid=(count,),
            in_specs=in_specs,
            out_specs=[pl.BlockSpec((1,) + o.shape[1:], lambda q, me: (q, 0, 0)) for o in outs],
        ),
        out_shape=outs,
        compiler_params=pltpu.CompilerParams(vmem_limit_bytes=12 << 20),
        cost_estimate=pl.CostEstimate(flops=0, bytes_accessed=4 * count * rows * width * (1 + per), transcendentals=0),
        name="big_part",
    )(bits["me"], *args)


def big_swaps(values, step):
    if step >= 2:
        return [swap(v, o[step]) for v, o in zip(values, BIG[0] + BIG[1])]
    return [swap(v, pair[0][step]) for v, pair in zip(values, BIG)]


def shard_rows(value, bits):
    return jnp.concatenate([rows_from(value, bits["one"], 32), rows_from(value, bits["two"], 32)], axis=0)


def halves(value, bits):
    return rows_from(value, bits["send"], 256), rows_from(value, bits["keep"], 256)


def reduce_tp(products, operands, bits, beside=None):
    count = len(products)
    pairs = [halves(v, bits) for v in operands]
    send = jnp.concatenate([p(v[0]).astype(BF) for p, v in zip(products, pairs)], axis=0)
    first = swap(send, "C")
    kept = [p(v[1]) for p, v in zip(products, pairs)]
    events = [send]
    if beside:
        first = after(first, beside(0, events, kept))
    totals = [v + first[i * 256 : (i + 1) * 256].astype(F32) for i, v in enumerate(kept)]
    events.append(first)
    streams = [[v[:128] for v in totals], [v[128:] for v in totals]]
    for stage, kinds in enumerate((("Z1", "Z3"), ("Z3", "Z1"))):
        n = streams[0][0].shape[0] // 2
        give = [
            jnp.concatenate([pick(bits[t], v[n:], v[:n]).astype(BF) for v in parts], axis=0)
            for t, parts in zip(kinds, streams)
        ]
        got = [swap(v, t) for v, t in zip(give, kinds)]
        if beside:
            got = after(got, beside(1 + stage, events, kept))
        events.append(got)
        streams = [
            [pick(bits[t], v[:n], v[n:]) + g[i * n : (i + 1) * n].astype(F32) for i, v in enumerate(parts)]
            for t, parts, g in zip(kinds, streams, got)
        ]
    out = [jnp.concatenate([streams[0][i], streams[1][i]], axis=0) for i in range(count)]
    return out, events, kept


def merge_rows(bit, own, got):
    return jnp.concatenate([pick(bit, own, got), pick(bit, got, own)], axis=1)


def gather_tp(shards, bits, beside=None, whole=True):
    parts = [shards[:, :32], shards[:, 32:]]
    events = [shards]
    for stage, kinds in enumerate((("Z3", "Z1"), ("Z1", "Z3"))):
        got = [swap(v, t) for v, t in zip(parts, kinds)]
        if beside:
            got = after(got, beside(3 + stage, events, None))
        events.append(got)
        parts = [merge_rows(bits[t], v, g) for t, v, g in zip(kinds, parts, got)]
    own = jnp.concatenate(parts, axis=1)
    last = swap(own, "C")
    if beside:
        last = after(last, beside(5, events, None))
    events.append(last)
    return (merge_rows(bits["C"], own, last) if whole else (own, last)), events


Y_FLIP = PERM["Y1"]
Y_FLIP_DOWN = pairs_xy(lambda x, y: (x, y ^ 1) if y % 2 == 1 else None)
Y_FLIP_UP = pairs_xy(lambda x, y: (x, y ^ 1) if y % 2 == 0 else None)
X_UP = pairs_xy(lambda x, y: (x + 1, y) if x < 3 else None)
X_UP2 = pairs_xy(lambda x, y: (x + 2, y) if x < 2 else None)
X_DOWN = pairs_xy(lambda x, y: (x - 1, y) if x > 0 else None)
X_DOWN2 = pairs_xy(lambda x, y: (x - 2, y) if x > 1 else None)
SLOTS = 6


def slot_block(slot, c):
    back = slot // 2 * 2
    return c - back if slot % 2 == 0 else (c ^ 1) - back


def slot_needed(slot, c, length, first_ref):
    block = slot_block(slot, c)
    return (block >= 0) & (block < c) & (block * length + length - 1 >= first_ref[0])


def nt(a, b):
    return lax.dot_general(a, b, (((1,), (1,)), ((), ())), preferred_element_type=F32)


def tn(a, b):
    return lax.dot_general(a, b, (((0,), (0,)), ((), ())), preferred_element_type=F32)


def nn(a, b):
    return jnp.dot(a, b, preferred_element_type=F32)


def visible(slot, block, length, start_ref, c):
    keys = lax.broadcasted_iota(jnp.int32, (length, length), 0) + block * length
    mask = keys >= start_ref[...]
    if slot == 0:
        mask = mask & (keys <= lax.broadcasted_iota(jnp.int32, (length, length), 1) + c * length)
    return mask


def attn_fwd_kernel(heads, me_ref, first_ref, start_ref, q_ref, *refs):
    kv = refs[:SLOTS]
    att_ref, mix_ref, lse_ref, m_ref, l_ref = refs[SLOTS:]
    length = q_ref.shape[0]
    hidden = heads * HEAD_DIM
    c = me_ref[0] % 8
    for slot in range(SLOTS):
        block = slot_block(slot, c)

        def run(slot=slot, block=block):
            mask = visible(slot, block, length, start_ref, c)
            for h in range(heads):
                cols = slice(h * HEAD_DIM, (h + 1) * HEAD_DIM)
                key = kv[slot][:, cols]
                val = kv[slot][:, hidden + h * HEAD_DIM : hidden + (h + 1) * HEAD_DIM]
                s = jnp.where(mask, nt(key, q_ref[:, cols]) * SCALE, NEG)
                top = jnp.max(s, axis=0, keepdims=True)
                if slot == 0:
                    p = jnp.exp(s - top)
                    m_ref[h : h + 1] = top
                    l_ref[h : h + 1] = jnp.sum(p, axis=0, keepdims=True)
                    mix_ref[cols] = tn(val, p.astype(BF))
                else:
                    old = m_ref[h : h + 1]
                    new = jnp.maximum(old, top)
                    p = jnp.exp(s - new)
                    shrink = jnp.exp(old - new)
                    m_ref[h : h + 1] = new
                    l_ref[h : h + 1] = l_ref[h : h + 1] * shrink + jnp.sum(p, axis=0, keepdims=True)
                    mix_ref[cols] = mix_ref[cols] * shrink + tn(val, p.astype(BF))

        if slot == 0:
            run()
        else:
            pl.when(slot_needed(slot, c, length, first_ref))(run)
    for h in range(heads):
        cols = slice(h * HEAD_DIM, (h + 1) * HEAD_DIM)
        out = mix_ref[cols] / l_ref[h : h + 1]
        mix_ref[cols] = out
        att_ref[:, cols] = out.T.astype(BF)
        lse_ref[h : h + 1] = m_ref[h : h + 1] + jnp.log(l_ref[h : h + 1])


def attn_bwd_kernel(heads, me_ref, first_ref, start_ref, q_ref, do_ref, mix_ref, lse_ref, *refs):
    kv = refs[:SLOTS]
    dq_ref, dkv = refs[SLOTS], refs[SLOTS + 1 : 2 * SLOTS + 1]
    dqt_ref, delta_ref = refs[2 * SLOTS + 1 :]
    length = q_ref.shape[0]
    hidden = heads * HEAD_DIM
    c = me_ref[0] % 8
    for h in range(heads):
        cols = slice(h * HEAD_DIM, (h + 1) * HEAD_DIM)
        dot_t = do_ref[:, cols].astype(F32).T
        delta_ref[h : h + 1] = jnp.sum(dot_t * mix_ref[cols], axis=0, keepdims=True)
    for slot in range(SLOTS):
        block = slot_block(slot, c)

        def run(slot=slot, block=block):
            mask = visible(slot, block, length, start_ref, c)
            for h in range(heads):
                cols = slice(h * HEAD_DIM, (h + 1) * HEAD_DIM)
                vcols = slice(hidden + h * HEAD_DIM, hidden + (h + 1) * HEAD_DIM)
                key, val = kv[slot][:, cols], kv[slot][:, vcols]
                q, do = q_ref[:, cols], do_ref[:, cols]
                s = jnp.where(mask, nt(key, q) * SCALE, NEG)
                p = jnp.exp(s - lse_ref[h : h + 1])
                ds = (p * (nt(val, do) - delta_ref[h : h + 1])).astype(BF)
                dkv[slot][:, cols] = (nn(ds, q) * SCALE).astype(dkv[slot].dtype)
                dkv[slot][:, vcols] = nn(p.astype(BF), do).astype(dkv[slot].dtype)
                part = tn(key, ds)
                if slot == 0:
                    dqt_ref[cols] = part
                else:
                    dqt_ref[cols] = dqt_ref[cols] + part

        if slot == 0:
            run()
        else:
            pl.when(slot_needed(slot, c, length, first_ref))(run)

            @pl.when(jnp.logical_not(slot_needed(slot, c, length, first_ref)))
            def _(slot=slot):
                dkv[slot][...] = jnp.zeros(dkv[slot].shape, dkv[slot].dtype)

    for h in range(heads):
        cols = slice(h * HEAD_DIM, (h + 1) * HEAD_DIM)
        dq_ref[:, cols] = (dqt_ref[cols] * SCALE).T.astype(BF)


def stats_kernel(x_ref, mean_ref, spread_ref):
    for r in range(0, x_ref.shape[0], 64):
        v = x_ref[r : r + 64].astype(F32)
        mean = jnp.mean(v, axis=-1, keepdims=True)
        centre = v - mean
        spread = lax.rsqrt(jnp.mean(centre * centre, axis=-1, keepdims=True) + 1e-05)
        mean_ref[r : r + 64] = jnp.broadcast_to(mean, (64, 128))
        spread_ref[r : r + 64] = jnp.broadcast_to(spread, (64, 128))


def norm_kv_kernel(me_ref, x_ref, mean_ref, spread_ref, k_own, v_own, k_got, v_got, normed_ref, kv_ref, acc_ref):
    me = me_ref[0]
    hidden = k_own.shape[2]
    zero = jnp.zeros((1, 128), F32)
    bias = [zero, zero]
    away_k, away_v = offsets(ORDER_A), offsets(ORDER_B)
    for q in range(8):
        parts = []
        for src, p in ((k_own, q), (k_got, q + 8)):
            block = me ^ away_k[p]
            cols = pl.ds(pl.multiple_of(block * 128, 128), 128)
            small = src[q, 128:144, :128].astype(F32)
            scaled = (x_ref[:, cols].astype(F32) - mean_ref[...]) * spread_ref[...]
            part = (scaled * small[0:1] + small[1:2]).astype(BF)
            normed_ref[:, cols] = part
            parts.append(part)
            turned = pltpu.roll(small[:8], (block % 8) * 16, 1)[7:8]
            bias = [bias[0] + jnp.where(block < 8, turned, zero), bias[1] + jnp.where(block < 8, zero, turned)]
        weights = jnp.concatenate([k_own[q, :128], k_got[q, :128]], axis=0)
        term = jnp.dot(jnp.concatenate(parts, axis=1), weights, preferred_element_type=F32)
        acc_ref[...] = term if q == 0 else acc_ref[...] + term
    kv_ref[:, :hidden] = acc_ref[...].astype(BF)
    for q in range(8):
        parts = []
        for p in (q, q + 8):
            parts.append(normed_ref[:, pl.ds(pl.multiple_of((me ^ away_v[p]) * 128, 128), 128)])
        weights = jnp.concatenate([v_own[q], v_got[q]], axis=0)
        term = jnp.dot(jnp.concatenate(parts, axis=1), weights, preferred_element_type=F32)
        acc_ref[...] = term if q == 0 else acc_ref[...] + term
    kv_ref[:, hidden:] = (acc_ref[...] + jnp.concatenate(bias, axis=1)).astype(BF)


def early_kernel(att_ref, query_ref, pre_ref, attn_ref, norm_ref, scaled_ref, cot_ref, out_ref):
    def total(v):
        return jnp.sum(v.astype(F32), axis=0, keepdims=True)

    out_ref[0:2] = jnp.zeros((2, out_ref.shape[1]), F32)
    out_ref[2:3] = total(attn_ref[...])
    out_ref[3:4] = total(norm_ref[...] * scaled_ref[...])
    out_ref[4:5] = total(norm_ref[...])
    out_ref[5:6] = total(cot_ref[...])
    value, query, expand = total(att_ref[...]), total(query_ref[...]), total(pre_ref[...])
    lane = lax.broadcasted_iota(jnp.int32, (8, 128), 1)

    def taken(row, size, block, to):
        at = block * size
        wide = jnp.broadcast_to(row[:, at // 128 * 128 : at // 128 * 128 + 128], (8, 128))
        wide = pltpu.roll(wide, (128 - at % 128 + to) % 128, 1)
        return jnp.where((lane >= to) & (lane < to + size), wide, 0.0)[0:1]

    nb, ne = value.shape[1] // 16, expand.shape[1] // 16
    for block in range(16):
        cols = slice(block * 128, block * 128 + 128)
        out_ref[6:7, cols] = taken(value, nb, block, 0) + taken(expand, ne, block, nb)
        out_ref[7:8, cols] = taken(query, nb, block, 0)


def late_kernel(core_ref, x_ref, mean_ref, spread_ref, gone_ref, kept_ref, early_ref, out_ref):
    core = core_ref[0]
    size = gone_ref.shape[0]
    out_ref[...] = early_ref[...]
    first = jnp.zeros((1, x_ref.shape[1]), F32)
    second = first
    for src, base in ((gone_ref, (1 - core) * size), (kept_ref, core * size)):
        for r in range(0, size, 32):
            rows = pl.ds(pl.multiple_of(base + r, 32), 32)
            scaled = (x_ref[rows].astype(F32) - mean_ref[rows][:, :1]) * spread_ref[rows][:, :1]
            grad = src[r : r + 32].astype(F32)
            first = first + jnp.sum(grad * scaled, axis=0, keepdims=True)
            second = second + jnp.sum(grad, axis=0, keepdims=True)
    out_ref[0:1] = first
    out_ref[1:2] = second


def final_ffn_kernel(*refs):
    kept, one, zero, outs = refs[:2], refs[2:4], refs[4:6], refs[6:]
    total = [k[0] + a[0].astype(F32) + b[0].astype(F32) for k, a, b in zip(kept, one, zero)]
    outs[0][...] = total[0]
    for j in range(0, total[1].shape[1], 128):
        outs[1][j : j + 128] = total[1][:, j : j + 128].T


def final_rows_kernel(core_ref, own_ref, last_ref, grad_ref, out_ref):
    size = own_ref.shape[1]
    core = core_ref[0]
    for src, base in ((own_ref, core * size), (last_ref, (1 - core) * size)):
        for r in range(0, size, 64):
            rows = pl.ds(pl.multiple_of(base + r, 64), 64)
            grad_ref[rows] = src[0, r : r + 64].astype(F32)
            out_ref[rows] = src[1, r : r + 64]


def final_qo_kernel(me_ref, grad_ref, *refs):
    gots, outs = refs[:-2], refs[-2:]
    piece = grad_ref[pl.ds(pl.multiple_of(me_ref[0] * 128, 128), 128)].astype(F32)
    for got in gots:
        piece = piece + got[0].astype(F32)
    half = piece.shape[1] // 2
    outs[0][...] = piece[:, :half]
    outs[1][...] = piece[:, half:].T


def norm_stats(v):
    mean = jnp.mean(v, axis=-1, keepdims=True)
    centre = v - mean
    spread = lax.rsqrt(jnp.mean(centre * centre, axis=-1, keepdims=True) + 1e-05)
    return centre * spread, spread


def norm_back(grad, gain, scaled, spread):
    weighted = grad * gain
    inner = jnp.mean(weighted, axis=-1, keepdims=True)
    cross = jnp.mean(weighted * scaled, axis=-1, keepdims=True)
    return spread * (weighted - inner - scaled * cross)


def cols_of(w, n=4):
    k = w.shape[1] // n
    return [w[:, i * k : (i + 1) * k] for i in range(n)]


def body(
    layer_input,
    doc_ids,
    pre_gain,
    pre_shift,
    query_weight,
    query_bias,
    key_weight,
    value_weight,
    value_bias,
    output_weight,
    output_bias,
    mid_gain,
    mid_shift,
    expand_weight,
    expand_bias,
    contract_weight,
    contract_bias,
    cotangent,
):
    bits = own_bits(layer_input.shape[1])
    x = layer_input[0]
    cot = cotangent[0]
    length, width = x.shape
    hidden = query_weight.shape[1]
    heads = hidden // HEAD_DIM
    inner = expand_weight.shape[1]

    nb, ne = query_bias.shape[1], expand_bias.shape[1]
    pre_gain = after(pre_gain, bits)
    vectors = [pre_gain, pre_shift, output_bias, mid_gain, mid_shift, contract_bias]
    weights = [key_weight, value_weight, query_weight, output_weight]
    packed = shape((128, hidden))
    bufs = fetch_call(
        pack_kernel,
        "pack",
        [shape((144, hidden)), packed, packed, packed],
        [*weights, *[v[None] for v in vectors], query_bias, value_bias, expand_bias],
        scratch=[pltpu.VMEM((16, 128), F32)],
        moved=800 << 10,
    )
    bufs = [v[None] for v in bufs]
    first_orders, big_orders = (ORDER_A, ORDER_B, ORDER_C, ORDER_D), (ORDER_E, ORDER_F)
    kv_orders, qo_orders = (ORDER_A, ORDER_B), (ORDER_D,)
    half_shape = shape((128, inner // 2))
    ffn = fetch_call(
        pack_ffn_kernel, "pack_ffn", [half_shape] * 4, [expand_weight, contract_weight], moved=1536 << 10
    )
    con = [v[None] for v in ffn[2:]]
    bufs = join(bufs, swaps(bufs, first_orders, 0))
    got = swaps(bufs, first_orders, 1)
    stats = [shape((length, 128), F32)] * 2
    mean1, spread1 = local_call(stats_kernel, "stats", stats, [after(x, bufs)], mib=8, moved=3 << 20)
    one = swaps(con[:1], big_orders[:1], 0)
    bufs = join(bufs, after(got, one, mean1))
    got = swaps(bufs, first_orders, 2)
    two = swaps(con[1:], big_orders[1:], 0)
    bufs = join(bufs, after(got, two))
    con = join(con, one + two)
    got = swaps(bufs, first_orders, 3)
    got_con = swaps(after(con, got), big_orders, 1)
    exp_orders = (ORDER_A, ORDER_B)
    exp = [v[None] for v in ffn[:2]]
    got_exp = swaps(after(exp, got), exp_orders, 0)

    docs = doc_ids[0]
    own_docs = rows_from(docs, bits["place"], length)
    start = jnp.sum((docs[:, None] < own_docs[None, :]).astype(jnp.int32), axis=0)
    first_key = start[:1]
    start = start[None]

    normed, kv_own = local_call(
        norm_kv_kernel,
        "norm_kv",
        [shape((length, width)), shape((length, 2 * hidden))],
        [bits["me"], x, mean1, spread1, bufs[0], bufs[1], got[0], got[1]],
        in_smem=1,
        mib=10,
        scratch=[pltpu.VMEM((length, hidden), F32)],
        flops=2 * length * width * 2 * hidden,
        moved=6 << 20,
    )
    kv_own = after(kv_own, got_con, got_exp)
    kv_e1 = lax.ppermute(kv_own, XY, Y_FLIP)
    kv_f1 = lax.ppermute(kv_own, XY, X_UP)
    kv_f2 = lax.ppermute(kv_own, XY, X_UP2)
    con = join(con, got_con)
    exp = join(exp, got_exp)
    got_con = swaps(con, big_orders, 2)
    kv_e1 = after(kv_e1, exp, con, kv_f1)
    plan = [(ORDER_A, 0, 0), (ORDER_B, 0, hidden), (ORDER_C, 1, 0), (ORDER_D, 2, 0)]
    kv_full, q_full, o_full, vec, q_bias, e_bias = place(
        after(bufs, kv_e1), got, bits, 128, plan, [2 * hidden, hidden, hidden], [hidden, inner]
    )
    gain1, out_bias, gain2, shift2, con_bias = [vec[i : i + 1] for i in (0, 2, 3, 4, 5)]
    kv_g1 = lax.ppermute(after(kv_e1, kv_f2), XY, X_UP)
    kv_e3 = lax.ppermute(kv_f2, XY, Y_FLIP_DOWN)
    queries = (nn(normed, q_full) + q_bias).astype(BF)
    con = join(con, after(got_con, kv_e1))
    got_con = swaps(con, big_orders, 3)

    slots = [kv_own, kv_e1, kv_f1, kv_g1, kv_f2, kv_e3]
    attended, mixture, lse = local_call(
        lambda *refs: attn_fwd_kernel(heads, *refs),
        "attn_fwd",
        [shape((length, hidden)), shape((hidden, length), F32), shape((heads, length), F32)],
        [bits["me"], first_key, start, after(queries, con), *slots],
        in_smem=2,
        mib=12,
        scratch=[pltpu.VMEM((heads, length), F32), pltpu.VMEM((heads, length), F32)],
        flops=10**9,
        moved=6 << 20,
        exps=3 * 10**6,
    )

    feed = {}

    def beside_a(stage, events, kept):
        now = events[-1]
        if stage == 0:
            plan = [(ORDER_E, 0, 0), (ORDER_F, 0, inner // 2)]
            feed["contract"] = place(con, got_con, bits, 128, plan, [inner])[0]
            feed["got"] = swaps(after(exp, now), exp_orders, 1)
            return [feed["contract"], feed["got"]]
        if stage == 1:
            feed["exp"] = join(exp, after(feed["got"], now))
            feed["got"] = swaps(feed["exp"], exp_orders, 2)
        if stage == 2:
            return feed["got"]
        if stage == 3:
            feed["exp"] = join(feed["exp"], after(feed["got"], now))
            feed["got"] = swaps(feed["exp"], exp_orders, 3)
        return []

    (attn_total,), _, _ = reduce_tp([lambda v: nt(v, o_full)], [attended], bits, beside_a)
    contract_full = feed["contract"]
    x_shard = shard_rows(x, bits).astype(F32)
    middle = x_shard + (attn_total + out_bias)
    scaled2, spread2 = norm_stats(middle)
    normed_two, _ = gather_tp((scaled2 * gain2 + shift2).astype(BF)[None], bits, beside_a)
    normed_two = normed_two[0]

    plan = [(ORDER_A, 0, 0), (ORDER_B, 0, inner // 2)]
    expand_full = place(feed["exp"], feed["got"], bits, 128, plan, [inner])[0]
    grad_act = nn(cot, contract_full)
    pre_act = nn(normed_two, expand_full) + e_bias
    cdf = 0.5 * (1.0 + lax.erf(pre_act * (1.0 / math.sqrt(2.0))))
    activated = (pre_act * cdf).astype(BF)
    slope = cdf + pre_act * jnp.exp(-0.5 * pre_act * pre_act) * (1.0 / math.sqrt(2.0 * math.pi))
    grad_pre = (slope * grad_act).astype(BF)
    big = {}

    def beside_de(stage, events, kept):
        if stage == 0:
            held = after((cot, activated, normed_two, grad_pre), events[-1])
            big["grads"] = [tn(held[2], held[3]).astype(BF), tn(held[0], held[1]).astype(BF)]
            big["send"] = big_part(big["grads"], [], bits, 3)
            return big["send"]
        if stage == 1:
            big["got3"] = big_swaps(after(big["send"], events[-1]), 3)
            return []
        if stage == 4:
            return big["got3"]
        if stage < 5:
            return []
        big["send"] = big_part(big["grads"], [after(big["got3"], events[-1])], bits, 2)
        big["got2"] = big_swaps(big["send"], 2)
        return big["send"]

    (grad_norm2,), _, _ = reduce_tp([lambda v: nt(v, expand_full)], [grad_pre], bits, beside_de)

    cot_shard = shard_rows(cot, bits).astype(F32)
    grad_middle = cot_shard + norm_back(grad_norm2, gain2, scaled2, spread2)
    grad_attn_shard = grad_middle.astype(BF)
    grad_attn, _ = gather_tp(grad_attn_shard[None], bits, beside_de)
    grad_attn = grad_attn[0]

    grad_att = nn(grad_attn, o_full).astype(BF)
    dkv = shape((length, 2 * hidden))
    grad_q, own_part, p_e1, p_f1, p_g1, p_f2, p_e3 = local_call(
        lambda *refs: attn_bwd_kernel(heads, *refs),
        "attn_bwd",
        [shape((length, hidden)), shape((length, 2 * hidden), F32)] + [dkv] * 5,
        [bits["me"], first_key, start, queries, after(grad_att, big["send"]), mixture, lse, *slots],
        in_smem=2,
        mib=16,
        scratch=[pltpu.VMEM((hidden, length), F32), pltpu.VMEM((heads, length), F32)],
        flops=2 * 10**9,
        moved=10 << 20,
        exps=3 * 10**6,
    )
    got2 = after(big["got2"], grad_q)
    both = big_part(big["grads"], [big["got3"], got2], bits, 1)
    rest = both[2:]
    from_g1 = lax.ppermute(after(p_g1, got2), XY, X_DOWN)
    from_e3 = lax.ppermute(after(p_e3, got2), XY, Y_FLIP_UP)
    got1 = big_swaps(both[:2], 1)
    mlp_send, mlp_keep = halves(activated, bits)
    mlp_got = swap(after(nt(mlp_send, contract_full).astype(BF), got2), "C")

    grad_o = tn(grad_attn, after(attended, grad_q)).astype(BF)
    qo_grads = [jnp.concatenate([tn(normed, grad_q).astype(BF), grad_o], axis=1)]
    qo_plan = [(ORDER_D, 0, 0, 2 * hidden)]
    qo_send = part(qo_grads, [], bits, qo_plan, 3, 0), part(qo_grads, [], bits, qo_plan, 3, 1)
    from_g1 = after(from_g1, got1, qo_send)
    from_f1 = lax.ppermute(after(p_f1, from_g1), XY, X_DOWN)
    total = nt(mlp_keep, contract_full) + after(mlp_got, from_g1).astype(F32)
    one, two = total[:128], total[128:]
    two = [jnp.concatenate([two[i : i + 32], two[i + 64 : i + 96]], axis=0) for i in (0, 32)]
    give = [pick(bits["Z1"], one[64:], one[:64]), pick(bits["Z1"], two[1], two[0])]
    mlp_got = swap(jnp.concatenate(give, axis=0).astype(BF), "Z1")
    one = pick(bits["Z1"], one[:64], one[64:])
    two = pick(bits["Z1"], two[0], two[1])
    from_e1 = lax.ppermute((p_e1.astype(F32) + from_g1.astype(F32)).astype(BF), XY, Y_FLIP)
    from_f2 = lax.ppermute((p_f2.astype(F32) + from_e3.astype(F32)).astype(BF), XY, X_DOWN2)
    early = local_call(
        early_kernel,
        "early",
        shape((8, width), F32),
        [grad_att, grad_q, grad_pre, grad_attn_shard, grad_norm2, scaled2, cot_shard],
        mib=8,
        moved=4 << 20,
    )
    from_e1 = after(from_e1, early)
    send0 = [(v[1:] + g[1:].astype(F32)).astype(BF) for v, g in zip(rest, got1)]
    from_f2 = after(from_f2, send0)
    mlp_got = after(mlp_got, from_e1).astype(F32)
    one, two = one + mlp_got[:64], two + mlp_got[64:]
    give = [pick(bits["Z3"], v[32:], v[:32]).astype(BF) for v in (one, two)]
    mlp_give = jnp.concatenate(give, axis=0)
    mlp_kept = jnp.concatenate([pick(bits["Z3"], v[:32], v[32:]) for v in (one, two)], axis=0)
    from_f2 = after(from_f2, mlp_give)
    grad_kv = (own_part + from_f1.astype(F32) + from_e1.astype(F32) + from_f2.astype(F32)).astype(BF)

    qkv_full = jnp.concatenate([q_full, kv_full], axis=1)
    grad_qkv = jnp.concatenate([grad_q, grad_kv], axis=1)
    tail = {}

    kv_plan = [(ORDER_A, 0, 0, hidden), (ORDER_B, 0, hidden, hidden)]

    def beside_fg(stage, events, kept):
        now = events[-1]
        if stage == 0:
            tail["q3"] = swaps(after(qo_send[0], now), qo_orders, 3)
            big["got0"] = big_swaps(after(send0, now), 0)
            tail["mlp"] = swap(after(mlp_give, now), "Z3")
            tail["kv"] = [tn(normed, after(grad_kv, now)).astype(BF)]
            return [tail["kv"], big["got0"], tail["mlp"]]
        if stage == 1:
            tail["small"] = local_call(
                late_kernel,
                "late",
                shape((8, width), F32),
                [bits["core"], x, mean1, spread1, events[0], kept[0], early],
                in_smem=1,
                mib=8,
                moved=6 << 20,
            )
            tail["send"] = part(tail["kv"], [], bits, kv_plan, 3, small=tail["small"])
            tail["k3"] = swaps(tail["send"], kv_orders, 3)
            tail["q3_high"] = swaps(after(qo_send[1], tail["q3"], now), qo_orders, 3)
            return [tail["send"], tail["q3"]]
        if stage == 2:
            big["final"] = local_call(
                final_ffn_kernel,
                "final_ffn",
                [shape((width // 16, inner), F32), shape((inner, width // 16), F32)],
                [*rest, *got1, *after(big["got0"], now)],
                mib=8,
                moved=4 << 20,
            )
            return [tail["k3"], tail["q3_high"], big["final"]]
        small = dict(small=tail["small"])
        if stage == 3:
            tail["k2"] = swaps(part(tail["kv"], [(after(tail["k3"], now), 0)], bits, kv_plan, 2, **small), kv_orders, 2)
            tail["q2"] = swaps(part(qo_grads, [(after(tail["q3_high"], now), 4)], bits, qo_plan, 2), qo_orders, 2)
            return [tail["k2"], tail["q2"]]
        if stage == 4:
            gots = [(tail["k3"], 0), (after(tail["k2"], now), 0)]
            tail["k1"] = swaps(part(tail["kv"], gots, bits, kv_plan, 1, **small), kv_orders, 1)
            gots = [(tail["q3"], 0), (after(tail["q2"], now), 0)]
            tail["q1"] = swaps(part(qo_grads, gots, bits, qo_plan, 1), qo_orders, 1)
            return [tail["k1"], tail["q1"]]
        gots = [(tail["k3"], 0), (tail["k2"], 0), (after(tail["k1"], now), 0)]
        tail["k0"] = swaps(part(tail["kv"], gots, bits, kv_plan, 0, **small), kv_orders, 0)
        gots = [(tail["q3"], 0), (tail["q2"], 0), (after(tail["q1"], now), 0)]
        tail["q0"] = swaps(part(qo_grads, gots, bits, qo_plan, 0), qo_orders, 0)
        return [tail["k0"], tail["q0"]]

    (grad_norm1,), _, _ = reduce_tp([lambda v: nt(v, qkv_full)], [grad_qkv], bits, beside_fg)
    x_scaled, x_spread = norm_stats(x_shard)
    grad_x = grad_middle + norm_back(grad_norm1, gain1, x_scaled, x_spread)
    mlp_total = mlp_kept + tail["mlp"].astype(F32)
    layer_shard = (middle + (mlp_total + con_bias)).astype(BF)
    (own, last), _ = gather_tp(jnp.stack([grad_x.astype(BF), layer_shard]), bits, beside_fg, whole=False)
    input_grad, layer_output = local_call(
        final_rows_kernel,
        "final_rows",
        [shape((length, width), F32), shape((length, width))],
        [bits["core"], own, last],
        in_smem=1,
        mib=8,
        moved=10 << 20,
    )
    gots = [(tail[k], 0) for k in ("k3", "k2", "k1", "k0")]
    k_grad, v_grad, small = part(tail["kv"], gots, bits, kv_plan, -1, small=tail["small"])
    biases, q_bias_grad = small[6:7], small[7:8]
    for kind in ("C", "Z1", "Z3"):
        small = small + swap(small, kind)
    gots = [(tail[k], 0) for k in ("q3", "q2", "q1", "q0")]
    q_grad, o_grad = local_call(
        final_qo_kernel,
        "final_qo",
        [shape((width // 16, hidden), F32), shape((hidden, width // 16), F32)],
        [bits["me"], *qo_grads, *[g for got, _ in gots for g in got]],
        in_smem=1,
        mib=6,
        moved=1 << 20,
    )
    expand_grad, contract_grad = big["final"]

    return (
        layer_output[None],
        input_grad[None],
        small[0],
        small[1],
        q_grad,
        q_bias_grad[:, :nb],
        k_grad[0],
        v_grad[0],
        biases[:, :nb],
        o_grad,
        small[2],
        small[3],
        small[4],
        expand_grad,
        biases[:, nb : nb + ne],
        contract_grad,
        small[5],
    )


def solution(mesh):
    both = ("fsdp", "ctx")
    rows, cols, vec = P(both, "tp"), P("tp", both), P(both)
    act = P("fsdp", "ctx", None)
    return jax.shard_map(
        body,
        mesh=mesh,
        in_specs=(
            act, P("fsdp", None), vec, vec, rows, cols, rows, rows, cols, cols, vec, vec, vec,
            rows, cols, cols, vec, act,
        ),
        out_specs=(
            act, act, vec, vec, rows, cols, rows, rows, cols, cols, vec, vec, vec, rows, cols, cols, vec,
        ),
        check_vma=False,
    )
```

```python
import math

import jax
import jax.numpy as jnp
from jax import lax
from jax.experimental import pallas as pl
from jax.experimental.pallas import tpu as pltpu
from jax.sharding import PartitionSpec as P

HEAD_DIM = 128
BF = jnp.bfloat16
F32 = jnp.float32
XY = ("fsdp", "ctx")
NEG = -1e30
SCALE = 1.0 / math.sqrt(HEAD_DIM)
SCALE2 = SCALE / math.log(2.0)


def lin(x, y):
    return (y // 2) * 8 + x * 2 + y % 2


def pairs_xy(move):
    out = []
    for x in range(4):
        for y in range(4):
            to = move(x, y)
            if to is not None:
                out.append((lin(x, y), lin(*to)))
    return out


PERM = {
    "X1": pairs_xy(lambda x, y: (x ^ 1, y)),
    "X3": pairs_xy(lambda x, y: (x ^ 3, y)),
    "Y1": pairs_xy(lambda x, y: (x, y ^ 1)),
    "Y3": pairs_xy(lambda x, y: (x, y ^ 3)),
    "C": [(t, t ^ 1) for t in range(8)],
    "Z1": [(t, t ^ 2) for t in range(8)],
    "Z3": [(t, t ^ 6) for t in range(8)],
}
VEC = {"X1": (1, 0), "X3": (3, 0), "Y1": (0, 1), "Y3": (0, 3)}
ORDER_A = ("X1", "Y1", "X3", "Y3")
ORDER_B = ("Y1", "X3", "Y3", "X1")
ORDER_C = ("X3", "Y3", "X1", "Y1")
ORDER_D = ("Y3", "X1", "Y1", "X3")
ORDER_E = ("X1", "X3", "Y1", "Y3")
ORDER_F = ("X3", "X1", "Y3", "Y1")
ORDER_P = ("X1", "X3", "Y3", "Y1")
ORDER_Q = ("X1", "X3", "Y1", "Y3")
ORDER_R = ("Y1", "Y3", "X3", "X1")
ORDER_S = ("Y1", "Y3", "X1", "X3")


def swap(value, kind):
    return lax.ppermute(value, XY if kind in VEC else "tp", PERM[kind])


def offsets(order):
    out = []
    for p in range(16):
        x = y = 0
        for k, kind in enumerate(order):
            if (p >> k) & 1:
                x ^= VEC[kind][0]
                y ^= VEC[kind][1]
        out.append(lin(x, y))
    return out


def own_bits(length):
    c = lax.axis_index("ctx").astype(jnp.int32)
    t = lax.axis_index("tp").astype(jnp.int32)
    z1, z0, k = t >> 2, (t >> 1) & 1, t & 1
    near, far = z0 ^ z1, z1
    base = k * 256
    return lax.optimization_barrier(
        {
            "Z1": near == 1,
            "Z3": far == 1,
            "C": k == 1,
            "me": (lax.axis_index("fsdp").astype(jnp.int32) * 8 + c)[None],
            "core": k[None],
            "send": (1 - k) * 256,
            "keep": base,
            "one": base + near * 64 + far * 32,
            "two": base + 128 + far * 64 + near * 32,
            "place": c * length,
        }
    )


def rows_from(value, start, size):
    starts = (start,) + (jnp.int32(0),) * (value.ndim - 1)
    return lax.dynamic_slice(value, starts, (size,) + value.shape[1:], allow_negative_indices=False)


def pick(bit, if_zero, if_one):
    return jnp.where(bit, if_one, if_zero)


def merge(bit, own, got):
    return jnp.concatenate([pick(bit, own, got), pick(bit, got, own)], axis=0)


VMEM = pl.BlockSpec(memory_space=pltpu.VMEM)
SMEM = pl.BlockSpec(memory_space=pltpu.SMEM)


def local_call(kernel, name, out_shape, args, in_smem=0, mib=20, scratch=(), flops=0, moved=0, exps=0):
    return pl.pallas_call(
        kernel,
        out_shape=out_shape,
        in_specs=[SMEM] * in_smem + [VMEM] * (len(args) - in_smem),
        out_specs=jax.tree.map(lambda _: VMEM, out_shape),
        scratch_shapes=list(scratch),
        compiler_params=pltpu.CompilerParams(vmem_limit_bytes=mib << 20),
        cost_estimate=pl.CostEstimate(flops=flops, bytes_accessed=moved, transcendentals=exps),
        name=name,
    )(*args)


def fetch_call(kernel, name, out_shape, args, scratch=(), moved=0):
    args = [pltpu.with_memory_space_constraint(v, pltpu.HBM) for v in args]

    def whole(v):
        return pl.BlockSpec(v.shape, lambda i: (0,) * len(v.shape))

    return pl.pallas_call(
        kernel,
        grid=(1,),
        out_shape=out_shape,
        in_specs=[whole(v) for v in args],
        out_specs=jax.tree.map(whole, out_shape),
        scratch_shapes=list(scratch),
        compiler_params=pltpu.CompilerParams(vmem_limit_bytes=12 << 20),
        cost_estimate=pl.CostEstimate(flops=0, bytes_accessed=moved, transcendentals=0),
        name=name,
    )(*args)


def shape(dims, dtype=BF):
    return jax.ShapeDtypeStruct(dims, dtype)


def after(value, *events):
    return lax.optimization_barrier((value, events))[0]


def pack_kernel(key_ref, value_ref, query_ref, output_ref, *refs):
    vectors, outs, rows_ref = refs[:9], refs[9:13], refs[13]
    rows_ref[...] = jnp.zeros(rows_ref.shape, F32)
    for i, v in enumerate(vectors):
        rows_ref[i : i + 1, : v.shape[1]] = v[...]
    rows, width = key_ref.shape
    outs[0][:rows] = key_ref[...].astype(BF)
    outs[0][rows:, :128] = rows_ref[...].astype(BF)
    outs[0][rows:, 128:] = jnp.zeros((16, width - 128), BF)
    outs[1][...] = value_ref[...].astype(BF)
    outs[2][...] = query_ref[...].astype(BF)
    outs[3][...] = output_ref[...].T.astype(BF)


def pack_ffn_kernel(expand_ref, contract_ref, *outs):
    half = expand_ref.shape[1] // 2
    for i in range(2):
        outs[i][...] = expand_ref[:, i * half : (i + 1) * half].astype(BF)
        outs[2 + i][...] = contract_ref[i * half : (i + 1) * half].T.astype(BF)


def join_kernel(count, *refs):
    for own, got, out in zip(refs[:count], refs[count : 2 * count], refs[2 * count :]):
        n = own.shape[0]
        out[:n] = own[...]
        out[n:] = got[...]


def join(owns, gots):
    shapes = [shape((2 * v.shape[0],) + v.shape[1:]) for v in owns]
    size = sum(v.size for v in owns)
    count = len(owns)
    return local_call(lambda *r: join_kernel(count, *r), "join", shapes, [*owns, *gots], mib=4, moved=8 * size)


def swaps(bufs, orders, k):
    return [swap(b, o[k]) for b, o in zip(bufs, orders)]


def place_kernel(rows, plan, count, small, me_ref, *refs):
    owns, gots, outs = refs[:count], refs[count : 2 * count], refs[2 * count :]
    me = me_ref[0]
    if small:
        vec_ref, query_ref, expand_ref = outs[-3:]
        query_ref[...] = jnp.zeros(query_ref.shape, F32)
        expand_ref[...] = jnp.zeros(expand_ref.shape, F32)
    for s, (order, target, column) in enumerate(plan):
        width = owns[s].shape[2]
        away = offsets(order)
        for p in range(16):
            src = owns[s] if p < 8 else gots[s]
            block = me ^ away[p]
            row = pl.multiple_of(block * rows, rows)
            outs[target][pl.ds(row, rows), column : column + width] = src[p % 8, :rows]
            if small and s == 0:
                more = src[p % 8, rows:, :128].astype(F32)
                vec_ref[:, pl.ds(pl.multiple_of(block * 128, 128), 128)] = more[:8]
                cols = pl.ds(pl.multiple_of((block // 8) * 128, 128), 128)
                query_ref[:, cols] = query_ref[:, cols] + pltpu.roll(more[:8], (block % 8) * 16, 1)[6:7]
                cols = pl.ds(pl.multiple_of((block // 2) * 128, 128), 128)
                expand_ref[:, cols] = expand_ref[:, cols] + pltpu.roll(more[8:], (block % 2) * 64, 1)[0:1]


def place(owns, gots, bits, rows, plan, widths, small=()):
    shapes = [shape((16 * rows, w)) for w in widths]
    if small:
        shapes += [shape((8, 2048), F32)] + [shape((1, w), F32) for w in small]
    count = len(owns)
    return local_call(
        lambda *r: place_kernel(rows, plan, count, bool(small), *r),
        "place",
        shapes,
        [bits["me"], *owns, *gots],
        in_smem=1,
        mib=6,
        moved=64 * rows * sum(widths),
    )


def part(grads, gots, bits, plan, step, half=None, small=None):
    rows = grads[0].shape[0] // 16
    low, count = (1 << step, 1 << step) if step >= 0 else (0, 1)
    if half is not None:
        count //= 2
        low += half * count
    n, ng = len(plan), len(grads)
    extra = 16 if small is not None and step >= 0 else 0
    shapes = [shape((count, rows + (extra if s == 0 else 0), p[3]), BF if step >= 0 else F32) for s, p in enumerate(plan)]
    if small is not None and step < 0:
        shapes.append(shape((8, 128), F32))

    def kernel(me_ref, *refs):
        me = me_ref[0]
        first = ng + n * len(gots)
        outs = refs[first + (small is not None) :]
        for s, (order, source, column, width) in enumerate(plan):
            away = offsets(order)
            for q in range(count):
                p = low + q
                row = pl.multiple_of((me ^ away[p]) * rows, rows)
                piece = refs[source][pl.ds(row, rows), column : column + width]
                if gots:
                    piece = piece.astype(F32)
                    for j, (_, base) in enumerate(gots):
                        piece = piece + refs[ng + n * j + s][p - base, :rows].astype(F32)
                outs[s][q, :rows] = piece.astype(outs[s].dtype)
                if small is not None and s == 0:
                    lane = pl.multiple_of((me ^ away[p]) * 128, 128)
                    vectors = jnp.concatenate([refs[first][:, pl.ds(lane, 128)], jnp.zeros((8, 128), F32)], axis=0)
                    for j, (_, base) in enumerate(gots):
                        vectors = vectors + refs[ng + n * j][p - base, rows:, :128].astype(F32)
                    if step >= 0:
                        outs[0][q, rows:, :128] = vectors.astype(BF)
                        outs[0][q, rows:, 128:] = jnp.zeros((16, width - 128), BF)
                    else:
                        outs[-1][...] = vectors[:8]

    args = [bits["me"], *grads, *[g for got, _ in gots for g in got]] + ([small] if small is not None else [])
    moved = 2 * count * rows * sum(p[3] for p in plan) * (2 + len(gots))
    return local_call(kernel, "part", shapes, args, in_smem=1, mib=6, moved=moved)


BIG = ((ORDER_P, ORDER_Q), (ORDER_R, ORDER_S))


def big_part(grads, gots, bits, step):
    rows, width = grads[0].shape[0] // 16, grads[0].shape[1]
    half = width // 2
    count = 1 << step
    in_specs, args, spans, outs = [], [], [], []
    per = 1 + len(gots)
    for low in (count, 0) if step == 1 else (count,):
        for m, pair in enumerate(BIG):
            for s, order in enumerate(pair):
                near = [offsets(order)[1 << k] for k in range(4)]

                def block_at(q, me, near=near, low=low, s=s):
                    p = low + q
                    where = me[0]
                    for k, away in enumerate(near):
                        where = where ^ (((p >> k) & 1) * away)
                    return (where, s)

                in_specs.append(pl.BlockSpec((rows, half), block_at))
                args.append(grads[m])
                for got in gots:
                    in_specs.append(pl.BlockSpec((1, rows, half), lambda q, me, low=low: (low + q, 0, 0)))
                    args.append(got[2 * m + s])
                if step > 1:
                    outs.append(shape((count, rows, half)))
                    spans.append((len(outs) - 1, 0))
                elif s == 0:
                    outs.append(shape((count, rows, width), BF if low else F32))
                    spans.append((len(outs) - 1, 0))
                else:
                    spans.append((len(outs) - 1, half))

    def kernel(me_ref, *refs):
        out_refs = refs[len(args) :]
        for i, (at, column) in enumerate(spans):
            piece = refs[per * i][...]
            if gots:
                piece = piece.astype(F32)
                for j in range(1, per):
                    piece = piece + refs[per * i + j][0].astype(F32)
            out_refs[at][0, :, column : column + half] = piece.astype(outs[at].dtype)

    return pl.pallas_call(
        kernel,
        grid_spec=pltpu.PrefetchScalarGridSpec(
            num_scalar_prefetch=1,
            grid=(count,),
            in_specs=in_specs,
            out_specs=[pl.BlockSpec((1,) + o.shape[1:], lambda q, me: (q, 0, 0)) for o in outs],
        ),
        out_shape=outs,
        compiler_params=pltpu.CompilerParams(vmem_limit_bytes=12 << 20),
        cost_estimate=pl.CostEstimate(flops=0, bytes_accessed=4 * count * rows * width * (1 + per), transcendentals=0),
        name="big_part",
    )(bits["me"], *args)


def big_swaps(values, step):
    if step >= 2:
        return [swap(v, o[step]) for v, o in zip(values, BIG[0] + BIG[1])]
    return [swap(v, pair[0][step]) for v, pair in zip(values, BIG)]


def shard_rows(value, bits):
    return jnp.concatenate([rows_from(value, bits["one"], 32), rows_from(value, bits["two"], 32)], axis=0)


def halves(value, bits):
    return rows_from(value, bits["send"], 256), rows_from(value, bits["keep"], 256)


def reduce_tp(products, operands, bits, beside=None):
    count = len(products)
    pairs = [halves(v, bits) for v in operands]
    send = jnp.concatenate([p(v[0]).astype(BF) for p, v in zip(products, pairs)], axis=0)
    first = swap(send, "C")
    kept = [p(v[1]) for p, v in zip(products, pairs)]
    events = [send]
    if beside:
        first = after(first, beside(0, events, kept))
    totals = [v + first[i * 256 : (i + 1) * 256].astype(F32) for i, v in enumerate(kept)]
    events.append(first)
    streams = [[v[:128] for v in totals], [v[128:] for v in totals]]
    for stage, kinds in enumerate((("Z1", "Z3"), ("Z3", "Z1"))):
        n = streams[0][0].shape[0] // 2
        give = [
            jnp.concatenate([pick(bits[t], v[n:], v[:n]).astype(BF) for v in parts], axis=0)
            for t, parts in zip(kinds, streams)
        ]
        got = [swap(v, t) for v, t in zip(give, kinds)]
        if beside:
            got = after(got, beside(1 + stage, events, kept))
        events.append(got)
        streams = [
            [pick(bits[t], v[:n], v[n:]) + g[i * n : (i + 1) * n].astype(F32) for i, v in enumerate(parts)]
            for t, parts, g in zip(kinds, streams, got)
        ]
    out = [jnp.concatenate([streams[0][i], streams[1][i]], axis=0) for i in range(count)]
    return out, events, kept


def merge_rows(bit, own, got):
    return jnp.concatenate([pick(bit, own, got), pick(bit, got, own)], axis=1)


def gather_tp(shards, bits, beside=None, whole=True):
    parts = [shards[:, :32], shards[:, 32:]]
    events = [shards]
    for stage, kinds in enumerate((("Z3", "Z1"), ("Z1", "Z3"))):
        got = [swap(v, t) for v, t in zip(parts, kinds)]
        if beside:
            got = after(got, beside(3 + stage, events, None))
        events.append(got)
        parts = [merge_rows(bits[t], v, g) for t, v, g in zip(kinds, parts, got)]
    own = jnp.concatenate(parts, axis=1)
    last = swap(own, "C")
    if beside:
        last = after(last, beside(5, events, None))
    events.append(last)
    return (merge_rows(bits["C"], own, last) if whole else (own, last)), events


Y_FLIP = PERM["Y1"]
Y_FLIP_DOWN = pairs_xy(lambda x, y: (x, y ^ 1) if y % 2 == 1 else None)
Y_FLIP_UP = pairs_xy(lambda x, y: (x, y ^ 1) if y % 2 == 0 else None)
X_UP = pairs_xy(lambda x, y: (x + 1, y) if x < 3 else None)
X_UP2 = pairs_xy(lambda x, y: (x + 2, y) if x < 2 else None)
X_DOWN = pairs_xy(lambda x, y: (x - 1, y) if x > 0 else None)
X_DOWN2 = pairs_xy(lambda x, y: (x - 2, y) if x > 1 else None)
SLOTS = 6


def slot_block(slot, c):
    back = slot // 2 * 2
    return c - back if slot % 2 == 0 else (c ^ 1) - back


def slot_needed(slot, c, length, first_ref):
    block = slot_block(slot, c)
    return (block >= 0) & (block < c) & (block * length + length - 1 >= first_ref[0])


def nt(a, b):
    return lax.dot_general(a, b, (((1,), (1,)), ((), ())), preferred_element_type=F32)


def tn(a, b):
    return lax.dot_general(a, b, (((0,), (0,)), ((), ())), preferred_element_type=F32)


def nn(a, b):
    return jnp.dot(a, b, preferred_element_type=F32)


def visible(slot, block, length, start_ref, c):
    keys = lax.broadcasted_iota(jnp.int32, (length, length), 0) + block * length
    mask = keys >= start_ref[...]
    if slot == 0:
        mask = mask & (keys <= lax.broadcasted_iota(jnp.int32, (length, length), 1) + c * length)
    return mask


def attn_fwd_kernel(heads, me_ref, first_ref, start_ref, q_ref, *refs):
    kv = refs[:SLOTS]
    att_ref, mix_ref, lse_ref, m_ref, l_ref = refs[SLOTS:]
    length = q_ref.shape[0]
    hidden = heads * HEAD_DIM
    c = me_ref[0] % 8
    for slot in range(SLOTS):
        block = slot_block(slot, c)

        def run(slot=slot, block=block):
            mask = visible(slot, block, length, start_ref, c)
            for h in range(heads):
                cols = slice(h * HEAD_DIM, (h + 1) * HEAD_DIM)
                key = kv[slot][:, cols]
                val = kv[slot][:, hidden + h * HEAD_DIM : hidden + (h + 1) * HEAD_DIM]
                s = jnp.where(mask, nt(key, q_ref[:, cols]), NEG)
                top = jnp.max(s, axis=0, keepdims=True)
                if slot == 0:
                    p = jnp.exp2((s - top) * SCALE2)
                    m_ref[h : h + 1] = top
                    l_ref[h : h + 1] = jnp.sum(p, axis=0, keepdims=True)
                    mix_ref[cols] = tn(val, p.astype(BF))
                else:
                    old = m_ref[h : h + 1]
                    new = jnp.maximum(old, top)
                    p = jnp.exp2((s - new) * SCALE2)
                    shrink = jnp.exp2((old - new) * SCALE2)
                    m_ref[h : h + 1] = new
                    l_ref[h : h + 1] = l_ref[h : h + 1] * shrink + jnp.sum(p, axis=0, keepdims=True)
                    mix_ref[cols] = mix_ref[cols] * shrink + tn(val, p.astype(BF))

        if slot == 0:
            run()
        else:
            pl.when(slot_needed(slot, c, length, first_ref))(run)
    for h in range(heads):
        cols = slice(h * HEAD_DIM, (h + 1) * HEAD_DIM)
        out = mix_ref[cols] / l_ref[h : h + 1]
        mix_ref[cols] = out
        att_ref[:, cols] = out.T.astype(BF)
        lse_ref[h : h + 1] = m_ref[h : h + 1] * SCALE2 + jnp.log2(l_ref[h : h + 1])


def attn_bwd_kernel(heads, me_ref, first_ref, start_ref, q_ref, do_ref, mix_ref, lse_ref, *refs):
    kv = refs[:SLOTS]
    dq_ref, dkv = refs[SLOTS], refs[SLOTS + 1 : 2 * SLOTS + 1]
    dqt_ref, delta_ref = refs[2 * SLOTS + 1 :]
    length = q_ref.shape[0]
    hidden = heads * HEAD_DIM
    c = me_ref[0] % 8
    for h in range(heads):
        cols = slice(h * HEAD_DIM, (h + 1) * HEAD_DIM)
        dot_t = do_ref[:, cols].astype(F32).T
        delta_ref[h : h + 1] = jnp.sum(dot_t * mix_ref[cols], axis=0, keepdims=True)
    for slot in range(SLOTS):
        block = slot_block(slot, c)

        def run(slot=slot, block=block):
            mask = visible(slot, block, length, start_ref, c)
            for h in range(heads):
                cols = slice(h * HEAD_DIM, (h + 1) * HEAD_DIM)
                vcols = slice(hidden + h * HEAD_DIM, hidden + (h + 1) * HEAD_DIM)
                key, val = kv[slot][:, cols], kv[slot][:, vcols]
                q, do = q_ref[:, cols], do_ref[:, cols]
                s = jnp.where(mask, nt(key, q), NEG)
                p = jnp.exp2(s * SCALE2 - lse_ref[h : h + 1])
                ds = (p * (nt(val, do) - delta_ref[h : h + 1])).astype(BF)
                dkv[slot][:, cols] = (nn(ds, q) * SCALE).astype(dkv[slot].dtype)
                dkv[slot][:, vcols] = nn(p.astype(BF), do).astype(dkv[slot].dtype)
                part = tn(key, ds)
                if slot == 0:
                    dqt_ref[cols] = part
                else:
                    dqt_ref[cols] = dqt_ref[cols] + part

        if slot == 0:
            run()
        else:
            pl.when(slot_needed(slot, c, length, first_ref))(run)

            @pl.when(jnp.logical_not(slot_needed(slot, c, length, first_ref)))
            def _(slot=slot):
                dkv[slot][...] = jnp.zeros(dkv[slot].shape, dkv[slot].dtype)

    for h in range(heads):
        cols = slice(h * HEAD_DIM, (h + 1) * HEAD_DIM)
        dq_ref[:, cols] = (dqt_ref[cols] * SCALE).T.astype(BF)


def stats_kernel(x_ref, mean_ref, spread_ref):
    for r in range(0, x_ref.shape[0], 64):
        v = x_ref[r : r + 64].astype(F32)
        mean = jnp.mean(v, axis=-1, keepdims=True)
        centre = v - mean
        spread = lax.rsqrt(jnp.mean(centre * centre, axis=-1, keepdims=True) + 1e-05)
        mean_ref[r : r + 64] = jnp.broadcast_to(mean, (64, 128))
        spread_ref[r : r + 64] = jnp.broadcast_to(spread, (64, 128))


def norm_kv_kernel(me_ref, x_ref, mean_ref, spread_ref, k_own, v_own, k_got, v_got, normed_ref, kv_ref, acc_ref):
    me = me_ref[0]
    hidden = k_own.shape[2]
    zero = jnp.zeros((1, 128), F32)
    bias = [zero, zero]
    away_k, away_v = offsets(ORDER_A), offsets(ORDER_B)
    for q in range(8):
        parts = []
        for src, p in ((k_own, q), (k_got, q + 8)):
            block = me ^ away_k[p]
            cols = pl.ds(pl.multiple_of(block * 128, 128), 128)
            small = src[q, 128:144, :128].astype(F32)
            scaled = (x_ref[:, cols].astype(F32) - mean_ref[...]) * spread_ref[...]
            part = (scaled * small[0:1] + small[1:2]).astype(BF)
            normed_ref[:, cols] = part
            parts.append(part)
            turned = pltpu.roll(small[:8], (block % 8) * 16, 1)[7:8]
            bias = [bias[0] + jnp.where(block < 8, turned, zero), bias[1] + jnp.where(block < 8, zero, turned)]
        weights = jnp.concatenate([k_own[q, :128], k_got[q, :128]], axis=0)
        term = jnp.dot(jnp.concatenate(parts, axis=1), weights, preferred_element_type=F32)
        acc_ref[...] = term if q == 0 else acc_ref[...] + term
    kv_ref[:, :hidden] = acc_ref[...].astype(BF)
    for q in range(8):
        parts = []
        for p in (q, q + 8):
            parts.append(normed_ref[:, pl.ds(pl.multiple_of((me ^ away_v[p]) * 128, 128), 128)])
        weights = jnp.concatenate([v_own[q], v_got[q]], axis=0)
        term = jnp.dot(jnp.concatenate(parts, axis=1), weights, preferred_element_type=F32)
        acc_ref[...] = term if q == 0 else acc_ref[...] + term
    kv_ref[:, hidden:] = (acc_ref[...] + jnp.concatenate(bias, axis=1)).astype(BF)


def early_kernel(att_ref, query_ref, pre_ref, attn_ref, norm_ref, scaled_ref, cot_ref, out_ref):
    def total(v):
        return jnp.sum(v.astype(F32), axis=0, keepdims=True)

    out_ref[0:2] = jnp.zeros((2, out_ref.shape[1]), F32)
    out_ref[2:3] = total(attn_ref[...])
    out_ref[3:4] = total(norm_ref[...] * scaled_ref[...])
    out_ref[4:5] = total(norm_ref[...])
    out_ref[5:6] = total(cot_ref[...])
    value, query, expand = total(att_ref[...]), total(query_ref[...]), total(pre_ref[...])
    lane = lax.broadcasted_iota(jnp.int32, (8, 128), 1)

    def taken(row, size, block, to):
        at = block * size
        wide = jnp.broadcast_to(row[:, at // 128 * 128 : at // 128 * 128 + 128], (8, 128))
        wide = pltpu.roll(wide, (128 - at % 128 + to) % 128, 1)
        return jnp.where((lane >= to) & (lane < to + size), wide, 0.0)[0:1]

    nb, ne = value.shape[1] // 16, expand.shape[1] // 16
    for block in range(16):
        cols = slice(block * 128, block * 128 + 128)
        out_ref[6:7, cols] = taken(value, nb, block, 0) + taken(expand, ne, block, nb)
        out_ref[7:8, cols] = taken(query, nb, block, 0)


def late_kernel(core_ref, x_ref, mean_ref, spread_ref, gone_ref, kept_ref, early_ref, out_ref):
    core = core_ref[0]
    size = gone_ref.shape[0]
    out_ref[...] = early_ref[...]
    first = jnp.zeros((1, x_ref.shape[1]), F32)
    second = first
    for src, base in ((gone_ref, (1 - core) * size), (kept_ref, core * size)):
        for r in range(0, size, 32):
            rows = pl.ds(pl.multiple_of(base + r, 32), 32)
            scaled = (x_ref[rows].astype(F32) - mean_ref[rows][:, :1]) * spread_ref[rows][:, :1]
            grad = src[r : r + 32].astype(F32)
            first = first + jnp.sum(grad * scaled, axis=0, keepdims=True)
            second = second + jnp.sum(grad, axis=0, keepdims=True)
    out_ref[0:1] = first
    out_ref[1:2] = second


def final_ffn_kernel(*refs):
    kept, one, zero, outs = refs[:2], refs[2:4], refs[4:6], refs[6:]
    total = [k[0] + a[0].astype(F32) + b[0].astype(F32) for k, a, b in zip(kept, one, zero)]
    outs[0][...] = total[0]
    for j in range(0, total[1].shape[1], 128):
        outs[1][j : j + 128] = total[1][:, j : j + 128].T


def final_rows_kernel(core_ref, own_ref, last_ref, grad_ref, out_ref):
    size = own_ref.shape[1]
    core = core_ref[0]
    for src, base in ((own_ref, core * size), (last_ref, (1 - core) * size)):
        for r in range(0, size, 64):
            rows = pl.ds(pl.multiple_of(base + r, 64), 64)
            grad_ref[rows] = src[0, r : r + 64].astype(F32)
            out_ref[rows] = src[1, r : r + 64]


def final_qo_kernel(me_ref, grad_ref, *refs):
    gots, outs = refs[:-2], refs[-2:]
    piece = grad_ref[pl.ds(pl.multiple_of(me_ref[0] * 128, 128), 128)].astype(F32)
    for got in gots:
        piece = piece + got[0].astype(F32)
    half = piece.shape[1] // 2
    outs[0][...] = piece[:, :half]
    outs[1][...] = piece[:, half:].T


def norm_stats(v):
    mean = jnp.mean(v, axis=-1, keepdims=True)
    centre = v - mean
    spread = lax.rsqrt(jnp.mean(centre * centre, axis=-1, keepdims=True) + 1e-05)
    return centre * spread, spread


def norm_back(grad, gain, scaled, spread):
    weighted = grad * gain
    inner = jnp.mean(weighted, axis=-1, keepdims=True)
    cross = jnp.mean(weighted * scaled, axis=-1, keepdims=True)
    return spread * (weighted - inner - scaled * cross)


def cols_of(w, n=4):
    k = w.shape[1] // n
    return [w[:, i * k : (i + 1) * k] for i in range(n)]


def body(
    layer_input,
    doc_ids,
    pre_gain,
    pre_shift,
    query_weight,
    query_bias,
    key_weight,
    value_weight,
    value_bias,
    output_weight,
    output_bias,
    mid_gain,
    mid_shift,
    expand_weight,
    expand_bias,
    contract_weight,
    contract_bias,
    cotangent,
):
    bits = own_bits(layer_input.shape[1])
    x = layer_input[0]
    cot = cotangent[0]
    length, width = x.shape
    hidden = query_weight.shape[1]
    heads = hidden // HEAD_DIM
    inner = expand_weight.shape[1]

    nb, ne = query_bias.shape[1], expand_bias.shape[1]
    pre_gain = after(pre_gain, bits)
    vectors = [pre_gain, pre_shift, output_bias, mid_gain, mid_shift, contract_bias]
    weights = [key_weight, value_weight, query_weight, output_weight]
    packed = shape((128, hidden))
    bufs = fetch_call(
        pack_kernel,
        "pack",
        [shape((144, hidden)), packed, packed, packed],
        [*weights, *[v[None] for v in vectors], query_bias, value_bias, expand_bias],
        scratch=[pltpu.VMEM((16, 128), F32)],
        moved=800 << 10,
    )
    bufs = [v[None] for v in bufs]
    first_orders, big_orders = (ORDER_A, ORDER_B, ORDER_C, ORDER_D), (ORDER_E, ORDER_F)
    kv_orders, qo_orders = (ORDER_A, ORDER_B), (ORDER_D,)
    half_shape = shape((128, inner // 2))
    ffn = fetch_call(
        pack_ffn_kernel, "pack_ffn", [half_shape] * 4, [expand_weight, contract_weight], moved=1536 << 10
    )
    con = [v[None] for v in ffn[2:]]
    bufs = join(bufs, swaps(bufs, first_orders, 0))
    got = swaps(bufs, first_orders, 1)
    stats = [shape((length, 128), F32)] * 2
    mean1, spread1 = local_call(stats_kernel, "stats", stats, [after(x, bufs)], mib=8, moved=3 << 20)
    one = swaps(con[:1], big_orders[:1], 0)
    bufs = join(bufs, after(got, one, mean1))
    got = swaps(bufs, first_orders, 2)
    two = swaps(con[1:], big_orders[1:], 0)
    bufs = join(bufs, after(got, two))
    con = join(con, one + two)
    got = swaps(bufs, first_orders, 3)
    got_con = swaps(after(con, got), big_orders, 1)
    exp_orders = (ORDER_A, ORDER_B)
    exp = [v[None] for v in ffn[:2]]
    got_exp = swaps(after(exp, got), exp_orders, 0)

    docs = doc_ids[0]
    own_docs = rows_from(docs, bits["place"], length)
    start = jnp.sum((docs[:, None] < own_docs[None, :]).astype(jnp.int32), axis=0)
    first_key = start[:1]
    start = start[None]

    normed, kv_own = local_call(
        norm_kv_kernel,
        "norm_kv",
        [shape((length, width)), shape((length, 2 * hidden))],
        [bits["me"], x, mean1, spread1, bufs[0], bufs[1], got[0], got[1]],
        in_smem=1,
        mib=10,
        scratch=[pltpu.VMEM((length, hidden), F32)],
        flops=2 * length * width * 2 * hidden,
        moved=6 << 20,
    )
    kv_own = after(kv_own, got_con, got_exp)
    kv_e1 = lax.ppermute(kv_own, XY, Y_FLIP)
    kv_f1 = lax.ppermute(kv_own, XY, X_UP)
    kv_f2 = lax.ppermute(kv_own, XY, X_UP2)
    con = join(con, got_con)
    exp = join(exp, got_exp)
    got_con = swaps(con, big_orders, 2)
    kv_e1 = after(kv_e1, exp, con, kv_f1)
    plan = [(ORDER_A, 0, 0), (ORDER_B, 0, hidden), (ORDER_C, 1, 0), (ORDER_D, 2, 0)]
    kv_full, q_full, o_full, vec, q_bias, e_bias = place(
        after(bufs, kv_e1), got, bits, 128, plan, [2 * hidden, hidden, hidden], [hidden, inner]
    )
    gain1, out_bias, gain2, shift2, con_bias = [vec[i : i + 1] for i in (0, 2, 3, 4, 5)]
    kv_g1 = lax.ppermute(after(kv_e1, kv_f2), XY, X_UP)
    kv_e3 = lax.ppermute(kv_f2, XY, Y_FLIP_DOWN)
    queries = (nn(normed, q_full) + q_bias).astype(BF)
    con = join(con, after(got_con, kv_e1))
    got_con = swaps(con, big_orders, 3)

    slots = [kv_own, kv_e1, kv_f1, kv_g1, kv_f2, kv_e3]
    attended, mixture, lse = local_call(
        lambda *refs: attn_fwd_kernel(heads, *refs),
        "attn_fwd",
        [shape((length, hidden)), shape((hidden, length), F32), shape((heads, length), F32)],
        [bits["me"], first_key, start, after(queries, con), *slots],
        in_smem=2,
        mib=12,
        scratch=[pltpu.VMEM((heads, length), F32), pltpu.VMEM((heads, length), F32)],
        flops=10**9,
        moved=6 << 20,
        exps=3 * 10**6,
    )

    feed = {}

    def beside_a(stage, events, kept):
        now = events[-1]
        if stage == 0:
            plan = [(ORDER_E, 0, 0), (ORDER_F, 0, inner // 2)]
            feed["contract"] = place(con, got_con, bits, 128, plan, [inner])[0]
            feed["got"] = swaps(after(exp, now), exp_orders, 1)
            return [feed["contract"], feed["got"]]
        if stage == 1:
            feed["exp"] = join(exp, after(feed["got"], now))
            feed["got"] = swaps(feed["exp"], exp_orders, 2)
        if stage == 2:
            return feed["got"]
        if stage == 3:
            feed["exp"] = join(feed["exp"], after(feed["got"], now))
            feed["got"] = swaps(feed["exp"], exp_orders, 3)
        return []

    (attn_total,), _, _ = reduce_tp([lambda v: nt(v, o_full)], [attended], bits, beside_a)
    contract_full = feed["contract"]
    x_shard = shard_rows(x, bits).astype(F32)
    middle = x_shard + (attn_total + out_bias)
    scaled2, spread2 = norm_stats(middle)
    normed_two, _ = gather_tp((scaled2 * gain2 + shift2).astype(BF)[None], bits, beside_a)
    normed_two = normed_two[0]

    plan = [(ORDER_A, 0, 0), (ORDER_B, 0, inner // 2)]
    expand_full = place(feed["exp"], feed["got"], bits, 128, plan, [inner])[0]
    grad_act = nn(cot, contract_full)
    pre_act = nn(normed_two, expand_full) + e_bias
    cdf = 0.5 * (1.0 + lax.erf(pre_act * (1.0 / math.sqrt(2.0))))
    activated = (pre_act * cdf).astype(BF)
    slope = cdf + pre_act * jnp.exp(-0.5 * pre_act * pre_act) * (1.0 / math.sqrt(2.0 * math.pi))
    grad_pre = (slope * grad_act).astype(BF)
    big = {}

    def beside_de(stage, events, kept):
        if stage == 1:
            held = after((cot, activated, normed_two, grad_pre), kept)
            big["grads"] = [tn(held[2], held[3]).astype(BF), tn(held[0], held[1]).astype(BF)]
            big["send"] = big_part(big["grads"], [], bits, 3)
            return big["send"]
        if stage == 2:
            big["got3"] = big_swaps(after(big["send"], events[-1]), 3)
        if stage == 4:
            return big["got3"]
        if stage < 5:
            return []
        big["send"] = big_part(big["grads"], [after(big["got3"], events[-1])], bits, 2)
        big["got2"] = big_swaps(big["send"], 2)
        return big["send"]

    (grad_norm2,), _, _ = reduce_tp([lambda v: nt(v, expand_full)], [grad_pre], bits, beside_de)

    cot_shard = shard_rows(cot, bits).astype(F32)
    grad_middle = cot_shard + norm_back(grad_norm2, gain2, scaled2, spread2)
    grad_attn_shard = grad_middle.astype(BF)
    grad_attn, _ = gather_tp(grad_attn_shard[None], bits, beside_de)
    grad_attn = grad_attn[0]

    grad_att = nn(grad_attn, o_full).astype(BF)
    dkv = shape((length, 2 * hidden))
    grad_q, own_part, p_e1, p_f1, p_g1, p_f2, p_e3 = local_call(
        lambda *refs: attn_bwd_kernel(heads, *refs),
        "attn_bwd",
        [shape((length, hidden)), shape((length, 2 * hidden), F32)] + [dkv] * 5,
        [bits["me"], first_key, start, queries, after(grad_att, big["send"]), mixture, lse, *slots],
        in_smem=2,
        mib=16,
        scratch=[pltpu.VMEM((hidden, length), F32), pltpu.VMEM((heads, length), F32)],
        flops=2 * 10**9,
        moved=10 << 20,
        exps=3 * 10**6,
    )
    got2 = after(big["got2"], grad_q)
    both = big_part(big["grads"], [big["got3"], got2], bits, 1)
    rest = both[2:]
    from_g1 = lax.ppermute(after(p_g1, got2), XY, X_DOWN)
    from_e3 = lax.ppermute(after(p_e3, got2), XY, Y_FLIP_UP)
    got1 = big_swaps(both[:2], 1)
    mlp_send, mlp_keep = halves(after(activated, got2), bits)
    mlp_got = swap(after(nt(mlp_send, contract_full).astype(BF), got2), "C")

    grad_o = tn(grad_attn, after(attended, grad_q)).astype(BF)
    qo_grads = [jnp.concatenate([tn(normed, grad_q).astype(BF), grad_o], axis=1)]
    qo_plan = [(ORDER_D, 0, 0, 2 * hidden)]
    qo_send = part(qo_grads, [], bits, qo_plan, 3, 0), part(qo_grads, [], bits, qo_plan, 3, 1)
    from_g1 = after(from_g1, got1, qo_send)
    from_f1 = lax.ppermute(after(p_f1, from_g1), XY, X_DOWN)
    total = nt(mlp_keep, contract_full) + after(mlp_got, from_g1).astype(F32)
    one, two = total[:128], total[128:]
    two = [jnp.concatenate([two[i : i + 32], two[i + 64 : i + 96]], axis=0) for i in (0, 32)]
    give = [pick(bits["Z1"], one[64:], one[:64]), pick(bits["Z1"], two[1], two[0])]
    mlp_got = swap(jnp.concatenate(give, axis=0).astype(BF), "Z1")
    one = pick(bits["Z1"], one[:64], one[64:])
    two = pick(bits["Z1"], two[0], two[1])
    from_e1 = lax.ppermute((p_e1.astype(F32) + from_g1.astype(F32)).astype(BF), XY, Y_FLIP)
    from_f2 = lax.ppermute((p_f2.astype(F32) + from_e3.astype(F32)).astype(BF), XY, X_DOWN2)
    early = local_call(
        early_kernel,
        "early",
        shape((8, width), F32),
        [grad_att, grad_q, grad_pre, grad_attn_shard, grad_norm2, scaled2, cot_shard],
        mib=8,
        moved=4 << 20,
    )
    from_e1 = after(from_e1, early)
    send0 = [(v[1:] + g[1:].astype(F32)).astype(BF) for v, g in zip(rest, got1)]
    from_f2 = after(from_f2, send0)
    mlp_got = after(mlp_got, from_e1).astype(F32)
    one, two = one + mlp_got[:64], two + mlp_got[64:]
    give = [pick(bits["Z3"], v[32:], v[:32]).astype(BF) for v in (one, two)]
    mlp_give = jnp.concatenate(give, axis=0)
    mlp_kept = jnp.concatenate([pick(bits["Z3"], v[:32], v[32:]) for v in (one, two)], axis=0)
    from_f2 = after(from_f2, mlp_give)
    grad_kv = (own_part + from_f1.astype(F32) + from_e1.astype(F32) + from_f2.astype(F32)).astype(BF)

    qkv_full = jnp.concatenate([after(q_full, grad_q), kv_full], axis=1)
    grad_qkv = jnp.concatenate([grad_q, grad_kv], axis=1)
    tail = {}

    kv_plan = [(ORDER_A, 0, 0, hidden), (ORDER_B, 0, hidden, hidden)]

    def beside_fg(stage, events, kept):
        now = events[-1]
        if stage == 0:
            tail["q3"] = swaps(after(qo_send[0], now), qo_orders, 3)
            big["got0"] = big_swaps(after(send0, now), 0)
            tail["mlp"] = swap(after(mlp_give, now), "Z3")
            tail["kv"] = [tn(normed, after(grad_kv, now)).astype(BF)]
            return [tail["kv"], big["got0"], tail["mlp"]]
        if stage == 1:
            tail["small"] = local_call(
                late_kernel,
                "late",
                shape((8, width), F32),
                [bits["core"], x, mean1, spread1, events[0], kept[0], early],
                in_smem=1,
                mib=8,
                moved=6 << 20,
            )
            tail["send"] = part(tail["kv"], [], bits, kv_plan, 3, small=tail["small"])
            tail["k3"] = swaps(tail["send"], kv_orders, 3)
            tail["q3_high"] = swaps(after(qo_send[1], tail["q3"], now), qo_orders, 3)
            return [tail["send"], tail["q3"]]
        if stage == 2:
            big["final"] = local_call(
                final_ffn_kernel,
                "final_ffn",
                [shape((width // 16, inner), F32), shape((inner, width // 16), F32)],
                [*rest, *got1, *after(big["got0"], now)],
                mib=8,
                moved=4 << 20,
            )
            return [tail["k3"], tail["q3_high"], big["final"]]
        small = dict(small=tail["small"])
        if stage == 3:
            tail["k2"] = swaps(part(tail["kv"], [(after(tail["k3"], now), 0)], bits, kv_plan, 2, **small), kv_orders, 2)
            tail["q2"] = swaps(part(qo_grads, [(after(tail["q3_high"], now), 4)], bits, qo_plan, 2), qo_orders, 2)
            return [tail["k2"], tail["q2"]]
        if stage == 4:
            gots = [(tail["k3"], 0), (after(tail["k2"], now), 0)]
            tail["k1"] = swaps(part(tail["kv"], gots, bits, kv_plan, 1, **small), kv_orders, 1)
            gots = [(tail["q3"], 0), (after(tail["q2"], now), 0)]
            tail["q1"] = swaps(part(qo_grads, gots, bits, qo_plan, 1), qo_orders, 1)
            return [tail["k1"], tail["q1"]]
        gots = [(tail["k3"], 0), (tail["k2"], 0), (after(tail["k1"], now), 0)]
        tail["k0"] = swaps(part(tail["kv"], gots, bits, kv_plan, 0, **small), kv_orders, 0)
        gots = [(tail["q3"], 0), (tail["q2"], 0), (after(tail["q1"], now), 0)]
        tail["q0"] = swaps(part(qo_grads, gots, bits, qo_plan, 0), qo_orders, 0)
        return [tail["k0"], tail["q0"]]

    (grad_norm1,), _, _ = reduce_tp([lambda v: nt(v, qkv_full)], [grad_qkv], bits, beside_fg)
    x_scaled, x_spread = norm_stats(x_shard)
    grad_x = grad_middle + norm_back(grad_norm1, gain1, x_scaled, x_spread)
    mlp_total = mlp_kept + tail["mlp"].astype(F32)
    layer_shard = (middle + (mlp_total + con_bias)).astype(BF)
    (own, last), _ = gather_tp(jnp.stack([grad_x.astype(BF), layer_shard]), bits, beside_fg, whole=False)
    input_grad, layer_output = local_call(
        final_rows_kernel,
        "final_rows",
        [shape((length, width), F32), shape((length, width))],
        [bits["core"], own, last],
        in_smem=1,
        mib=8,
        moved=10 << 20,
    )
    gots = [(tail[k], 0) for k in ("k3", "k2", "k1", "k0")]
    k_grad, v_grad, small = part(tail["kv"], gots, bits, kv_plan, -1, small=tail["small"])
    biases, q_bias_grad = small[6:7], small[7:8]
    for kind in ("C", "Z1", "Z3"):
        small = small + swap(small, kind)
    gots = [(tail[k], 0) for k in ("q3", "q2", "q1", "q0")]
    q_grad, o_grad = local_call(
        final_qo_kernel,
        "final_qo",
        [shape((width // 16, hidden), F32), shape((hidden, width // 16), F32)],
        [bits["me"], *qo_grads, *[g for got, _ in gots for g in got]],
        in_smem=1,
        mib=6,
        moved=1 << 20,
    )
    expand_grad, contract_grad = big["final"]

    return (
        layer_output[None],
        input_grad[None],
        small[0],
        small[1],
        q_grad,
        q_bias_grad[:, :nb],
        k_grad[0],
        v_grad[0],
        biases[:, :nb],
        o_grad,
        small[2],
        small[3],
        small[4],
        expand_grad,
        biases[:, nb : nb + ne],
        contract_grad,
        small[5],
    )


def solution(mesh):
    both = ("fsdp", "ctx")
    rows, cols, vec = P(both, "tp"), P("tp", both), P(both)
    act = P("fsdp", "ctx", None)
    return jax.shard_map(
        body,
        mesh=mesh,
        in_specs=(
            act, P("fsdp", None), vec, vec, rows, cols, rows, rows, cols, cols, vec, vec, vec,
            rows, cols, cols, vec, act,
        ),
        out_specs=(
            act, act, vec, vec, rows, cols, rows, rows, cols, cols, vec, vec, vec, rows, cols, cols, vec,
        ),
        check_vma=False,
    )
```

```python
import math

import jax
import jax.numpy as jnp
from jax import lax
from jax.experimental import pallas as pl
from jax.experimental.pallas import tpu as pltpu
from jax.sharding import PartitionSpec as P

HEAD_DIM = 128
BF = jnp.bfloat16
F32 = jnp.float32
XY = ("fsdp", "ctx")
NEG = -1e30
SCALE = 1.0 / math.sqrt(HEAD_DIM)
SCALE2 = SCALE / math.log(2.0)


def lin(x, y):
    return (y // 2) * 8 + x * 2 + y % 2


def pairs_xy(move):
    out = []
    for x in range(4):
        for y in range(4):
            to = move(x, y)
            if to is not None:
                out.append((lin(x, y), lin(*to)))
    return out


PERM = {
    "X1": pairs_xy(lambda x, y: (x ^ 1, y)),
    "X3": pairs_xy(lambda x, y: (x ^ 3, y)),
    "Y1": pairs_xy(lambda x, y: (x, y ^ 1)),
    "Y3": pairs_xy(lambda x, y: (x, y ^ 3)),
    "C": [(t, t ^ 1) for t in range(8)],
    "Z1": [(t, t ^ 2) for t in range(8)],
    "Z3": [(t, t ^ 6) for t in range(8)],
}
VEC = {"X1": (1, 0), "X3": (3, 0), "Y1": (0, 1), "Y3": (0, 3)}
ORDER_A = ("X1", "Y1", "X3", "Y3")
ORDER_B = ("Y1", "X3", "Y3", "X1")
ORDER_C = ("X3", "Y3", "X1", "Y1")
ORDER_D = ("Y3", "X1", "Y1", "X3")
ORDER_E = ("X1", "X3", "Y1", "Y3")
ORDER_F = ("X3", "X1", "Y3", "Y1")
ORDER_G = ("Y1", "X1", "X3", "Y3")
ORDER_H = ("Y3", "X3", "X1", "Y1")
ORDER_P = ("X1", "X3", "Y3", "Y1")
ORDER_Q = ("X1", "X3", "Y1", "Y3")
ORDER_R = ("Y1", "Y3", "X3", "X1")
ORDER_S = ("Y1", "Y3", "X1", "X3")


def swap(value, kind):
    return lax.ppermute(value, XY if kind in VEC else "tp", PERM[kind])


def offsets(order):
    out = []
    for p in range(16):
        x = y = 0
        for k, kind in enumerate(order):
            if (p >> k) & 1:
                x ^= VEC[kind][0]
                y ^= VEC[kind][1]
        out.append(lin(x, y))
    return out


def own_bits(length):
    c = lax.axis_index("ctx").astype(jnp.int32)
    t = lax.axis_index("tp").astype(jnp.int32)
    z1, z0, k = t >> 2, (t >> 1) & 1, t & 1
    near, far = z0 ^ z1, z1
    base = k * 256
    return lax.optimization_barrier(
        {
            "Z1": near == 1,
            "Z3": far == 1,
            "C": k == 1,
            "me": (lax.axis_index("fsdp").astype(jnp.int32) * 8 + c)[None],
            "core": k[None],
            "send": (1 - k) * 256,
            "keep": base,
            "one": base + near * 64 + far * 32,
            "two": base + 128 + far * 64 + near * 32,
            "place": c * length,
        }
    )


def rows_from(value, start, size):
    starts = (start,) + (jnp.int32(0),) * (value.ndim - 1)
    return lax.dynamic_slice(value, starts, (size,) + value.shape[1:], allow_negative_indices=False)


def pick(bit, if_zero, if_one):
    return jnp.where(bit, if_one, if_zero)


def merge(bit, own, got):
    return jnp.concatenate([pick(bit, own, got), pick(bit, got, own)], axis=0)


VMEM = pl.BlockSpec(memory_space=pltpu.VMEM)
SMEM = pl.BlockSpec(memory_space=pltpu.SMEM)


def local_call(kernel, name, out_shape, args, in_smem=0, mib=20, scratch=(), flops=0, moved=0, exps=0):
    return pl.pallas_call(
        kernel,
        out_shape=out_shape,
        in_specs=[SMEM] * in_smem + [VMEM] * (len(args) - in_smem),
        out_specs=jax.tree.map(lambda _: VMEM, out_shape),
        scratch_shapes=list(scratch),
        compiler_params=pltpu.CompilerParams(vmem_limit_bytes=mib << 20),
        cost_estimate=pl.CostEstimate(flops=flops, bytes_accessed=moved, transcendentals=exps),
        name=name,
    )(*args)


def fetch_call(kernel, name, out_shape, args, scratch=(), moved=0):
    args = [pltpu.with_memory_space_constraint(v, pltpu.HBM) for v in args]

    def whole(v):
        return pl.BlockSpec(v.shape, lambda i: (0,) * len(v.shape))

    return pl.pallas_call(
        kernel,
        grid=(1,),
        out_shape=out_shape,
        in_specs=[whole(v) for v in args],
        out_specs=jax.tree.map(whole, out_shape),
        scratch_shapes=list(scratch),
        compiler_params=pltpu.CompilerParams(vmem_limit_bytes=12 << 20),
        cost_estimate=pl.CostEstimate(flops=0, bytes_accessed=moved, transcendentals=0),
        name=name,
    )(*args)


def shape(dims, dtype=BF):
    return jax.ShapeDtypeStruct(dims, dtype)


def after(value, *events):
    return lax.optimization_barrier((value, events))[0]


def pack_kernel(key_ref, value_ref, query_ref, output_ref, *refs):
    vectors, outs, rows_ref = refs[:9], refs[9:13], refs[13]
    rows_ref[...] = jnp.zeros(rows_ref.shape, F32)
    for i, v in enumerate(vectors):
        rows_ref[i : i + 1, : v.shape[1]] = v[...]
    rows, width = key_ref.shape
    outs[0][:rows] = key_ref[...].astype(BF)
    outs[0][rows:, :128] = rows_ref[...].astype(BF)
    outs[0][rows:, 128:] = jnp.zeros((16, width - 128), BF)
    outs[1][...] = value_ref[...].astype(BF)
    outs[2][...] = query_ref[...].astype(BF)
    outs[3][...] = output_ref[...].T.astype(BF)


def pack_ffn_kernel(expand_ref, contract_ref, *outs):
    half = expand_ref.shape[1] // 2
    for i in range(2):
        outs[i][...] = expand_ref[:, i * half : (i + 1) * half].astype(BF)
        outs[2 + i][...] = contract_ref[i * half : (i + 1) * half].T.astype(BF)


def join_kernel(count, *refs):
    for own, got, out in zip(refs[:count], refs[count : 2 * count], refs[2 * count :]):
        n = own.shape[0]
        out[:n] = own[...]
        out[n:] = got[...]


def join(owns, gots):
    shapes = [shape((2 * v.shape[0],) + v.shape[1:]) for v in owns]
    size = sum(v.size for v in owns)
    count = len(owns)
    return local_call(lambda *r: join_kernel(count, *r), "join", shapes, [*owns, *gots], mib=4, moved=8 * size)


def swaps(bufs, orders, k):
    return [swap(b, o[k]) for b, o in zip(bufs, orders)]


def place_kernel(rows, plan, count, small, me_ref, *refs):
    owns, gots, outs = refs[:count], refs[count : 2 * count], refs[2 * count :]
    me = me_ref[0]
    if small:
        vec_ref, query_ref, expand_ref = outs[-3:]
        query_ref[...] = jnp.zeros(query_ref.shape, F32)
        expand_ref[...] = jnp.zeros(expand_ref.shape, F32)
    for s, (order, target, column) in enumerate(plan):
        width = owns[s].shape[2]
        away = offsets(order)
        for p in range(16):
            src = owns[s] if p < 8 else gots[s]
            block = me ^ away[p]
            row = pl.multiple_of(block * rows, rows)
            outs[target][pl.ds(row, rows), column : column + width] = src[p % 8, :rows]
            if small and s == 0:
                more = src[p % 8, rows:, :128].astype(F32)
                vec_ref[:, pl.ds(pl.multiple_of(block * 128, 128), 128)] = more[:8]
                cols = pl.ds(pl.multiple_of((block // 8) * 128, 128), 128)
                query_ref[:, cols] = query_ref[:, cols] + pltpu.roll(more[:8], (block % 8) * 16, 1)[6:7]
                cols = pl.ds(pl.multiple_of((block // 2) * 128, 128), 128)
                expand_ref[:, cols] = expand_ref[:, cols] + pltpu.roll(more[8:], (block % 2) * 64, 1)[0:1]


def place(owns, gots, bits, rows, plan, widths, small=()):
    shapes = [shape((16 * rows, w)) for w in widths]
    if small:
        shapes += [shape((8, 2048), F32)] + [shape((1, w), F32) for w in small]
    count = len(owns)
    return local_call(
        lambda *r: place_kernel(rows, plan, count, bool(small), *r),
        "place",
        shapes,
        [bits["me"], *owns, *gots],
        in_smem=1,
        mib=6,
        moved=64 * rows * sum(widths),
    )


def part(grads, gots, bits, plan, step, half=None, small=None):
    rows = grads[0].shape[0] // 16
    low, count = (1 << step, 1 << step) if step >= 0 else (0, 1)
    if half is not None:
        count //= 2
        low += half * count
    n, ng = len(plan), len(grads)
    extra = 16 if small is not None and step >= 0 else 0
    shapes = [shape((count, rows + (extra if s == 0 else 0), p[3]), BF if step >= 0 else F32) for s, p in enumerate(plan)]
    if small is not None and step < 0:
        shapes.append(shape((8, 128), F32))

    def kernel(me_ref, *refs):
        me = me_ref[0]
        first = ng + n * len(gots)
        outs = refs[first + (small is not None) :]
        for s, (order, source, column, width) in enumerate(plan):
            away = offsets(order)
            for q in range(count):
                p = low + q
                row = pl.multiple_of((me ^ away[p]) * rows, rows)
                piece = refs[source][pl.ds(row, rows), column : column + width]
                if gots:
                    piece = piece.astype(F32)
                    for j, (_, base) in enumerate(gots):
                        piece = piece + refs[ng + n * j + s][p - base, :rows].astype(F32)
                outs[s][q, :rows] = piece.astype(outs[s].dtype)
                if small is not None and s == 0:
                    lane = pl.multiple_of((me ^ away[p]) * 128, 128)
                    vectors = jnp.concatenate([refs[first][:, pl.ds(lane, 128)], jnp.zeros((8, 128), F32)], axis=0)
                    for j, (_, base) in enumerate(gots):
                        vectors = vectors + refs[ng + n * j][p - base, rows:, :128].astype(F32)
                    if step >= 0:
                        outs[0][q, rows:, :128] = vectors.astype(BF)
                        outs[0][q, rows:, 128:] = jnp.zeros((16, width - 128), BF)
                    else:
                        outs[-1][...] = vectors[:8]

    args = [bits["me"], *grads, *[g for got, _ in gots for g in got]] + ([small] if small is not None else [])
    moved = 2 * count * rows * sum(p[3] for p in plan) * (2 + len(gots))
    return local_call(kernel, "part", shapes, args, in_smem=1, mib=6, moved=moved)


BIG = ((ORDER_P, ORDER_Q), (ORDER_R, ORDER_S))


def big_part(grads, gots, bits, step):
    rows, width = grads[0].shape[0] // 16, grads[0].shape[1]
    half = width // 2
    count = 1 << step
    in_specs, args, spans, outs = [], [], [], []
    per = 1 + len(gots)
    for low in (count, 0) if step == 1 else (count,):
        for m, pair in enumerate(BIG):
            for s, order in enumerate(pair):
                near = [offsets(order)[1 << k] for k in range(4)]

                def block_at(q, me, near=near, low=low, s=s):
                    p = low + q
                    where = me[0]
                    for k, away in enumerate(near):
                        where = where ^ (((p >> k) & 1) * away)
                    return (where, s)

                in_specs.append(pl.BlockSpec((rows, half), block_at))
                args.append(grads[m])
                for got in gots:
                    in_specs.append(pl.BlockSpec((1, rows, half), lambda q, me, low=low: (low + q, 0, 0)))
                    args.append(got[2 * m + s])
                if step > 1:
                    outs.append(shape((count, rows, half)))
                    spans.append((len(outs) - 1, 0))
                elif s == 0:
                    outs.append(shape((count, rows, width), BF if low else F32))
                    spans.append((len(outs) - 1, 0))
                else:
                    spans.append((len(outs) - 1, half))

    def kernel(me_ref, *refs):
        out_refs = refs[len(args) :]
        for i, (at, column) in enumerate(spans):
            piece = refs[per * i][...]
            if gots:
                piece = piece.astype(F32)
                for j in range(1, per):
                    piece = piece + refs[per * i + j][0].astype(F32)
            out_refs[at][0, :, column : column + half] = piece.astype(outs[at].dtype)

    return pl.pallas_call(
        kernel,
        grid_spec=pltpu.PrefetchScalarGridSpec(
            num_scalar_prefetch=1,
            grid=(count,),
            in_specs=in_specs,
            out_specs=[pl.BlockSpec((1,) + o.shape[1:], lambda q, me: (q, 0, 0)) for o in outs],
        ),
        out_shape=outs,
        compiler_params=pltpu.CompilerParams(vmem_limit_bytes=12 << 20),
        cost_estimate=pl.CostEstimate(flops=0, bytes_accessed=4 * count * rows * width * (1 + per), transcendentals=0),
        name="big_part",
    )(bits["me"], *args)


def big_swaps(values, step):
    if step >= 2:
        return [swap(v, o[step]) for v, o in zip(values, BIG[0] + BIG[1])]
    return [swap(v, pair[0][step]) for v, pair in zip(values, BIG)]


def shard_rows(value, bits):
    return jnp.concatenate([rows_from(value, bits["one"], 32), rows_from(value, bits["two"], 32)], axis=0)


def halves(value, bits):
    return rows_from(value, bits["send"], 256), rows_from(value, bits["keep"], 256)


def reduce_tp(products, operands, bits, beside=None):
    count = len(products)
    pairs = [halves(v, bits) for v in operands]
    send = jnp.concatenate([p(v[0]).astype(BF) for p, v in zip(products, pairs)], axis=0)
    first = swap(send, "C")
    kept = [p(v[1]) for p, v in zip(products, pairs)]
    events = [send]
    if beside:
        first = after(first, beside(0, events, kept))
    totals = [v + first[i * 256 : (i + 1) * 256].astype(F32) for i, v in enumerate(kept)]
    events.append(first)
    streams = [[v[:128] for v in totals], [v[128:] for v in totals]]
    for stage, kinds in enumerate((("Z1", "Z3"), ("Z3", "Z1"))):
        n = streams[0][0].shape[0] // 2
        give = [
            jnp.concatenate([pick(bits[t], v[n:], v[:n]).astype(BF) for v in parts], axis=0)
            for t, parts in zip(kinds, streams)
        ]
        got = [swap(v, t) for v, t in zip(give, kinds)]
        if beside:
            got = after(got, beside(1 + stage, events, kept))
        events.append(got)
        streams = [
            [pick(bits[t], v[:n], v[n:]) + g[i * n : (i + 1) * n].astype(F32) for i, v in enumerate(parts)]
            for t, parts, g in zip(kinds, streams, got)
        ]
    out = [jnp.concatenate([streams[0][i], streams[1][i]], axis=0) for i in range(count)]
    return out, events, kept


def merge_rows(bit, own, got):
    return jnp.concatenate([pick(bit, own, got), pick(bit, got, own)], axis=1)


def gather_tp(shards, bits, beside=None, whole=True):
    parts = [shards[:, :32], shards[:, 32:]]
    events = [shards]
    for stage, kinds in enumerate((("Z3", "Z1"), ("Z1", "Z3"))):
        got = [swap(v, t) for v, t in zip(parts, kinds)]
        if beside:
            got = after(got, beside(3 + stage, events, None))
        events.append(got)
        parts = [merge_rows(bits[t], v, g) for t, v, g in zip(kinds, parts, got)]
    own = jnp.concatenate(parts, axis=1)
    last = swap(own, "C")
    if beside:
        last = after(last, beside(5, events, None))
    events.append(last)
    return (merge_rows(bits["C"], own, last) if whole else (own, last)), events


Y_FLIP = PERM["Y1"]
Y_FLIP_DOWN = pairs_xy(lambda x, y: (x, y ^ 1) if y % 2 == 1 else None)
Y_FLIP_UP = pairs_xy(lambda x, y: (x, y ^ 1) if y % 2 == 0 else None)
X_UP = pairs_xy(lambda x, y: (x + 1, y) if x < 3 else None)
X_UP2 = pairs_xy(lambda x, y: (x + 2, y) if x < 2 else None)
X_DOWN = pairs_xy(lambda x, y: (x - 1, y) if x > 0 else None)
X_DOWN2 = pairs_xy(lambda x, y: (x - 2, y) if x > 1 else None)
SLOTS = 6


def slot_block(slot, c):
    back = slot // 2 * 2
    return c - back if slot % 2 == 0 else (c ^ 1) - back


def slot_needed(slot, c, length, first_ref):
    block = slot_block(slot, c)
    return (block >= 0) & (block < c) & (block * length + length - 1 >= first_ref[0])


def nt(a, b):
    return lax.dot_general(a, b, (((1,), (1,)), ((), ())), preferred_element_type=F32)


def tn(a, b):
    return lax.dot_general(a, b, (((0,), (0,)), ((), ())), preferred_element_type=F32)


def nn(a, b):
    return jnp.dot(a, b, preferred_element_type=F32)


def visible(slot, block, length, start_ref, c):
    keys = lax.broadcasted_iota(jnp.int32, (length, length), 0) + block * length
    mask = keys >= start_ref[...]
    if slot == 0:
        mask = mask & (keys <= lax.broadcasted_iota(jnp.int32, (length, length), 1) + c * length)
    return mask


def attn_fwd_kernel(heads, me_ref, first_ref, start_ref, q_ref, *refs):
    kv = refs[:SLOTS]
    att_ref, mix_ref, lse_ref, m_ref, l_ref = refs[SLOTS:]
    length = q_ref.shape[0]
    hidden = heads * HEAD_DIM
    c = me_ref[0] % 8
    for slot in range(SLOTS):
        block = slot_block(slot, c)

        def run(slot=slot, block=block):
            mask = visible(slot, block, length, start_ref, c)
            for h in range(heads):
                cols = slice(h * HEAD_DIM, (h + 1) * HEAD_DIM)
                key = kv[slot][:, cols]
                val = kv[slot][:, hidden + h * HEAD_DIM : hidden + (h + 1) * HEAD_DIM]
                s = jnp.where(mask, nt(key, q_ref[:, cols]), NEG)
                top = jnp.max(s, axis=0, keepdims=True)
                if slot == 0:
                    p = jnp.exp2((s - top) * SCALE2)
                    m_ref[h : h + 1] = top
                    l_ref[h : h + 1] = jnp.sum(p, axis=0, keepdims=True)
                    mix_ref[cols] = tn(val, p.astype(BF))
                else:
                    old = m_ref[h : h + 1]
                    new = jnp.maximum(old, top)
                    p = jnp.exp2((s - new) * SCALE2)
                    shrink = jnp.exp2((old - new) * SCALE2)
                    m_ref[h : h + 1] = new
                    l_ref[h : h + 1] = l_ref[h : h + 1] * shrink + jnp.sum(p, axis=0, keepdims=True)
                    mix_ref[cols] = mix_ref[cols] * shrink + tn(val, p.astype(BF))

        if slot == 0:
            run()
        else:
            pl.when(slot_needed(slot, c, length, first_ref))(run)
    for h in range(heads):
        cols = slice(h * HEAD_DIM, (h + 1) * HEAD_DIM)
        out = mix_ref[cols] / l_ref[h : h + 1]
        mix_ref[cols] = out
        att_ref[:, cols] = out.T.astype(BF)
        lse_ref[h : h + 1] = m_ref[h : h + 1] * SCALE2 + jnp.log2(l_ref[h : h + 1])


def attn_bwd_kernel(heads, me_ref, first_ref, start_ref, q_ref, do_ref, mix_ref, lse_ref, *refs):
    kv = refs[:SLOTS]
    dq_ref, dkv = refs[SLOTS], refs[SLOTS + 1 : 2 * SLOTS + 1]
    dqt_ref, delta_ref = refs[2 * SLOTS + 1 :]
    length = q_ref.shape[0]
    hidden = heads * HEAD_DIM
    c = me_ref[0] % 8
    for h in range(heads):
        cols = slice(h * HEAD_DIM, (h + 1) * HEAD_DIM)
        dot_t = do_ref[:, cols].astype(F32).T
        delta_ref[h : h + 1] = jnp.sum(dot_t * mix_ref[cols], axis=0, keepdims=True)
    for slot in range(SLOTS):
        block = slot_block(slot, c)

        def run(slot=slot, block=block):
            mask = visible(slot, block, length, start_ref, c)
            for h in range(heads):
                cols = slice(h * HEAD_DIM, (h + 1) * HEAD_DIM)
                vcols = slice(hidden + h * HEAD_DIM, hidden + (h + 1) * HEAD_DIM)
                key, val = kv[slot][:, cols], kv[slot][:, vcols]
                q, do = q_ref[:, cols], do_ref[:, cols]
                s = jnp.where(mask, nt(key, q), NEG)
                p = jnp.exp2(s * SCALE2 - lse_ref[h : h + 1])
                ds = (p * (nt(val, do) - delta_ref[h : h + 1])).astype(BF)
                dkv[slot][:, cols] = (nn(ds, q) * SCALE).astype(dkv[slot].dtype)
                dkv[slot][:, vcols] = nn(p.astype(BF), do).astype(dkv[slot].dtype)
                part = tn(key, ds)
                if slot == 0:
                    dqt_ref[cols] = part
                else:
                    dqt_ref[cols] = dqt_ref[cols] + part

        if slot == 0:
            run()
        else:
            pl.when(slot_needed(slot, c, length, first_ref))(run)

            @pl.when(jnp.logical_not(slot_needed(slot, c, length, first_ref)))
            def _(slot=slot):
                dkv[slot][...] = jnp.zeros(dkv[slot].shape, dkv[slot].dtype)

    for h in range(heads):
        cols = slice(h * HEAD_DIM, (h + 1) * HEAD_DIM)
        dq_ref[:, cols] = (dqt_ref[cols] * SCALE).T.astype(BF)


def stats_kernel(x_ref, mean_ref, spread_ref):
    for r in range(0, x_ref.shape[0], 64):
        v = x_ref[r : r + 64].astype(F32)
        mean = jnp.mean(v, axis=-1, keepdims=True)
        centre = v - mean
        spread = lax.rsqrt(jnp.mean(centre * centre, axis=-1, keepdims=True) + 1e-05)
        mean_ref[r : r + 64] = jnp.broadcast_to(mean, (64, 128))
        spread_ref[r : r + 64] = jnp.broadcast_to(spread, (64, 128))


def norm_kv_kernel(me_ref, x_ref, mean_ref, spread_ref, k_own, v_own, k_got, v_got, normed_ref, kv_ref, acc_ref):
    me = me_ref[0]
    hidden = k_own.shape[2]
    zero = jnp.zeros((1, 128), F32)
    bias = [zero, zero]
    away_k, away_v = offsets(ORDER_A), offsets(ORDER_B)
    for q in range(8):
        parts = []
        for src, p in ((k_own, q), (k_got, q + 8)):
            block = me ^ away_k[p]
            cols = pl.ds(pl.multiple_of(block * 128, 128), 128)
            small = src[q, 128:144, :128].astype(F32)
            scaled = (x_ref[:, cols].astype(F32) - mean_ref[...]) * spread_ref[...]
            part = (scaled * small[0:1] + small[1:2]).astype(BF)
            normed_ref[:, cols] = part
            parts.append(part)
            turned = pltpu.roll(small[:8], (block % 8) * 16, 1)[7:8]
            bias = [bias[0] + jnp.where(block < 8, turned, zero), bias[1] + jnp.where(block < 8, zero, turned)]
        weights = jnp.concatenate([k_own[q, :128], k_got[q, :128]], axis=0)
        term = jnp.dot(jnp.concatenate(parts, axis=1), weights, preferred_element_type=F32)
        acc_ref[...] = term if q == 0 else acc_ref[...] + term
    kv_ref[:, :hidden] = acc_ref[...].astype(BF)
    for q in range(8):
        parts = []
        for p in (q, q + 8):
            parts.append(normed_ref[:, pl.ds(pl.multiple_of((me ^ away_v[p]) * 128, 128), 128)])
        weights = jnp.concatenate([v_own[q], v_got[q]], axis=0)
        term = jnp.dot(jnp.concatenate(parts, axis=1), weights, preferred_element_type=F32)
        acc_ref[...] = term if q == 0 else acc_ref[...] + term
    kv_ref[:, hidden:] = (acc_ref[...] + jnp.concatenate(bias, axis=1)).astype(BF)


def early_kernel(att_ref, query_ref, pre_ref, attn_ref, norm_ref, scaled_ref, cot_ref, out_ref):
    def total(v):
        return jnp.sum(v.astype(F32), axis=0, keepdims=True)

    out_ref[0:2] = jnp.zeros((2, out_ref.shape[1]), F32)
    out_ref[2:3] = total(attn_ref[...])
    out_ref[3:4] = total(norm_ref[...] * scaled_ref[...])
    out_ref[4:5] = total(norm_ref[...])
    out_ref[5:6] = total(cot_ref[...])
    value, query, expand = total(att_ref[...]), total(query_ref[...]), total(pre_ref[...])
    lane = lax.broadcasted_iota(jnp.int32, (8, 128), 1)

    def taken(row, size, block, to):
        at = block * size
        wide = jnp.broadcast_to(row[:, at // 128 * 128 : at // 128 * 128 + 128], (8, 128))
        wide = pltpu.roll(wide, (128 - at % 128 + to) % 128, 1)
        return jnp.where((lane >= to) & (lane < to + size), wide, 0.0)[0:1]

    nb, ne = value.shape[1] // 16, expand.shape[1] // 16
    for block in range(16):
        cols = slice(block * 128, block * 128 + 128)
        out_ref[6:7, cols] = taken(value, nb, block, 0) + taken(expand, ne, block, nb)
        out_ref[7:8, cols] = taken(query, nb, block, 0)


def late_kernel(core_ref, x_ref, mean_ref, spread_ref, gone_ref, kept_ref, early_ref, out_ref):
    core = core_ref[0]
    size = gone_ref.shape[0]
    out_ref[...] = early_ref[...]
    first = jnp.zeros((1, x_ref.shape[1]), F32)
    second = first
    for src, base in ((gone_ref, (1 - core) * size), (kept_ref, core * size)):
        for r in range(0, size, 32):
            rows = pl.ds(pl.multiple_of(base + r, 32), 32)
            scaled = (x_ref[rows].astype(F32) - mean_ref[rows][:, :1]) * spread_ref[rows][:, :1]
            grad = src[r : r + 32].astype(F32)
            first = first + jnp.sum(grad * scaled, axis=0, keepdims=True)
            second = second + jnp.sum(grad, axis=0, keepdims=True)
    out_ref[0:1] = first
    out_ref[1:2] = second


def final_ffn_kernel(*refs):
    kept, one, zero, outs = refs[:2], refs[2:4], refs[4:6], refs[6:]
    total = [k[0] + a[0].astype(F32) + b[0].astype(F32) for k, a, b in zip(kept, one, zero)]
    outs[0][...] = total[0]
    for j in range(0, total[1].shape[1], 128):
        outs[1][j : j + 128] = total[1][:, j : j + 128].T


def final_rows_kernel(core_ref, own_ref, last_ref, grad_ref, out_ref):
    size = own_ref.shape[1]
    core = core_ref[0]
    for src, base in ((own_ref, core * size), (last_ref, (1 - core) * size)):
        for r in range(0, size, 64):
            rows = pl.ds(pl.multiple_of(base + r, 64), 64)
            grad_ref[rows] = src[0, r : r + 64].astype(F32)
            out_ref[rows] = src[1, r : r + 64]


def final_qo_kernel(me_ref, grad_ref, *refs):
    gots, outs = refs[:-2], refs[-2:]
    piece = grad_ref[pl.ds(pl.multiple_of(me_ref[0] * 128, 128), 128)].astype(F32)
    for got in gots:
        piece = piece + got[0].astype(F32)
    half = piece.shape[1] // 2
    outs[0][...] = piece[:, :half]
    outs[1][...] = piece[:, half:].T


def norm_stats(v):
    mean = jnp.mean(v, axis=-1, keepdims=True)
    centre = v - mean
    spread = lax.rsqrt(jnp.mean(centre * centre, axis=-1, keepdims=True) + 1e-05)
    return centre * spread, spread


def norm_back(grad, gain, scaled, spread):
    weighted = grad * gain
    inner = jnp.mean(weighted, axis=-1, keepdims=True)
    cross = jnp.mean(weighted * scaled, axis=-1, keepdims=True)
    return spread * (weighted - inner - scaled * cross)


def cols_of(w, n=4):
    k = w.shape[1] // n
    return [w[:, i * k : (i + 1) * k] for i in range(n)]


def body(
    layer_input,
    doc_ids,
    pre_gain,
    pre_shift,
    query_weight,
    query_bias,
    key_weight,
    value_weight,
    value_bias,
    output_weight,
    output_bias,
    mid_gain,
    mid_shift,
    expand_weight,
    expand_bias,
    contract_weight,
    contract_bias,
    cotangent,
):
    bits = own_bits(layer_input.shape[1])
    x = layer_input[0]
    cot = cotangent[0]
    length, width = x.shape
    hidden = query_weight.shape[1]
    heads = hidden // HEAD_DIM
    inner = expand_weight.shape[1]

    nb, ne = query_bias.shape[1], expand_bias.shape[1]
    pre_gain = after(pre_gain, bits)
    vectors = [pre_gain, pre_shift, output_bias, mid_gain, mid_shift, contract_bias]
    weights = [key_weight, value_weight, query_weight, output_weight]
    packed = shape((128, hidden))
    bufs = fetch_call(
        pack_kernel,
        "pack",
        [shape((144, hidden)), packed, packed, packed],
        [*weights, *[v[None] for v in vectors], query_bias, value_bias, expand_bias],
        scratch=[pltpu.VMEM((16, 128), F32)],
        moved=800 << 10,
    )
    bufs = [v[None] for v in bufs]
    first_orders, big_orders = (ORDER_A, ORDER_B, ORDER_C, ORDER_D), (ORDER_E, ORDER_F)
    kv_orders, qo_orders = (ORDER_A, ORDER_B), (ORDER_D,)
    half_shape = shape((128, inner // 2))
    ffn = fetch_call(
        pack_ffn_kernel, "pack_ffn", [half_shape] * 4, [expand_weight, contract_weight], moved=1536 << 10
    )
    con = [v[None] for v in ffn[2:]]
    bufs = join(bufs, swaps(bufs, first_orders, 0))
    got = swaps(bufs, first_orders, 1)
    stats = [shape((length, 128), F32)] * 2
    mean1, spread1 = local_call(stats_kernel, "stats", stats, [after(x, bufs)], mib=8, moved=3 << 20)
    one = swaps(con[:1], big_orders[:1], 0)
    bufs = join(bufs, after(got, one, mean1))
    got = swaps(bufs, first_orders, 2)
    two = swaps(con[1:], big_orders[1:], 0)
    bufs = join(bufs, after(got, two))
    con = join(con, one + two)
    got = swaps(bufs, first_orders, 3)
    got_con = swaps(after(con, got), big_orders, 1)
    exp_orders = (ORDER_G, ORDER_H)
    exp = [v[None] for v in ffn[:2]]
    got_exp = swaps(after(exp, got), exp_orders, 0)

    docs = doc_ids[0]
    own_docs = rows_from(docs, bits["place"], length)
    start = jnp.sum((docs[:, None] < own_docs[None, :]).astype(jnp.int32), axis=0)
    first_key = start[:1]
    start = start[None]

    normed, kv_own = local_call(
        norm_kv_kernel,
        "norm_kv",
        [shape((length, width)), shape((length, 2 * hidden))],
        [bits["me"], x, mean1, spread1, bufs[0], bufs[1], got[0], got[1]],
        in_smem=1,
        mib=10,
        scratch=[pltpu.VMEM((length, hidden), F32)],
        flops=2 * length * width * 2 * hidden,
        moved=6 << 20,
    )
    kv_own = after(kv_own, got_con, got_exp)
    kv_e1 = lax.ppermute(kv_own, XY, Y_FLIP)
    kv_f1 = lax.ppermute(kv_own, XY, X_UP)
    kv_f2 = lax.ppermute(kv_own, XY, X_UP2)
    con = join(con, got_con)
    exp = join(exp, got_exp)
    got_con = swaps(con, big_orders, 2)
    kv_e1 = after(kv_e1, exp, con, kv_f1)
    plan = [(ORDER_A, 0, 0), (ORDER_B, 0, hidden), (ORDER_C, 1, 0), (ORDER_D, 2, 0)]
    kv_full, q_full, o_full, vec, q_bias, e_bias = place(
        after(bufs, kv_e1), got, bits, 128, plan, [2 * hidden, hidden, hidden], [hidden, inner]
    )
    gain1, out_bias, gain2, shift2, con_bias = [vec[i : i + 1] for i in (0, 2, 3, 4, 5)]
    kv_g1 = lax.ppermute(after(kv_e1, kv_f2), XY, X_UP)
    kv_e3 = lax.ppermute(kv_f2, XY, Y_FLIP_DOWN)
    queries = (nn(normed, q_full) + q_bias).astype(BF)
    con = join(con, after(got_con, kv_e1))
    got_con = swaps(con, big_orders, 3)

    slots = [kv_own, kv_e1, kv_f1, kv_g1, kv_f2, kv_e3]
    attended, mixture, lse = local_call(
        lambda *refs: attn_fwd_kernel(heads, *refs),
        "attn_fwd",
        [shape((length, hidden)), shape((hidden, length), F32), shape((heads, length), F32)],
        [bits["me"], first_key, start, after(queries, con), *slots],
        in_smem=2,
        mib=12,
        scratch=[pltpu.VMEM((heads, length), F32), pltpu.VMEM((heads, length), F32)],
        flops=10**9,
        moved=6 << 20,
        exps=3 * 10**6,
    )

    feed = {}

    def beside_a(stage, events, kept):
        now = events[-1]
        if stage == 0:
            plan = [(ORDER_E, 0, 0), (ORDER_F, 0, inner // 2)]
            feed["contract"] = place(con, got_con, bits, 128, plan, [inner])[0]
            feed["got"] = swaps(after(exp, now), exp_orders, 1)
            return [feed["contract"], feed["got"]]
        if stage == 1:
            feed["exp"] = join(exp, after(feed["got"], now))
            feed["got"] = swaps(feed["exp"], exp_orders, 2)
        if stage == 2:
            return feed["got"]
        if stage == 3:
            feed["exp"] = join(feed["exp"], after(feed["got"], now))
            feed["got"] = swaps(feed["exp"], exp_orders, 3)
        return []

    (attn_total,), _, _ = reduce_tp([lambda v: nt(v, o_full)], [attended], bits, beside_a)
    contract_full = feed["contract"]
    x_shard = shard_rows(x, bits).astype(F32)
    middle = x_shard + (attn_total + out_bias)
    scaled2, spread2 = norm_stats(middle)
    normed_two, _ = gather_tp((scaled2 * gain2 + shift2).astype(BF)[None], bits, beside_a)
    normed_two = normed_two[0]

    plan = [(ORDER_G, 0, 0), (ORDER_H, 0, inner // 2)]
    expand_full = place(feed["exp"], feed["got"], bits, 128, plan, [inner])[0]
    grad_act = nn(cot, contract_full)
    pre_act = nn(normed_two, expand_full) + e_bias
    cdf = 0.5 * (1.0 + lax.erf(pre_act * (1.0 / math.sqrt(2.0))))
    activated = (pre_act * cdf).astype(BF)
    slope = cdf + pre_act * jnp.exp(-0.5 * pre_act * pre_act) * (1.0 / math.sqrt(2.0 * math.pi))
    grad_pre = (slope * grad_act).astype(BF)
    big = {}

    def beside_de(stage, events, kept):
        if stage == 1:
            held = after((cot, activated, normed_two, grad_pre), kept)
            big["grads"] = [tn(held[2], held[3]).astype(BF), tn(held[0], held[1]).astype(BF)]
            big["send"] = big_part(big["grads"], [], bits, 3)
            return big["send"]
        if stage == 2:
            big["got3"] = big_swaps(after(big["send"], events[-1]), 3)
        if stage == 3:
            return big["got3"]
        if stage != 4:
            return []
        big["send"] = big_part(big["grads"], [after(big["got3"], events[-1])], bits, 2)
        big["got2"] = big_swaps(big["send"], 2)
        return big["send"]

    (grad_norm2,), _, _ = reduce_tp([lambda v: nt(v, expand_full)], [grad_pre], bits, beside_de)

    cot_shard = shard_rows(cot, bits).astype(F32)
    grad_middle = cot_shard + norm_back(grad_norm2, gain2, scaled2, spread2)
    grad_attn_shard = grad_middle.astype(BF)
    grad_attn, _ = gather_tp(grad_attn_shard[None], bits, beside_de)
    grad_attn = grad_attn[0]

    grad_att = nn(grad_attn, o_full).astype(BF)
    dkv = shape((length, 2 * hidden))
    grad_q, own_part, p_e1, p_f1, p_g1, p_f2, p_e3 = local_call(
        lambda *refs: attn_bwd_kernel(heads, *refs),
        "attn_bwd",
        [shape((length, hidden)), shape((length, 2 * hidden), F32)] + [dkv] * 5,
        [bits["me"], first_key, start, queries, after(grad_att, big["send"]), mixture, lse, *slots],
        in_smem=2,
        mib=16,
        scratch=[pltpu.VMEM((hidden, length), F32), pltpu.VMEM((heads, length), F32)],
        flops=2 * 10**9,
        moved=10 << 20,
        exps=3 * 10**6,
    )
    got2 = after(big["got2"], grad_q)
    both = big_part(big["grads"], [big["got3"], got2], bits, 1)
    rest = both[2:]
    from_g1 = lax.ppermute(after(p_g1, got2), XY, X_DOWN)
    from_e3 = lax.ppermute(after(p_e3, got2), XY, Y_FLIP_UP)
    got1 = big_swaps(both[:2], 1)
    mlp_send, mlp_keep = halves(after(activated, got2), bits)
    mlp_got = swap(after(nt(mlp_send, contract_full).astype(BF), got2), "C")

    grad_o = tn(grad_attn, after(attended, grad_q)).astype(BF)
    qo_grads = [jnp.concatenate([tn(normed, grad_q).astype(BF), grad_o], axis=1)]
    qo_plan = [(ORDER_D, 0, 0, 2 * hidden)]
    qo_send = part(qo_grads, [], bits, qo_plan, 3, 0), part(qo_grads, [], bits, qo_plan, 3, 1)
    from_f1 = lax.ppermute(after(p_f1, from_g1), XY, X_DOWN)
    total = nt(mlp_keep, contract_full) + after(mlp_got, from_g1).astype(F32)
    one, two = total[:128], total[128:]
    two = [jnp.concatenate([two[i : i + 32], two[i + 64 : i + 96]], axis=0) for i in (0, 32)]
    give = [pick(bits["Z1"], one[64:], one[:64]), pick(bits["Z1"], two[1], two[0])]
    mlp_got = swap(after(jnp.concatenate(give, axis=0).astype(BF), got1), "Z1")
    one = pick(bits["Z1"], one[:64], one[64:])
    two = pick(bits["Z1"], two[0], two[1])
    from_e1 = lax.ppermute((p_e1.astype(F32) + from_g1.astype(F32)).astype(BF), XY, Y_FLIP)
    from_f2 = lax.ppermute((p_f2.astype(F32) + from_e3.astype(F32)).astype(BF), XY, X_DOWN2)
    early = local_call(
        early_kernel,
        "early",
        shape((8, width), F32),
        [grad_att, grad_q, grad_pre, grad_attn_shard, grad_norm2, scaled2, cot_shard],
        mib=8,
        moved=4 << 20,
    )
    from_e1 = after(from_e1, early)
    send0 = [(v[1:] + g[1:].astype(F32)).astype(BF) for v, g in zip(rest, got1)]
    from_f2 = after(from_f2, send0, qo_send)
    mlp_got = after(mlp_got, from_e1).astype(F32)
    one, two = one + mlp_got[:64], two + mlp_got[64:]
    give = [pick(bits["Z3"], v[32:], v[:32]).astype(BF) for v in (one, two)]
    mlp_give = jnp.concatenate(give, axis=0)
    mlp_kept = jnp.concatenate([pick(bits["Z3"], v[:32], v[32:]) for v in (one, two)], axis=0)
    from_f2 = after(from_f2, mlp_give)
    grad_kv = (own_part + from_f1.astype(F32) + from_e1.astype(F32) + from_f2.astype(F32)).astype(BF)

    qkv_full = jnp.concatenate([after(q_full, grad_q), kv_full], axis=1)
    grad_qkv = jnp.concatenate([grad_q, grad_kv], axis=1)
    tail = {}

    kv_plan = [(ORDER_A, 0, 0, hidden), (ORDER_B, 0, hidden, hidden)]

    def beside_fg(stage, events, kept):
        now = events[-1]
        if stage == 0:
            tail["q3"] = swaps(after(qo_send[0], now), qo_orders, 3)
            big["got0"] = big_swaps(after(send0, now), 0)
            tail["mlp"] = swap(after(mlp_give, now), "Z3")
            tail["kv"] = [tn(normed, after(grad_kv, now)).astype(BF)]
            return [tail["kv"], big["got0"], tail["mlp"]]
        if stage == 1:
            tail["small"] = local_call(
                late_kernel,
                "late",
                shape((8, width), F32),
                [bits["core"], x, mean1, spread1, events[0], kept[0], early],
                in_smem=1,
                mib=8,
                moved=6 << 20,
            )
            tail["send"] = part(tail["kv"], [], bits, kv_plan, 3, small=tail["small"])
            tail["k3"] = swaps(tail["send"], kv_orders, 3)
            tail["q3_high"] = swaps(after(qo_send[1], tail["q3"], now), qo_orders, 3)
            return [tail["send"], tail["q3"]]
        if stage == 2:
            big["final"] = local_call(
                final_ffn_kernel,
                "final_ffn",
                [shape((width // 16, inner), F32), shape((inner, width // 16), F32)],
                [*rest, *got1, *after(big["got0"], now)],
                mib=8,
                moved=4 << 20,
            )
            return [tail["k3"], tail["q3_high"], big["final"]]
        small = dict(small=tail["small"])
        if stage == 3:
            tail["k2"] = swaps(part(tail["kv"], [(after(tail["k3"], now), 0)], bits, kv_plan, 2, **small), kv_orders, 2)
            tail["q2"] = swaps(part(qo_grads, [(after(tail["q3_high"], now), 4)], bits, qo_plan, 2), qo_orders, 2)
            return [tail["k2"], tail["q2"]]
        if stage == 4:
            gots = [(tail["k3"], 0), (after(tail["k2"], now), 0)]
            tail["k1"] = swaps(part(tail["kv"], gots, bits, kv_plan, 1, **small), kv_orders, 1)
            gots = [(tail["q3"], 0), (after(tail["q2"], now), 0)]
            tail["q1"] = swaps(part(qo_grads, gots, bits, qo_plan, 1), qo_orders, 1)
            return [tail["k1"], tail["q1"]]
        gots = [(tail["k3"], 0), (tail["k2"], 0), (after(tail["k1"], now), 0)]
        tail["k0"] = swaps(part(tail["kv"], gots, bits, kv_plan, 0, **small), kv_orders, 0)
        gots = [(tail["q3"], 0), (tail["q2"], 0), (after(tail["q1"], now), 0)]
        tail["q0"] = swaps(part(qo_grads, gots, bits, qo_plan, 0), qo_orders, 0)
        return [tail["k0"], tail["q0"]]

    (grad_norm1,), _, _ = reduce_tp([lambda v: nt(v, qkv_full)], [grad_qkv], bits, beside_fg)
    x_scaled, x_spread = norm_stats(x_shard)
    grad_x = grad_middle + norm_back(grad_norm1, gain1, x_scaled, x_spread)
    mlp_total = mlp_kept + tail["mlp"].astype(F32)
    layer_shard = (middle + (mlp_total + con_bias)).astype(BF)
    (own, last), _ = gather_tp(jnp.stack([grad_x.astype(BF), layer_shard]), bits, beside_fg, whole=False)
    input_grad, layer_output = local_call(
        final_rows_kernel,
        "final_rows",
        [shape((length, width), F32), shape((length, width))],
        [bits["core"], own, last],
        in_smem=1,
        mib=8,
        moved=10 << 20,
    )
    gots = [(tail[k], 0) for k in ("k3", "k2", "k1", "k0")]
    k_grad, v_grad, small = part(tail["kv"], gots, bits, kv_plan, -1, small=tail["small"])
    biases, q_bias_grad = small[6:7], small[7:8]
    for kind in ("C", "Z1", "Z3"):
        small = small + swap(small, kind)
    gots = [(tail[k], 0) for k in ("q3", "q2", "q1", "q0")]
    q_grad, o_grad = local_call(
        final_qo_kernel,
        "final_qo",
        [shape((width // 16, hidden), F32), shape((hidden, width // 16), F32)],
        [bits["me"], *qo_grads, *[g for got, _ in gots for g in got]],
        in_smem=1,
        mib=6,
        moved=1 << 20,
    )
    expand_grad, contract_grad = big["final"]

    return (
        layer_output[None],
        input_grad[None],
        small[0],
        small[1],
        q_grad,
        q_bias_grad[:, :nb],
        k_grad[0],
        v_grad[0],
        biases[:, :nb],
        o_grad,
        small[2],
        small[3],
        small[4],
        expand_grad,
        biases[:, nb : nb + ne],
        contract_grad,
        small[5],
    )


def solution(mesh):
    both = ("fsdp", "ctx")
    rows, cols, vec = P(both, "tp"), P("tp", both), P(both)
    act = P("fsdp", "ctx", None)
    return jax.shard_map(
        body,
        mesh=mesh,
        in_specs=(
            act, P("fsdp", None), vec, vec, rows, cols, rows, rows, cols, cols, vec, vec, vec,
            rows, cols, cols, vec, act,
        ),
        out_specs=(
            act, act, vec, vec, rows, cols, rows, rows, cols, cols, vec, vec, vec, rows, cols, cols, vec,
        ),
        check_vma=False,
    )
```

```python
import math

import jax
import jax.numpy as jnp
from jax import lax
from jax.experimental import pallas as pl
from jax.experimental.pallas import tpu as pltpu
from jax.sharding import PartitionSpec as P

HEAD_DIM = 128
BF = jnp.bfloat16
F32 = jnp.float32
XY = ("fsdp", "ctx")
NEG = -1e30
SCALE = 1.0 / math.sqrt(HEAD_DIM)
SCALE2 = SCALE / math.log(2.0)


def lin(x, y):
    return (y // 2) * 8 + x * 2 + y % 2


def pairs_xy(move):
    out = []
    for x in range(4):
        for y in range(4):
            to = move(x, y)
            if to is not None:
                out.append((lin(x, y), lin(*to)))
    return out


PERM = {
    "X1": pairs_xy(lambda x, y: (x ^ 1, y)),
    "X3": pairs_xy(lambda x, y: (x ^ 3, y)),
    "Y1": pairs_xy(lambda x, y: (x, y ^ 1)),
    "Y3": pairs_xy(lambda x, y: (x, y ^ 3)),
    "C": [(t, t ^ 1) for t in range(8)],
    "Z1": [(t, t ^ 2) for t in range(8)],
    "Z3": [(t, t ^ 6) for t in range(8)],
}
VEC = {"X1": (1, 0), "X3": (3, 0), "Y1": (0, 1), "Y3": (0, 3)}
ORDER_A = ("X1", "Y1", "X3", "Y3")
ORDER_B = ("Y1", "X3", "Y3", "X1")
ORDER_C = ("X3", "Y3", "X1", "Y1")
ORDER_D = ("Y3", "X1", "Y1", "X3")
ORDER_E = ("X1", "X3", "Y1", "Y3")
ORDER_F = ("X3", "X1", "Y3", "Y1")
ORDER_G = ("Y1", "X1", "X3", "Y3")
ORDER_H = ("Y3", "X3", "X1", "Y1")
ORDER_P = ("X1", "X3", "Y3", "Y1")
ORDER_Q = ("X1", "X3", "Y1", "Y3")
ORDER_R = ("Y1", "Y3", "X3", "X1")
ORDER_S = ("Y1", "Y3", "X1", "X3")


def swap(value, kind):
    return lax.ppermute(value, XY if kind in VEC else "tp", PERM[kind])


def offsets(order):
    out = []
    for p in range(16):
        x = y = 0
        for k, kind in enumerate(order):
            if (p >> k) & 1:
                x ^= VEC[kind][0]
                y ^= VEC[kind][1]
        out.append(lin(x, y))
    return out


def own_bits(length):
    c = lax.axis_index("ctx").astype(jnp.int32)
    t = lax.axis_index("tp").astype(jnp.int32)
    z1, z0, k = t >> 2, (t >> 1) & 1, t & 1
    near, far = z0 ^ z1, z1
    base = k * 256
    return lax.optimization_barrier(
        {
            "Z1": near == 1,
            "Z3": far == 1,
            "C": k == 1,
            "me": (lax.axis_index("fsdp").astype(jnp.int32) * 8 + c)[None],
            "core": k[None],
            "send": (1 - k) * 256,
            "keep": base,
            "one": base + near * 64 + far * 32,
            "two": base + 128 + far * 64 + near * 32,
            "place": c * length,
        }
    )


def rows_from(value, start, size):
    starts = (start,) + (jnp.int32(0),) * (value.ndim - 1)
    return lax.dynamic_slice(value, starts, (size,) + value.shape[1:], allow_negative_indices=False)


def pick(bit, if_zero, if_one):
    return jnp.where(bit, if_one, if_zero)


def merge(bit, own, got):
    return jnp.concatenate([pick(bit, own, got), pick(bit, got, own)], axis=0)


VMEM = pl.BlockSpec(memory_space=pltpu.VMEM)
SMEM = pl.BlockSpec(memory_space=pltpu.SMEM)


def local_call(kernel, name, out_shape, args, in_smem=0, mib=20, scratch=(), flops=0, moved=0, exps=0):
    return pl.pallas_call(
        kernel,
        out_shape=out_shape,
        in_specs=[SMEM] * in_smem + [VMEM] * (len(args) - in_smem),
        out_specs=jax.tree.map(lambda _: VMEM, out_shape),
        scratch_shapes=list(scratch),
        compiler_params=pltpu.CompilerParams(vmem_limit_bytes=mib << 20),
        cost_estimate=pl.CostEstimate(flops=flops, bytes_accessed=moved, transcendentals=exps),
        name=name,
    )(*args)


def fetch_call(kernel, name, out_shape, args, scratch=(), moved=0):
    args = [pltpu.with_memory_space_constraint(v, pltpu.HBM) for v in args]

    def whole(v):
        return pl.BlockSpec(v.shape, lambda i: (0,) * len(v.shape))

    return pl.pallas_call(
        kernel,
        grid=(1,),
        out_shape=out_shape,
        in_specs=[whole(v) for v in args],
        out_specs=jax.tree.map(whole, out_shape),
        scratch_shapes=list(scratch),
        compiler_params=pltpu.CompilerParams(vmem_limit_bytes=12 << 20),
        cost_estimate=pl.CostEstimate(flops=0, bytes_accessed=moved, transcendentals=0),
        name=name,
    )(*args)


def shape(dims, dtype=BF):
    return jax.ShapeDtypeStruct(dims, dtype)


def after(value, *events):
    return lax.optimization_barrier((value, events))[0]


def pack_kernel(key_ref, value_ref, query_ref, output_ref, *refs):
    vectors, outs, rows_ref = refs[:9], refs[9:13], refs[13]
    rows_ref[...] = jnp.zeros(rows_ref.shape, F32)
    for i, v in enumerate(vectors):
        rows_ref[i : i + 1, : v.shape[1]] = v[...]
    rows, width = key_ref.shape
    outs[0][:rows] = key_ref[...].astype(BF)
    outs[0][rows:, :128] = rows_ref[...].astype(BF)
    outs[0][rows:, 128:] = jnp.zeros((16, width - 128), BF)
    outs[1][...] = value_ref[...].astype(BF)
    outs[2][...] = query_ref[...].astype(BF)
    outs[3][...] = output_ref[...].T.astype(BF)


def pack_ffn_kernel(expand_ref, contract_ref, *outs):
    half = expand_ref.shape[1] // 2
    for i in range(2):
        outs[i][...] = expand_ref[:, i * half : (i + 1) * half].astype(BF)
        outs[2 + i][...] = contract_ref[i * half : (i + 1) * half].T.astype(BF)


def join_kernel(count, *refs):
    for own, got, out in zip(refs[:count], refs[count : 2 * count], refs[2 * count :]):
        n = own.shape[0]
        out[:n] = own[...]
        out[n:] = got[...]


def join(owns, gots):
    shapes = [shape((2 * v.shape[0],) + v.shape[1:]) for v in owns]
    size = sum(v.size for v in owns)
    count = len(owns)
    return local_call(lambda *r: join_kernel(count, *r), "join", shapes, [*owns, *gots], mib=4, moved=8 * size)


def swaps(bufs, orders, k):
    return [swap(b, o[k]) for b, o in zip(bufs, orders)]


def place_kernel(rows, plan, count, small, me_ref, *refs):
    owns, gots, outs = refs[:count], refs[count : 2 * count], refs[2 * count :]
    me = me_ref[0]
    if small:
        vec_ref, query_ref, expand_ref = outs[-3:]
        query_ref[...] = jnp.zeros(query_ref.shape, F32)
        expand_ref[...] = jnp.zeros(expand_ref.shape, F32)
    for s, (order, target, column) in enumerate(plan):
        width = owns[s].shape[2]
        away = offsets(order)
        for p in range(16):
            src = owns[s] if p < 8 else gots[s]
            block = me ^ away[p]
            row = pl.multiple_of(block * rows, rows)
            outs[target][pl.ds(row, rows), column : column + width] = src[p % 8, :rows]
            if small and s == 0:
                more = src[p % 8, rows:, :128].astype(F32)
                vec_ref[:, pl.ds(pl.multiple_of(block * 128, 128), 128)] = more[:8]
                cols = pl.ds(pl.multiple_of((block // 8) * 128, 128), 128)
                query_ref[:, cols] = query_ref[:, cols] + pltpu.roll(more[:8], (block % 8) * 16, 1)[6:7]
                cols = pl.ds(pl.multiple_of((block // 2) * 128, 128), 128)
                expand_ref[:, cols] = expand_ref[:, cols] + pltpu.roll(more[8:], (block % 2) * 64, 1)[0:1]


def place(owns, gots, bits, rows, plan, widths, small=()):
    shapes = [shape((16 * rows, w)) for w in widths]
    if small:
        shapes += [shape((8, 2048), F32)] + [shape((1, w), F32) for w in small]
    count = len(owns)
    return local_call(
        lambda *r: place_kernel(rows, plan, count, bool(small), *r),
        "place",
        shapes,
        [bits["me"], *owns, *gots],
        in_smem=1,
        mib=6,
        moved=64 * rows * sum(widths),
    )


def part(grads, gots, bits, plan, step, half=None, small=None):
    rows = grads[0].shape[0] // 16
    low, count = (1 << step, 1 << step) if step >= 0 else (0, 1)
    if half is not None:
        count //= 2
        low += half * count
    n, ng = len(plan), len(grads)
    extra = 16 if small is not None and step >= 0 else 0
    shapes = [shape((count, rows + (extra if s == 0 else 0), p[3]), BF if step >= 0 else F32) for s, p in enumerate(plan)]
    if small is not None and step < 0:
        shapes.append(shape((8, 128), F32))

    def kernel(me_ref, *refs):
        me = me_ref[0]
        first = ng + n * len(gots)
        outs = refs[first + (small is not None) :]
        for s, (order, source, column, width) in enumerate(plan):
            away = offsets(order)
            for q in range(count):
                p = low + q
                row = pl.multiple_of((me ^ away[p]) * rows, rows)
                piece = refs[source][pl.ds(row, rows), column : column + width]
                if gots:
                    piece = piece.astype(F32)
                    for j, (_, base) in enumerate(gots):
                        piece = piece + refs[ng + n * j + s][p - base, :rows].astype(F32)
                outs[s][q, :rows] = piece.astype(outs[s].dtype)
                if small is not None and s == 0:
                    lane = pl.multiple_of((me ^ away[p]) * 128, 128)
                    vectors = jnp.concatenate([refs[first][:, pl.ds(lane, 128)], jnp.zeros((8, 128), F32)], axis=0)
                    for j, (_, base) in enumerate(gots):
                        vectors = vectors + refs[ng + n * j][p - base, rows:, :128].astype(F32)
                    if step >= 0:
                        outs[0][q, rows:, :128] = vectors.astype(BF)
                        outs[0][q, rows:, 128:] = jnp.zeros((16, width - 128), BF)
                    else:
                        outs[-1][...] = vectors[:8]

    args = [bits["me"], *grads, *[g for got, _ in gots for g in got]] + ([small] if small is not None else [])
    moved = 2 * count * rows * sum(p[3] for p in plan) * (2 + len(gots))
    return local_call(kernel, "part", shapes, args, in_smem=1, mib=6, moved=moved)


BIG = ((ORDER_P, ORDER_Q), (ORDER_R, ORDER_S))


def big_part(grads, gots, bits, step):
    rows, width = grads[0].shape[0] // 16, grads[0].shape[1]
    half = width // 2
    count = 1 << step
    in_specs, args, spans, outs = [], [], [], []
    per = 1 + len(gots)
    for low in (count, 0) if step == 1 else (count,):
        for m, pair in enumerate(BIG):
            for s, order in enumerate(pair):
                near = [offsets(order)[1 << k] for k in range(4)]

                def block_at(q, me, near=near, low=low, s=s):
                    p = low + q
                    where = me[0]
                    for k, away in enumerate(near):
                        where = where ^ (((p >> k) & 1) * away)
                    return (where, s)

                in_specs.append(pl.BlockSpec((rows, half), block_at))
                args.append(grads[m])
                for got in gots:
                    in_specs.append(pl.BlockSpec((1, rows, half), lambda q, me, low=low: (low + q, 0, 0)))
                    args.append(got[2 * m + s])
                if step > 1:
                    outs.append(shape((count, rows, half)))
                    spans.append((len(outs) - 1, 0))
                elif s == 0:
                    outs.append(shape((count, rows, width), BF if low else F32))
                    spans.append((len(outs) - 1, 0))
                else:
                    spans.append((len(outs) - 1, half))

    def kernel(me_ref, *refs):
        out_refs = refs[len(args) :]
        for i, (at, column) in enumerate(spans):
            piece = refs[per * i][...]
            if gots:
                piece = piece.astype(F32)
                for j in range(1, per):
                    piece = piece + refs[per * i + j][0].astype(F32)
            out_refs[at][0, :, column : column + half] = piece.astype(outs[at].dtype)

    return pl.pallas_call(
        kernel,
        grid_spec=pltpu.PrefetchScalarGridSpec(
            num_scalar_prefetch=1,
            grid=(count,),
            in_specs=in_specs,
            out_specs=[pl.BlockSpec((1,) + o.shape[1:], lambda q, me: (q, 0, 0)) for o in outs],
        ),
        out_shape=outs,
        compiler_params=pltpu.CompilerParams(vmem_limit_bytes=12 << 20),
        cost_estimate=pl.CostEstimate(flops=0, bytes_accessed=4 * count * rows * width * (1 + per), transcendentals=0),
        name="big_part",
    )(bits["me"], *args)


def big_swaps(values, step):
    if step >= 2:
        return [swap(v, o[step]) for v, o in zip(values, BIG[0] + BIG[1])]
    return [swap(v, pair[0][step]) for v, pair in zip(values, BIG)]


def shard_rows(value, bits):
    return jnp.concatenate([rows_from(value, bits["one"], 32), rows_from(value, bits["two"], 32)], axis=0)


def halves(value, bits):
    return rows_from(value, bits["send"], 256), rows_from(value, bits["keep"], 256)


def reduce_tp(products, operands, bits, beside=None):
    count = len(products)
    pairs = [halves(v, bits) for v in operands]
    send = jnp.concatenate([p(v[0]).astype(BF) for p, v in zip(products, pairs)], axis=0)
    first = swap(send, "C")
    kept = [p(v[1]) for p, v in zip(products, pairs)]
    events = [send]
    if beside:
        first = after(first, beside(0, events, kept))
    totals = [v + first[i * 256 : (i + 1) * 256].astype(F32) for i, v in enumerate(kept)]
    events.append(first)
    streams = [[v[:128] for v in totals], [v[128:] for v in totals]]
    for stage, kinds in enumerate((("Z1", "Z3"), ("Z3", "Z1"))):
        n = streams[0][0].shape[0] // 2
        give = [
            jnp.concatenate([pick(bits[t], v[n:], v[:n]).astype(BF) for v in parts], axis=0)
            for t, parts in zip(kinds, streams)
        ]
        got = [swap(v, t) for v, t in zip(give, kinds)]
        if beside:
            got = after(got, beside(1 + stage, events, kept))
        events.append(got)
        streams = [
            [pick(bits[t], v[:n], v[n:]) + g[i * n : (i + 1) * n].astype(F32) for i, v in enumerate(parts)]
            for t, parts, g in zip(kinds, streams, got)
        ]
    out = [jnp.concatenate([streams[0][i], streams[1][i]], axis=0) for i in range(count)]
    return out, events, kept


def merge_rows(bit, own, got):
    return jnp.concatenate([pick(bit, own, got), pick(bit, got, own)], axis=1)


def gather_tp(shards, bits, beside=None, whole=True):
    parts = [shards[:, :32], shards[:, 32:]]
    events = [shards]
    for stage, kinds in enumerate((("Z3", "Z1"), ("Z1", "Z3"))):
        got = [swap(v, t) for v, t in zip(parts, kinds)]
        if beside:
            got = after(got, beside(3 + stage, events, None))
        events.append(got)
        parts = [merge_rows(bits[t], v, g) for t, v, g in zip(kinds, parts, got)]
    own = jnp.concatenate(parts, axis=1)
    last = swap(own, "C")
    if beside:
        last = after(last, beside(5, events, None))
    events.append(last)
    return (merge_rows(bits["C"], own, last) if whole else (own, last)), events


Y_FLIP = PERM["Y1"]
Y_FLIP_DOWN = pairs_xy(lambda x, y: (x, y ^ 1) if y % 2 == 1 else None)
Y_FLIP_UP = pairs_xy(lambda x, y: (x, y ^ 1) if y % 2 == 0 else None)
X_UP = pairs_xy(lambda x, y: (x + 1, y) if x < 3 else None)
X_UP2 = pairs_xy(lambda x, y: (x + 2, y) if x < 2 else None)
X_DOWN = pairs_xy(lambda x, y: (x - 1, y) if x > 0 else None)
X_DOWN2 = pairs_xy(lambda x, y: (x - 2, y) if x > 1 else None)
SLOTS = 6


def slot_block(slot, c):
    back = slot // 2 * 2
    return c - back if slot % 2 == 0 else (c ^ 1) - back


def slot_needed(slot, c, length, first_ref):
    block = slot_block(slot, c)
    return (block >= 0) & (block < c) & (block * length + length - 1 >= first_ref[0])


def nt(a, b):
    return lax.dot_general(a, b, (((1,), (1,)), ((), ())), preferred_element_type=F32)


def tn(a, b):
    return lax.dot_general(a, b, (((0,), (0,)), ((), ())), preferred_element_type=F32)


def nn(a, b):
    return jnp.dot(a, b, preferred_element_type=F32)


def visible(slot, block, length, start_ref, c):
    keys = lax.broadcasted_iota(jnp.int32, (length, length), 0) + block * length
    mask = keys >= start_ref[...]
    if slot == 0:
        mask = mask & (keys <= lax.broadcasted_iota(jnp.int32, (length, length), 1) + c * length)
    return mask


def attn_fwd_kernel(heads, me_ref, first_ref, start_ref, q_ref, *refs):
    kv = refs[:SLOTS]
    att_ref, mix_ref, lse_ref, m_ref, l_ref = refs[SLOTS:]
    length = q_ref.shape[0]
    hidden = heads * HEAD_DIM
    c = me_ref[0] % 8
    for slot in range(SLOTS):
        block = slot_block(slot, c)

        def run(slot=slot, block=block):
            mask = visible(slot, block, length, start_ref, c)
            for h in range(heads):
                cols = slice(h * HEAD_DIM, (h + 1) * HEAD_DIM)
                key = kv[slot][:, cols]
                val = kv[slot][:, hidden + h * HEAD_DIM : hidden + (h + 1) * HEAD_DIM]
                s = jnp.where(mask, nt(key, q_ref[:, cols]), NEG)
                top = jnp.max(s, axis=0, keepdims=True)
                if slot == 0:
                    p = jnp.exp2((s - top) * SCALE2)
                    m_ref[h : h + 1] = top
                    l_ref[h : h + 1] = jnp.sum(p, axis=0, keepdims=True)
                    mix_ref[cols] = tn(val, p.astype(BF))
                else:
                    old = m_ref[h : h + 1]
                    new = jnp.maximum(old, top)
                    p = jnp.exp2((s - new) * SCALE2)
                    shrink = jnp.exp2((old - new) * SCALE2)
                    m_ref[h : h + 1] = new
                    l_ref[h : h + 1] = l_ref[h : h + 1] * shrink + jnp.sum(p, axis=0, keepdims=True)
                    mix_ref[cols] = mix_ref[cols] * shrink + tn(val, p.astype(BF))

        if slot == 0:
            run()
        else:
            pl.when(slot_needed(slot, c, length, first_ref))(run)
    for h in range(heads):
        cols = slice(h * HEAD_DIM, (h + 1) * HEAD_DIM)
        out = mix_ref[cols] / l_ref[h : h + 1]
        mix_ref[cols] = out
        att_ref[:, cols] = out.T.astype(BF)
        lse_ref[h : h + 1] = m_ref[h : h + 1] * SCALE2 + jnp.log2(l_ref[h : h + 1])


def attn_bwd_kernel(heads, me_ref, first_ref, start_ref, q_ref, do_ref, mix_ref, lse_ref, *refs):
    kv = refs[:SLOTS]
    dq_ref, dkv = refs[SLOTS], refs[SLOTS + 1 : 2 * SLOTS + 1]
    dqt_ref, delta_ref = refs[2 * SLOTS + 1 :]
    length = q_ref.shape[0]
    hidden = heads * HEAD_DIM
    c = me_ref[0] % 8
    for h in range(heads):
        cols = slice(h * HEAD_DIM, (h + 1) * HEAD_DIM)
        dot_t = do_ref[:, cols].astype(F32).T
        delta_ref[h : h + 1] = jnp.sum(dot_t * mix_ref[cols], axis=0, keepdims=True)
    for slot in range(SLOTS):
        block = slot_block(slot, c)

        def run(slot=slot, block=block):
            mask = visible(slot, block, length, start_ref, c)
            for h in range(heads):
                cols = slice(h * HEAD_DIM, (h + 1) * HEAD_DIM)
                vcols = slice(hidden + h * HEAD_DIM, hidden + (h + 1) * HEAD_DIM)
                key, val = kv[slot][:, cols], kv[slot][:, vcols]
                q, do = q_ref[:, cols], do_ref[:, cols]
                s = jnp.where(mask, nt(key, q), NEG)
                p = jnp.exp2(s * SCALE2 - lse_ref[h : h + 1])
                ds = (p * (nt(val, do) - delta_ref[h : h + 1])).astype(BF)
                dkv[slot][:, cols] = (nn(ds, q) * SCALE).astype(dkv[slot].dtype)
                dkv[slot][:, vcols] = nn(p.astype(BF), do).astype(dkv[slot].dtype)
                part = tn(key, ds)
                if slot == 0:
                    dqt_ref[cols] = part
                else:
                    dqt_ref[cols] = dqt_ref[cols] + part

        if slot == 0:
            run()
        else:
            pl.when(slot_needed(slot, c, length, first_ref))(run)

            @pl.when(jnp.logical_not(slot_needed(slot, c, length, first_ref)))
            def _(slot=slot):
                dkv[slot][...] = jnp.zeros(dkv[slot].shape, dkv[slot].dtype)

    for h in range(heads):
        cols = slice(h * HEAD_DIM, (h + 1) * HEAD_DIM)
        dq_ref[:, cols] = (dqt_ref[cols] * SCALE).T.astype(BF)


def stats_kernel(x_ref, mean_ref, spread_ref):
    for r in range(0, x_ref.shape[0], 64):
        v = x_ref[r : r + 64].astype(F32)
        mean = jnp.mean(v, axis=-1, keepdims=True)
        centre = v - mean
        spread = lax.rsqrt(jnp.mean(centre * centre, axis=-1, keepdims=True) + 1e-05)
        mean_ref[r : r + 64] = jnp.broadcast_to(mean, (64, 128))
        spread_ref[r : r + 64] = jnp.broadcast_to(spread, (64, 128))


def norm_kv_kernel(me_ref, x_ref, mean_ref, spread_ref, k_own, v_own, k_got, v_got, normed_ref, kv_ref, acc_ref):
    me = me_ref[0]
    hidden = k_own.shape[2]
    zero = jnp.zeros((1, 128), F32)
    bias = [zero, zero]
    away_k, away_v = offsets(ORDER_A), offsets(ORDER_B)
    for q in range(8):
        parts = []
        for src, p in ((k_own, q), (k_got, q + 8)):
            block = me ^ away_k[p]
            cols = pl.ds(pl.multiple_of(block * 128, 128), 128)
            small = src[q, 128:144, :128].astype(F32)
            scaled = (x_ref[:, cols].astype(F32) - mean_ref[...]) * spread_ref[...]
            part = (scaled * small[0:1] + small[1:2]).astype(BF)
            normed_ref[:, cols] = part
            parts.append(part)
            turned = pltpu.roll(small[:8], (block % 8) * 16, 1)[7:8]
            bias = [bias[0] + jnp.where(block < 8, turned, zero), bias[1] + jnp.where(block < 8, zero, turned)]
        weights = jnp.concatenate([k_own[q, :128], k_got[q, :128]], axis=0)
        term = jnp.dot(jnp.concatenate(parts, axis=1), weights, preferred_element_type=F32)
        acc_ref[...] = term if q == 0 else acc_ref[...] + term
    kv_ref[:, :hidden] = acc_ref[...].astype(BF)
    for q in range(8):
        parts = []
        for p in (q, q + 8):
            parts.append(normed_ref[:, pl.ds(pl.multiple_of((me ^ away_v[p]) * 128, 128), 128)])
        weights = jnp.concatenate([v_own[q], v_got[q]], axis=0)
        term = jnp.dot(jnp.concatenate(parts, axis=1), weights, preferred_element_type=F32)
        acc_ref[...] = term if q == 0 else acc_ref[...] + term
    kv_ref[:, hidden:] = (acc_ref[...] + jnp.concatenate(bias, axis=1)).astype(BF)


def early_kernel(att_ref, query_ref, pre_ref, attn_ref, norm_ref, scaled_ref, cot_ref, out_ref):
    def total(v):
        return jnp.sum(v.astype(F32), axis=0, keepdims=True)

    out_ref[0:2] = jnp.zeros((2, out_ref.shape[1]), F32)
    out_ref[2:3] = total(attn_ref[...])
    out_ref[3:4] = total(norm_ref[...] * scaled_ref[...])
    out_ref[4:5] = total(norm_ref[...])
    out_ref[5:6] = total(cot_ref[...])
    value, query, expand = total(att_ref[...]), total(query_ref[...]), total(pre_ref[...])
    lane = lax.broadcasted_iota(jnp.int32, (8, 128), 1)

    def taken(row, size, block, to):
        at = block * size
        wide = jnp.broadcast_to(row[:, at // 128 * 128 : at // 128 * 128 + 128], (8, 128))
        wide = pltpu.roll(wide, (128 - at % 128 + to) % 128, 1)
        return jnp.where((lane >= to) & (lane < to + size), wide, 0.0)[0:1]

    nb, ne = value.shape[1] // 16, expand.shape[1] // 16
    for block in range(16):
        cols = slice(block * 128, block * 128 + 128)
        out_ref[6:7, cols] = taken(value, nb, block, 0) + taken(expand, ne, block, nb)
        out_ref[7:8, cols] = taken(query, nb, block, 0)


def late_kernel(core_ref, x_ref, mean_ref, spread_ref, gone_ref, kept_ref, early_ref, out_ref):
    core = core_ref[0]
    size = gone_ref.shape[0]
    out_ref[...] = early_ref[...]
    first = jnp.zeros((1, x_ref.shape[1]), F32)
    second = first
    for src, base in ((gone_ref, (1 - core) * size), (kept_ref, core * size)):
        for r in range(0, size, 32):
            rows = pl.ds(pl.multiple_of(base + r, 32), 32)
            scaled = (x_ref[rows].astype(F32) - mean_ref[rows][:, :1]) * spread_ref[rows][:, :1]
            grad = src[r : r + 32].astype(F32)
            first = first + jnp.sum(grad * scaled, axis=0, keepdims=True)
            second = second + jnp.sum(grad, axis=0, keepdims=True)
    out_ref[0:1] = first
    out_ref[1:2] = second


def final_ffn_kernel(*refs):
    kept, one, zero, outs = refs[:2], refs[2:4], refs[4:6], refs[6:]
    total = [k[0] + a[0].astype(F32) + b[0].astype(F32) for k, a, b in zip(kept, one, zero)]
    outs[0][...] = total[0]
    for j in range(0, total[1].shape[1], 128):
        outs[1][j : j + 128] = total[1][:, j : j + 128].T


def final_rows_kernel(core_ref, own_ref, last_ref, grad_ref, out_ref):
    size = own_ref.shape[1]
    core = core_ref[0]
    for src, base in ((own_ref, core * size), (last_ref, (1 - core) * size)):
        for r in range(0, size, 64):
            rows = pl.ds(pl.multiple_of(base + r, 64), 64)
            grad_ref[rows] = src[0, r : r + 64].astype(F32)
            out_ref[rows] = src[1, r : r + 64]


def final_qo_kernel(me_ref, grad_ref, *refs):
    gots, outs = refs[:-2], refs[-2:]
    piece = grad_ref[pl.ds(pl.multiple_of(me_ref[0] * 128, 128), 128)].astype(F32)
    for got in gots:
        piece = piece + got[0].astype(F32)
    half = piece.shape[1] // 2
    outs[0][...] = piece[:, :half]
    outs[1][...] = piece[:, half:].T


def norm_stats(v):
    mean = jnp.mean(v, axis=-1, keepdims=True)
    centre = v - mean
    spread = lax.rsqrt(jnp.mean(centre * centre, axis=-1, keepdims=True) + 1e-05)
    return centre * spread, spread


def norm_back(grad, gain, scaled, spread):
    weighted = grad * gain
    inner = jnp.mean(weighted, axis=-1, keepdims=True)
    cross = jnp.mean(weighted * scaled, axis=-1, keepdims=True)
    return spread * (weighted - inner - scaled * cross)


def cols_of(w, n=4):
    k = w.shape[1] // n
    return [w[:, i * k : (i + 1) * k] for i in range(n)]


def body(
    layer_input,
    doc_ids,
    pre_gain,
    pre_shift,
    query_weight,
    query_bias,
    key_weight,
    value_weight,
    value_bias,
    output_weight,
    output_bias,
    mid_gain,
    mid_shift,
    expand_weight,
    expand_bias,
    contract_weight,
    contract_bias,
    cotangent,
):
    bits = own_bits(layer_input.shape[1])
    x = layer_input[0]
    cot = cotangent[0]
    length, width = x.shape
    hidden = query_weight.shape[1]
    heads = hidden // HEAD_DIM
    inner = expand_weight.shape[1]

    nb, ne = query_bias.shape[1], expand_bias.shape[1]
    pre_gain = after(pre_gain, bits)
    vectors = [pre_gain, pre_shift, output_bias, mid_gain, mid_shift, contract_bias]
    weights = [key_weight, value_weight, query_weight, output_weight]
    packed = shape((128, hidden))
    bufs = fetch_call(
        pack_kernel,
        "pack",
        [shape((144, hidden)), packed, packed, packed],
        [*weights, *[v[None] for v in vectors], query_bias, value_bias, expand_bias],
        scratch=[pltpu.VMEM((16, 128), F32)],
        moved=800 << 10,
    )
    bufs = [v[None] for v in bufs]
    first_orders, big_orders = (ORDER_A, ORDER_B, ORDER_C, ORDER_D), (ORDER_E, ORDER_F)
    kv_orders, qo_orders = (ORDER_A, ORDER_B), (ORDER_D,)
    half_shape = shape((128, inner // 2))
    ffn = fetch_call(
        pack_ffn_kernel, "pack_ffn", [half_shape] * 4, [expand_weight, contract_weight], moved=1536 << 10
    )
    con = [v[None] for v in ffn[2:]]
    bufs = join(bufs, swaps(bufs, first_orders, 0))
    got = swaps(bufs, first_orders, 1)
    stats = [shape((length, 128), F32)] * 2
    mean1, spread1 = local_call(stats_kernel, "stats", stats, [after(x, bufs)], mib=8, moved=3 << 20)
    one = swaps(con[:1], big_orders[:1], 0)
    bufs = join(bufs, after(got, one, mean1))
    got = swaps(bufs, first_orders, 2)
    two = swaps(con[1:], big_orders[1:], 0)
    bufs = join(bufs, after(got, two))
    con = join(con, one + two)
    got = swaps(bufs, first_orders, 3)
    got_con = swaps(after(con, got), big_orders, 1)
    exp_orders = (ORDER_G, ORDER_H)
    exp = [v[None] for v in ffn[:2]]
    got_exp = swaps(after(exp, got), exp_orders, 0)

    docs = doc_ids[0]
    own_docs = rows_from(docs, bits["place"], length)
    start = jnp.sum((docs[:, None] < own_docs[None, :]).astype(jnp.int32), axis=0)
    first_key = start[:1]
    start = start[None]

    normed, kv_own = local_call(
        norm_kv_kernel,
        "norm_kv",
        [shape((length, width)), shape((length, 2 * hidden))],
        [bits["me"], x, mean1, spread1, bufs[0], bufs[1], got[0], got[1]],
        in_smem=1,
        mib=10,
        scratch=[pltpu.VMEM((length, hidden), F32)],
        flops=2 * length * width * 2 * hidden,
        moved=6 << 20,
    )
    kv_own = after(kv_own, got_con, got_exp)
    kv_e1 = lax.ppermute(kv_own, XY, Y_FLIP)
    kv_f1 = lax.ppermute(kv_own, XY, X_UP)
    kv_f2 = lax.ppermute(kv_own, XY, X_UP2)
    con = join(con, got_con)
    exp = join(exp, got_exp)
    got_con = swaps(con, big_orders, 2)
    kv_e1 = after(kv_e1, exp, con, kv_f1)
    plan = [(ORDER_A, 0, 0), (ORDER_B, 0, hidden), (ORDER_C, 1, 0), (ORDER_D, 2, 0)]
    kv_full, q_full, o_full, vec, q_bias, e_bias = place(
        after(bufs, kv_e1), got, bits, 128, plan, [2 * hidden, hidden, hidden], [hidden, inner]
    )
    gain1, out_bias, gain2, shift2, con_bias = [vec[i : i + 1] for i in (0, 2, 3, 4, 5)]
    kv_g1 = lax.ppermute(kv_e1, XY, X_UP)
    kv_e3 = lax.ppermute(kv_f2, XY, Y_FLIP_DOWN)
    queries = (nn(normed, q_full) + q_bias).astype(BF)
    con = join(con, after(got_con, kv_e1))
    got_con = swaps(con, big_orders, 3)

    slots = [kv_own, kv_e1, kv_f1, kv_g1, kv_f2, kv_e3]
    attended, mixture, lse = local_call(
        lambda *refs: attn_fwd_kernel(heads, *refs),
        "attn_fwd",
        [shape((length, hidden)), shape((hidden, length), F32), shape((heads, length), F32)],
        [bits["me"], first_key, start, after(queries, con), *slots],
        in_smem=2,
        mib=12,
        scratch=[pltpu.VMEM((heads, length), F32), pltpu.VMEM((heads, length), F32)],
        flops=10**9,
        moved=6 << 20,
        exps=3 * 10**6,
    )

    feed = {}

    def beside_a(stage, events, kept):
        now = events[-1]
        if stage == 0:
            plan = [(ORDER_E, 0, 0), (ORDER_F, 0, inner // 2)]
            feed["contract"] = place(con, got_con, bits, 128, plan, [inner])[0]
            feed["got"] = swaps(after(exp, now), exp_orders, 1)
            return [feed["contract"], feed["got"]]
        if stage == 1:
            feed["exp"] = join(exp, after(feed["got"], now))
            feed["got"] = swaps(feed["exp"], exp_orders, 2)
        if stage == 2:
            return feed["got"]
        if stage == 3:
            feed["exp"] = join(feed["exp"], after(feed["got"], now))
            feed["got"] = swaps(feed["exp"], exp_orders, 3)
        return []

    (attn_total,), _, _ = reduce_tp([lambda v: nt(v, o_full)], [attended], bits, beside_a)
    contract_full = feed["contract"]
    x_shard = shard_rows(x, bits).astype(F32)
    middle = x_shard + (attn_total + out_bias)
    scaled2, spread2 = norm_stats(middle)
    normed_two, _ = gather_tp((scaled2 * gain2 + shift2).astype(BF)[None], bits, beside_a)
    normed_two = normed_two[0]

    plan = [(ORDER_G, 0, 0), (ORDER_H, 0, inner // 2)]
    expand_full = place(feed["exp"], feed["got"], bits, 128, plan, [inner])[0]
    grad_act = nn(cot, contract_full)
    pre_act = nn(normed_two, expand_full) + e_bias
    cdf = 0.5 * (1.0 + lax.erf(pre_act * (1.0 / math.sqrt(2.0))))
    activated = (pre_act * cdf).astype(BF)
    slope = cdf + pre_act * jnp.exp(-0.5 * pre_act * pre_act) * (1.0 / math.sqrt(2.0 * math.pi))
    grad_pre = (slope * grad_act).astype(BF)
    big = {}

    def beside_de(stage, events, kept):
        if stage == 1:
            held = after((cot, activated, normed_two, grad_pre), kept)
            big["grads"] = [tn(held[2], held[3]).astype(BF), tn(held[0], held[1]).astype(BF)]
            big["send"] = big_part(big["grads"], [], bits, 3)
            return big["send"]
        if stage == 2:
            big["got3"] = big_swaps(after(big["send"], events[-1]), 3)
        if stage == 3:
            return big["got3"]
        if stage != 4:
            return []
        big["send"] = big_part(big["grads"], [after(big["got3"], events[-1])], bits, 2)
        big["got2"] = big_swaps(big["send"], 2)
        return big["send"]

    (grad_norm2,), _, _ = reduce_tp([lambda v: nt(v, expand_full)], [grad_pre], bits, beside_de)

    cot_shard = shard_rows(cot, bits).astype(F32)
    grad_middle = cot_shard + norm_back(grad_norm2, gain2, scaled2, spread2)
    grad_attn_shard = grad_middle.astype(BF)
    grad_attn, _ = gather_tp(grad_attn_shard[None], bits, beside_de)
    grad_attn = grad_attn[0]

    grad_att = nn(grad_attn, o_full).astype(BF)
    dkv = shape((length, 2 * hidden))
    grad_q, own_part, p_e1, p_f1, p_g1, p_f2, p_e3 = local_call(
        lambda *refs: attn_bwd_kernel(heads, *refs),
        "attn_bwd",
        [shape((length, hidden)), shape((length, 2 * hidden), F32)] + [dkv] * 5,
        [bits["me"], first_key, start, queries, after(grad_att, big["send"]), mixture, lse, *slots],
        in_smem=2,
        mib=16,
        scratch=[pltpu.VMEM((hidden, length), F32), pltpu.VMEM((heads, length), F32)],
        flops=2 * 10**9,
        moved=10 << 20,
        exps=3 * 10**6,
    )
    got2 = after(big["got2"], grad_q)
    both = big_part(big["grads"], [big["got3"], got2], bits, 1)
    rest = both[2:]
    from_g1 = lax.ppermute(after(p_g1, got2), XY, X_DOWN)
    from_e3 = lax.ppermute(after(p_e3, got2), XY, Y_FLIP_UP)
    got1 = big_swaps(both[:2], 1)
    mlp_send, mlp_keep = halves(after(activated, got2), bits)
    mlp_got = swap(after(nt(mlp_send, contract_full).astype(BF), got2), "C")

    grad_o = tn(grad_attn, after(attended, grad_q)).astype(BF)
    qo_grads = [jnp.concatenate([tn(normed, grad_q).astype(BF), grad_o], axis=1)]
    qo_plan = [(ORDER_D, 0, 0, 2 * hidden)]
    qo_send = part(qo_grads, [], bits, qo_plan, 3, 0), part(qo_grads, [], bits, qo_plan, 3, 1)
    from_f1 = lax.ppermute(after(p_f1, from_g1), XY, X_DOWN)
    total = nt(mlp_keep, contract_full) + after(mlp_got, from_g1).astype(F32)
    one, two = total[:128], total[128:]
    two = [jnp.concatenate([two[i : i + 32], two[i + 64 : i + 96]], axis=0) for i in (0, 32)]
    give = [pick(bits["Z1"], one[64:], one[:64]), pick(bits["Z1"], two[1], two[0])]
    mlp_got = swap(after(jnp.concatenate(give, axis=0).astype(BF), got1), "Z1")
    one = pick(bits["Z1"], one[:64], one[64:])
    two = pick(bits["Z1"], two[0], two[1])
    from_e1 = lax.ppermute((p_e1.astype(F32) + from_g1.astype(F32)).astype(BF), XY, Y_FLIP)
    from_f2 = lax.ppermute((p_f2.astype(F32) + from_e3.astype(F32)).astype(BF), XY, X_DOWN2)
    early = local_call(
        early_kernel,
        "early",
        shape((8, width), F32),
        [grad_att, grad_q, grad_pre, grad_attn_shard, grad_norm2, scaled2, cot_shard],
        mib=8,
        moved=4 << 20,
    )
    from_e1 = after(from_e1, early)
    send0 = [(v[1:] + g[1:].astype(F32)).astype(BF) for v, g in zip(rest, got1)]
    from_f2 = after(from_f2, send0, qo_send)
    mlp_got = after(mlp_got, from_e1).astype(F32)
    one, two = one + mlp_got[:64], two + mlp_got[64:]
    give = [pick(bits["Z3"], v[32:], v[:32]).astype(BF) for v in (one, two)]
    mlp_give = jnp.concatenate(give, axis=0)
    mlp_kept = jnp.concatenate([pick(bits["Z3"], v[:32], v[32:]) for v in (one, two)], axis=0)
    from_f2 = after(from_f2, mlp_give)
    grad_kv = (own_part + from_f1.astype(F32) + from_e1.astype(F32) + from_f2.astype(F32)).astype(BF)

    qkv_full = jnp.concatenate([after(q_full, grad_q), kv_full], axis=1)
    grad_qkv = jnp.concatenate([grad_q, grad_kv], axis=1)
    tail = {}

    kv_plan = [(ORDER_A, 0, 0, hidden), (ORDER_B, 0, hidden, hidden)]

    def beside_fg(stage, events, kept):
        now = events[-1]
        if stage == 0:
            tail["q3"] = swaps(after(qo_send[0], now), qo_orders, 3)
            big["got0"] = big_swaps(after(send0, now), 0)
            tail["mlp"] = swap(after(mlp_give, now), "Z3")
            tail["kv"] = [tn(normed, after(grad_kv, now)).astype(BF)]
            return [tail["kv"], big["got0"], tail["mlp"]]
        if stage == 1:
            tail["small"] = local_call(
                late_kernel,
                "late",
                shape((8, width), F32),
                [bits["core"], x, mean1, spread1, events[0], kept[0], early],
                in_smem=1,
                mib=8,
                moved=6 << 20,
            )
            tail["send"] = part(tail["kv"], [], bits, kv_plan, 3, small=tail["small"])
            tail["k3"] = swaps(tail["send"], kv_orders, 3)
            tail["q3_high"] = swaps(after(qo_send[1], tail["q3"], now), qo_orders, 3)
            return [tail["send"], tail["q3"]]
        if stage == 2:
            big["final"] = local_call(
                final_ffn_kernel,
                "final_ffn",
                [shape((width // 16, inner), F32), shape((inner, width // 16), F32)],
                [*rest, *got1, *after(big["got0"], now)],
                mib=8,
                moved=4 << 20,
            )
            return [tail["k3"], tail["q3_high"], big["final"]]
        small = dict(small=tail["small"])
        if stage == 3:
            tail["k2"] = swaps(part(tail["kv"], [(after(tail["k3"], now), 0)], bits, kv_plan, 2, **small), kv_orders, 2)
            tail["q2"] = swaps(part(qo_grads, [(after(tail["q3_high"], now), 4)], bits, qo_plan, 2), qo_orders, 2)
            return [tail["k2"], tail["q2"]]
        if stage == 4:
            gots = [(tail["k3"], 0), (after(tail["k2"], now), 0)]
            tail["k1"] = swaps(part(tail["kv"], gots, bits, kv_plan, 1, **small), kv_orders, 1)
            gots = [(tail["q3"], 0), (after(tail["q2"], now), 0)]
            tail["q1"] = swaps(part(qo_grads, gots, bits, qo_plan, 1), qo_orders, 1)
            return [tail["k1"], tail["q1"]]
        gots = [(tail["k3"], 0), (tail["k2"], 0), (after(tail["k1"], now), 0)]
        tail["k0"] = swaps(part(tail["kv"], gots, bits, kv_plan, 0, **small), kv_orders, 0)
        gots = [(tail["q3"], 0), (tail["q2"], 0), (after(tail["q1"], now), 0)]
        tail["q0"] = swaps(part(qo_grads, gots, bits, qo_plan, 0), qo_orders, 0)
        return [tail["k0"], tail["q0"]]

    (grad_norm1,), _, _ = reduce_tp([lambda v: nt(v, qkv_full)], [grad_qkv], bits, beside_fg)
    x_scaled, x_spread = norm_stats(x_shard)
    grad_x = grad_middle + norm_back(grad_norm1, gain1, x_scaled, x_spread)
    mlp_total = mlp_kept + tail["mlp"].astype(F32)
    layer_shard = (middle + (mlp_total + con_bias)).astype(BF)
    (own, last), _ = gather_tp(jnp.stack([grad_x.astype(BF), layer_shard]), bits, beside_fg, whole=False)
    input_grad, layer_output = local_call(
        final_rows_kernel,
        "final_rows",
        [shape((length, width), F32), shape((length, width))],
        [bits["core"], own, last],
        in_smem=1,
        mib=8,
        moved=10 << 20,
    )
    gots = [(tail[k], 0) for k in ("k3", "k2", "k1", "k0")]
    k_grad, v_grad, small = part(tail["kv"], gots, bits, kv_plan, -1, small=tail["small"])
    biases, q_bias_grad = small[6:7], small[7:8]
    for kind in ("C", "Z1", "Z3"):
        small = small + swap(small, kind)
    gots = [(tail[k], 0) for k in ("q3", "q2", "q1", "q0")]
    q_grad, o_grad = local_call(
        final_qo_kernel,
        "final_qo",
        [shape((width // 16, hidden), F32), shape((hidden, width // 16), F32)],
        [bits["me"], *qo_grads, *[g for got, _ in gots for g in got]],
        in_smem=1,
        mib=6,
        moved=1 << 20,
    )
    expand_grad, contract_grad = big["final"]

    return (
        layer_output[None],
        input_grad[None],
        small[0],
        small[1],
        q_grad,
        q_bias_grad[:, :nb],
        k_grad[0],
        v_grad[0],
        biases[:, :nb],
        o_grad,
        small[2],
        small[3],
        small[4],
        expand_grad,
        biases[:, nb : nb + ne],
        contract_grad,
        small[5],
    )


def solution(mesh):
    both = ("fsdp", "ctx")
    rows, cols, vec = P(both, "tp"), P("tp", both), P(both)
    act = P("fsdp", "ctx", None)
    return jax.shard_map(
        body,
        mesh=mesh,
        in_specs=(
            act, P("fsdp", None), vec, vec, rows, cols, rows, rows, cols, cols, vec, vec, vec,
            rows, cols, cols, vec, act,
        ),
        out_specs=(
            act, act, vec, vec, rows, cols, rows, rows, cols, cols, vec, vec, vec, rows, cols, cols, vec,
        ),
        check_vma=False,
    )
```
